32 devices in a mesh: groups: 2 (over y), seq: 4 (over z), head: 2 (over x), sub: 2 (over core).
Axes of the slice: x: 2, y: 2, z: 4, core: 2. Of those that a mesh axis runs over, the one named last changes fastest.
Arguments:
- tokens: bfloat16 [4096, 3072], P(('groups', 'seq')), parts along dimension 0, may hold values from -6 to 6
- modulation: float32 [3, 3072], replicated, may hold values from -4 to 4
- w_qkv: bfloat16 [3072, 8, 768], P('seq', ('head', 'sub')), may hold values from -0.15625 to 0.15625
- w_out: bfloat16 [2048, 3072], P('seq', ('head', 'sub')), may hold values from -0.125 to 0.125
- pattern: int32 [32, 4], P(('groups', 'seq')), parts along dimension 0, may hold values from 0 to 15, as said below
- counts: int32 [32], P(('groups', 'seq')), parts along dimension 0, may hold values from 1 to 4, as said below
- spatial_mask: int32 [8, 4, 4], P(('groups', 'seq')), parts along dimension 0, may hold values from 0 to 1, as said below
Outputs:
- update: bfloat16 [4096, 3072], P(('groups', 'seq'), ('head', 'sub')), parts along dimension 0
The draws below stay inside these ranges and needn't reach their ends.
There are 2 independent parts, one for each index of `groups`. The reference program is written for one: setup_inputs(seed, part) draws one part's arguments, and reference() takes and returns one part's arrays. A program takes and returns all parts, laid end to end along the dimension named above; an argument that names none is the same for every part. Nothing has to cross between parts.
Inputs may be any that keep to these rules, and one draw needn't show every extreme that they name: pattern[b, 0] = b; each further entry of row b is b plus a nonzero offset of size at most 2, the offsets of one row different, clipped to the blocks of the video. `counts`: blocks with a count above one all lie in one cyclic run of half of the 16 blocks. `spatial_mask`: every diagonal entry is 1.
All inputs are finite; a program needn't handle non-finite values.
Results may differ from the reference program's by a relative error of at most 0.012.
The reference program's roundings to bfloat16 on the way count: a program that leaves them out, or rounds other values in their place, can miss the bound.
Values may be sent and summed in bfloat16 or wider, within the bound.
A program may use at most 128 MiB of HBM per device.

```python
import math
import jax
import jax.numpy as jnp
from jax import lax

D = 3072
HD = 128
PAIRS = 8
BLOCK = 128
WIN = 2
SLOTS = 4
POS = 512
FRAMES = 4
ROWS = 2048
TB = 16
SB = 4


def draw_pattern(key, part):
    blocks = jnp.arange(TB, dtype=jnp.int32)
    scores = jax.random.randint(jax.random.fold_in(key, 11), (TB, 2 * WIN), 0, 4096, dtype=jnp.int32)
    scores = scores * (2 * WIN) + jnp.arange(2 * WIN, dtype=jnp.int32)[None, :]
    order = jnp.argsort(scores, axis=1)
    offset_table = jnp.concatenate([jnp.arange(-WIN, 0, dtype=jnp.int32), jnp.arange(1, WIN + 1, dtype=jnp.int32)])
    chosen = offset_table[order[:, :SLOTS - 1]]
    others = jnp.clip(blocks[:, None] + chosen, 0, TB - 1)
    return jnp.concatenate([blocks[:, None], others], axis=1).astype(jnp.int32)


def draw_counts(key, part):
    blocks = jnp.arange(TB, dtype=jnp.int32)
    first_hot = jax.random.randint(jax.random.fold_in(key, 21), (), 0, TB, dtype=jnp.int32)
    inside = (blocks - first_hot) % TB < TB // 2
    level = jax.random.randint(jax.random.fold_in(key, 22), (TB,), 1, SLOTS + 1, dtype=jnp.int32)
    values = jnp.where(inside, level, 1)
    return jnp.where(blocks == first_hot, SLOTS, values).astype(jnp.int32)


def draw_spatial_mask(key, part):
    random_bits = jax.random.randint(jax.random.fold_in(key, 31), (FRAMES, SB, SB), 0, 2, dtype=jnp.int32)
    diagonal = (jnp.arange(SB, dtype=jnp.int32)[:, None] == jnp.arange(SB, dtype=jnp.int32)[None, :]).astype(jnp.int32)
    return jnp.maximum(random_bits, diagonal[None, :, :]).astype(jnp.int32)


def levels(stream_key, extent, pieces, least, top_value):
    gain = 1.0
    for dim, shards_of in pieces:
        heights = jax.random.uniform(jax.random.fold_in(jax.random.fold_in(stream_key, 6), dim), (shards_of,), jnp.float32, least / len(pieces), top_value / len(pieces))
        gain = gain * jnp.repeat(jnp.exp(heights), extent[dim] // shards_of).reshape((-1,) + (1,) * (len(extent) - 1 - dim))
    return gain


def bell_draw(rng, dims, width, bound, split=(), kind=jnp.bfloat16):
    drawn = width * jax.random.normal(rng, dims, jnp.float32)
    if split:
        drawn = drawn * levels(rng, dims, split, -0.22, 0.18)
    return jnp.clip(drawn, -bound, bound).astype(kind)


def setup_inputs(seed: int = 0, part: int = 0) -> dict:
    splits = jax.random.split(jax.random.key(seed), 8)
    own_keys = jax.random.split(jax.random.fold_in(splits[7], part), 8)
    return {
        "tokens": bell_draw(own_keys[0], (ROWS, D), 1.0, 6.0, ((0, 4),)),
        "modulation": bell_draw(splits[1], (3, D), 1.0, 4.0, (), jnp.float32),
        "w_qkv": bell_draw(splits[2], (D, PAIRS, 6 * HD), (D // 2) ** -0.5, 0.15625, ((0, 4), (1, 4))),
        "w_out": bell_draw(splits[3], (2 * PAIRS * HD, D), (2 * PAIRS * HD) ** -0.5, 0.125, ((0, 4), (1, 4))),
        "pattern": draw_pattern(jax.random.fold_in(jax.random.fold_in(splits[7], part), 71), part),
        "counts": draw_counts(jax.random.fold_in(jax.random.fold_in(splits[7], part), 71), part),
        "spatial_mask": draw_spatial_mask(jax.random.fold_in(jax.random.fold_in(splits[7], part), 71), part),
    }


EPSILON = 1e-06

def modulate(tokens, modulation):
    values = tokens.astype(jnp.float32)
    center = lax.optimization_barrier(jnp.mean(values, axis=-1, keepdims=True))
    spread = lax.optimization_barrier(jnp.mean(jnp.square(values - center), axis=-1, keepdims=True))
    normed = (values - center) * lax.rsqrt(spread + EPSILON)
    return (normed * (1.0 + modulation[1]) + modulation[0]).astype(jnp.bfloat16)

def pair_attention(hidden, weight, pattern, counts, spatial_mask):
    scale_factor = 1.0 / math.sqrt(HD)
    qkv = jnp.dot(hidden, weight, preferred_element_type=jnp.float32).astype(jnp.bfloat16)
    temporal = qkv[:, :3 * HD].reshape(FRAMES, POS, 3 * HD).transpose(1, 0, 2).reshape(TB, BLOCK, 3 * HD)
    queries = temporal[:, :, :HD].astype(jnp.float32)
    key_blocks = temporal[:, :, HD:2 * HD][pattern].astype(jnp.float32)
    value_blocks = temporal[:, :, 2 * HD:][pattern].astype(jnp.float32)
    scores = jnp.einsum('bqc,bjkc->bjqk', queries, key_blocks) * scale_factor
    alive = (jnp.arange(SLOTS, dtype=jnp.int32)[None, :] < counts[:, None]).astype(jnp.float32)
    weights = jnp.exp(scores) * alive[:, :, None, None]
    denominator = lax.optimization_barrier(jnp.sum(weights, axis=(1, 3)))
    rounded = lax.optimization_barrier(weights.astype(jnp.bfloat16)).astype(jnp.float32)
    numerator = jnp.einsum('bjqk,bjkc->bqc', rounded, value_blocks)
    temporal_out = (numerator / denominator[:, :, None]).astype(jnp.bfloat16)
    temporal_out = temporal_out.reshape(POS, FRAMES, HD).transpose(1, 0, 2).reshape(ROWS, HD)
    spatial = qkv[:, 3 * HD:].reshape(FRAMES, POS, 3 * HD).astype(jnp.float32)
    scores = jnp.einsum('fpc,fqc->fpq', spatial[..., :HD], spatial[..., HD:2 * HD]) * scale_factor
    keep = spatial_mask.astype(jnp.float32)[:, :, None, :, None]
    weights = (jnp.exp(scores).reshape(FRAMES, SB, BLOCK, SB, BLOCK) * keep).reshape(FRAMES, POS, POS)
    denominator = lax.optimization_barrier(jnp.sum(weights, axis=-1))
    rounded = lax.optimization_barrier(weights.astype(jnp.bfloat16)).astype(jnp.float32)
    numerator = jnp.einsum('fpq,fqc->fpc', rounded, spatial[..., 2 * HD:])
    spatial_out = (numerator / denominator[..., None]).astype(jnp.bfloat16).reshape(ROWS, HD)
    return jnp.stack([temporal_out, spatial_out], axis=1)

def reference(tokens, modulation, w_qkv, w_out, pattern, counts, spatial_mask):
    hidden = modulate(tokens, modulation)

    def one_pair(weight):
        return pair_attention(hidden, weight, pattern, counts, spatial_mask)
    outputs = lax.map(one_pair, w_qkv.transpose(1, 0, 2))
    attention = outputs.transpose(1, 0, 2, 3).reshape(ROWS, 2 * PAIRS * HD)
    mixed = jnp.dot(attention, w_out, preferred_element_type=jnp.float32)
    return (modulation[2] * mixed).astype(jnp.bfloat16)
```

```python
import functools
import math

import jax
import jax.numpy as jnp
from jax import lax
from jax.experimental import pallas as pl
from jax.experimental.pallas import tpu as pltpu
from jax.sharding import PartitionSpec as P

BLOCK = 128
WIN = 2


EPSILON = 1e-06


def with_halo(cells, sides, width):
    for axis, dim in sides:
        count = lax.axis_size(axis)
        ends = count - 1
        head = lax.slice_in_dim(cells, 0, width, axis=dim)
        tail = lax.slice_in_dim(cells, cells.shape[dim] - width, cells.shape[dim], axis=dim)
        cells = jnp.concatenate(
            [
                lax.ppermute(tail, axis, [(i, (i + 1) % count) for i in range(ends)]),
                cells,
                lax.ppermute(head, axis, [((i + 1) % count, i) for i in range(ends)]),
            ],
            axis=dim,
        )
    return cells


MESH = pl.DeviceIdType.MESH


def pieces_of(rows, most=4):
    for count in range(most, 0, -1):
        if rows % (16 * count) == 0:
            return count
    return 1


class ShardLine:
    def __init__(self, own, slots, sems, chunks, count, parts):
        self.own, self.slots, self.chunks = own, slots, chunks
        self.sems, self.count, self.parts = sems, count, parts
        self.me = lax.axis_index("seq")
        self.group = lax.axis_index("groups")
        self.size = own.shape[0] // (parts * chunks)

    def rows(self, group, chunk):
        start = (group * self.chunks + chunk) * self.size
        return pl.ds(pl.multiple_of(start, self.size), self.size)

    def along(self, shard, chunk, way, own):
        rows = self.rows(self.group, chunk)
        source = self.own.at[rows] if own else self.slots.at[shard, rows]
        return pltpu.make_async_remote_copy(
            src_ref=source,
            dst_ref=self.slots.at[shard, rows],
            send_sem=self.sems.at[way, 0, shard, chunk],
            recv_sem=self.sems.at[way, 1, shard, chunk],
            device_id={"seq": self.me + (1 if way == 0 else -1)},
            device_id_type=MESH,
        )

    def across(self, shard, chunk, hop):
        rows = self.rows(self.group, chunk)
        return pltpu.make_async_remote_copy(
            src_ref=self.slots.at[shard, rows],
            dst_ref=self.slots.at[shard, rows],
            send_sem=self.sems.at[1 + hop, 0, shard, chunk],
            recv_sem=self.sems.at[1 + hop, 1, shard, chunk],
            device_id={"groups": lax.rem(self.group + hop, self.parts)},
            device_id_type=MESH,
        )

    def open_line(self):
        for chunk in range(self.chunks):
            for way in (0, 1):
                @pl.when(self.onward(way))
                def _():
                    self.along(self.me, chunk, way, True).start()

    def onward(self, way):
        return self.me < self.count - 1 if way == 0 else self.me > 0

    def shard_of(self, step, way):
        return self.me - step if way == 0 else self.me + step

    def present(self, step, way):
        return self.me >= step if way == 0 else self.me + step < self.count

    def relay(self, step):
        for chunk in range(self.chunks):
            for way in (0, 1):
                shard = self.shard_of(step, way)

                @pl.when(self.present(step, way))
                def _():
                    self.along(shard, chunk, way, False).wait_recv()

                    @pl.when(self.onward(way))
                    def _():
                        self.along(shard, chunk, way, False).start()

                    for hop in range(1, self.parts):
                        self.across(shard, chunk, hop).start()

    def complete(self, shard):
        for chunk in range(self.chunks):
            for hop in range(1, self.parts):
                self.across(shard, chunk, hop).wait_recv()

    def close_sends(self, step):
        for chunk in range(self.chunks):
            for way in (0, 1):
                shard = self.shard_of(step, way)

                @pl.when(self.present(step, way))
                def _():
                    @pl.when(self.onward(way))
                    def _():
                        self.along(shard, chunk, way, False).wait_send()

                    for hop in range(1, self.parts):
                        self.across(shard, chunk, hop).wait_send()

    def close_own(self):
        for chunk in range(self.chunks):
            for way in (0, 1):
                @pl.when(self.onward(way))
                def _():
                    self.along(self.me, chunk, way, True).wait_send()


def project_kernel(count, parts, q_chunks, o_chunks, hidden, w_own, o_own, qkv, o_all, slots, total, q_sems, o_sems, own_sem):
    me = lax.axis_index("seq")
    group = lax.axis_index("groups")
    barrier = pltpu.get_barrier_semaphore()

    @pl.when(me > 0)
    def _():
        pl.semaphore_signal(barrier, inc=1, device_id={"seq": me - 1}, device_id_type=MESH)

    @pl.when(me < count - 1)
    def _():
        pl.semaphore_signal(barrier, inc=1, device_id={"seq": me + 1}, device_id_type=MESH)

    for hop in range(1, parts):
        pl.semaphore_signal(
            barrier, inc=1, device_id={"groups": lax.rem(group + hop, parts)}, device_id_type=MESH
        )
    neighbours = jnp.where(me > 0, 1, 0) + jnp.where(me < count - 1, 1, 0) + (parts - 1)
    pl.semaphore_wait(barrier, neighbours)

    line = ShardLine(w_own, slots, q_sems, q_chunks, count, parts)
    outs = ShardLine(o_own, o_all, o_sems, o_chunks, count, parts)
    line.open_line()
    keep = pltpu.make_async_copy(o_own, o_all.at[me], own_sem)
    keep.start()
    tile = 256

    def add(shard, block, first):
        def column(j, carry):
            at = pl.ds(pl.multiple_of(j * tile, tile), tile)
            product = jnp.dot(hidden[shard], block[:, at], preferred_element_type=jnp.float32)
            total[:, at] = product if first else total[:, at] + product
            return carry

        lax.fori_loop(0, total.shape[1] // tile, column, 0)

    def finish(step):
        for way in (0, 1):
            shard = line.shard_of(step, way)

            @pl.when(line.present(step, way))
            def _():
                line.complete(shard)
                add(shard, slots.at[shard], False)

    add(me, w_own, True)

    def q_step(step, carry):
        line.relay(step)

        @pl.when(step > 1)
        def _():
            finish(step - 1)

        return carry

    lax.fori_loop(1, count, q_step, 0)
    outs.open_line()
    finish(count - 1)
    qkv[...] = total[...].astype(qkv.dtype)

    def o_step(step, carry):
        outs.relay(step)
        return carry

    lax.fori_loop(1, count, o_step, 0)

    def last(step, carry):
        line.close_sends(step)
        outs.close_sends(step)
        for way in (0, 1):
            shard = outs.shard_of(step, way)

            @pl.when(outs.present(step, way))
            def _():
                outs.complete(shard)

        return carry

    lax.fori_loop(1, count, last, 0)
    line.close_own()
    outs.close_own()
    keep.wait()


def project(hidden, w_own, o_own):
    count, parts = lax.axis_size("seq"), lax.axis_size("groups")
    rows, depth = hidden.shape
    hidden = hidden.reshape(rows, count, depth // count).transpose(1, 0, 2)
    width = w_own.shape[1]
    most = 4 if count <= 8 else 1
    q_chunks = pieces_of(w_own.shape[0] // parts, most)
    o_chunks = pieces_of(o_own.shape[0] // parts, most)
    vmem = pl.BlockSpec(memory_space=pltpu.VMEM)
    return pl.pallas_call(
        functools.partial(project_kernel, count, parts, q_chunks, o_chunks),
        out_shape=[
            jax.ShapeDtypeStruct((rows, width), jnp.bfloat16),
            jax.ShapeDtypeStruct((count,) + o_own.shape, jnp.bfloat16),
        ],
        in_specs=[vmem] * 3,
        out_specs=[vmem, pl.BlockSpec(memory_space=pl.ANY)],
        scratch_shapes=[
            pltpu.VMEM((count,) + w_own.shape, jnp.bfloat16),
            pltpu.VMEM((rows, width), jnp.float32),
            pltpu.SemaphoreType.DMA((1 + parts, 2, count, q_chunks)),
            pltpu.SemaphoreType.DMA((1 + parts, 2, count, o_chunks)),
            pltpu.SemaphoreType.DMA,
        ],
        compiler_params=pltpu.CompilerParams(
            collective_id=0, has_side_effects=True, vmem_limit_bytes=48 * 1024 * 1024
        ),
        name="project",
    )(hidden, w_own, o_own)


def mix_kernel(heads, subs, chunks, attn, w_all, gate, update, slots, total, x_sems, c_sems):
    head, sub = lax.axis_index("head"), lax.axis_index("sub")
    barrier = pltpu.get_barrier_semaphore()
    for hop in range(1, heads):
        pl.semaphore_signal(
            barrier, inc=1, device_id={"head": lax.rem(head + hop, heads)}, device_id_type=MESH
        )
    for hop in range(1, subs):
        pl.semaphore_signal(
            barrier, inc=1, device_id={"sub": lax.rem(sub + hop, subs)}, device_id_type=MESH
        )
    pl.semaphore_wait(barrier, heads + subs - 2)
    size = attn.shape[0] // chunks

    def to_head(hop, chunk):
        rows = pl.ds(chunk * size, size)
        return pltpu.make_async_remote_copy(
            src_ref=attn.at[rows],
            dst_ref=slots.at[hop, 0, rows],
            send_sem=x_sems.at[hop, 0, chunk],
            recv_sem=x_sems.at[hop, 1, chunk],
            device_id={"head": lax.rem(head + hop, heads)},
            device_id_type=MESH,
        )

    def to_sub(hop, turn, chunk):
        rows = pl.ds(chunk * size, size)
        return pltpu.make_async_remote_copy(
            src_ref=attn.at[rows] if hop == 0 else slots.at[hop, 0, rows],
            dst_ref=slots.at[hop, turn, rows],
            send_sem=c_sems.at[hop, turn, 0, chunk],
            recv_sem=c_sems.at[hop, turn, 1, chunk],
            device_id={"sub": lax.rem(sub + turn, subs)},
            device_id_type=MESH,
        )

    for chunk in range(chunks):
        for hop in range(1, heads):
            to_head(hop, chunk).start()
        for turn in range(1, subs):
            to_sub(0, turn, chunk).start()

    def add(chunk, hop, turn, first):
        rows = slice(chunk * size, (chunk + 1) * size)
        owner = lax.rem(head + heads - hop, heads) * subs + lax.rem(sub + subs - turn, subs)
        block = attn[rows, :] if hop == 0 and turn == 0 else slots[hop, turn, rows, :]
        product = jnp.dot(block, w_all[owner], preferred_element_type=jnp.float32)
        total[rows, :] = product if first else total[rows, :] + product

    for chunk in range(chunks):
        add(chunk, 0, 0, True)
    for chunk in range(chunks):
        for turn in range(1, subs):
            to_sub(0, turn, chunk).wait_recv()
            add(chunk, 0, turn, False)
    for chunk in range(chunks):
        for hop in range(1, heads):
            to_head(hop, chunk).wait_recv()
            for turn in range(1, subs):
                to_sub(hop, turn, chunk).start()
            add(chunk, hop, 0, False)
    for chunk in range(chunks):
        for hop in range(1, heads):
            for turn in range(1, subs):
                to_sub(hop, turn, chunk).wait_recv()
                add(chunk, hop, turn, False)
        rows = slice(chunk * size, (chunk + 1) * size)
        update[rows, :] = (gate[...] * total[rows, :]).astype(update.dtype)
    for chunk in range(chunks):
        for hop in range(1, heads):
            to_head(hop, chunk).wait_send()
        for hop in range(heads):
            for turn in range(1, subs):
                to_sub(hop, turn, chunk).wait_send()


def mix(attention, w_all, gate):
    heads, subs = lax.axis_size("head"), lax.axis_size("sub")
    rows, width = attention.shape
    chunks = pieces_of(rows, 2)
    vmem = pl.BlockSpec(memory_space=pltpu.VMEM)
    return pl.pallas_call(
        functools.partial(mix_kernel, heads, subs, chunks),
        out_shape=jax.ShapeDtypeStruct((rows, w_all.shape[-1]), jnp.bfloat16),
        in_specs=[vmem] * 3,
        out_specs=vmem,
        scratch_shapes=[
            pltpu.VMEM((heads, subs, rows, width), jnp.bfloat16),
            pltpu.VMEM((rows, w_all.shape[-1]), jnp.float32),
            pltpu.SemaphoreType.DMA((heads, 2, chunks)),
            pltpu.SemaphoreType.DMA((heads, subs, 2, chunks)),
        ],
        compiler_params=pltpu.CompilerParams(
            collective_id=1, has_side_effects=True, vmem_limit_bytes=40 * 1024 * 1024
        ),
        name="mix",
    )(attention, w_all, gate)


def modulate(tokens, modulation):
    values = tokens.astype(jnp.float32)
    center = jnp.mean(values, axis=-1, keepdims=True)
    spread = jnp.mean(jnp.square(values - center), axis=-1, keepdims=True)
    normed = (values - center) * lax.rsqrt(spread + EPSILON)
    return (normed * (1.0 + modulation[1]) + modulation[0]).astype(jnp.bfloat16)


def shards(tokens, modulation, w_qkv, w_out, pattern, counts, spatial_mask):
    row_count, feature_width = tokens.shape
    pairs_local = w_qkv.shape[1]
    head_size = w_qkv.shape[2] // 6
    frames_local = spatial_mask.shape[0]
    positions = row_count // frames_local
    slot_total = pattern.shape[1]
    scale_factor = 1.0 / math.sqrt(head_size)
    hidden = modulate(tokens, modulation)
    projected, whole_out = project(hidden, w_qkv.reshape(w_qkv.shape[0], -1), w_out)
    packed = projected.reshape(
        frames_local, positions, pairs_local, 6 * head_size
    )
    temporal_in = packed[..., : 3 * head_size].transpose(1, 0, 2, 3)
    received = lax.all_to_all(temporal_in, "seq", split_axis=0, concat_axis=1, tiled=True)
    position_span, frame_total, items, _ = received.shape
    relaid = received.reshape(position_span * frame_total, items, 3 * head_size)
    extended = with_halo(relaid[:, :, head_size:], (("seq", 0),), WIN * BLOCK)
    block_count = position_span * frame_total // BLOCK
    key_table = extended.reshape(block_count + 2 * WIN, BLOCK, items, 2 * head_size)
    queries = relaid[:, :, :head_size].reshape(block_count, BLOCK, items, head_size)
    offsets = pattern - (lax.axis_index("seq") * block_count - WIN)

    def slot_step(slot_index, state_pair):
        numerator, denominator = state_pair
        chosen = lax.dynamic_index_in_dim(offsets, slot_index, 1, keepdims=False)
        picked = jnp.take(key_table, chosen, axis=0)
        scores = (
            jnp.einsum(
                "bqnc,bknc->bnqk",
                queries,
                picked[..., :head_size],
                preferred_element_type=jnp.float32,
            )
            * scale_factor
        )
        alive = (slot_index < counts).astype(jnp.float32)
        weights = jnp.exp(scores) * alive[:, None, None, None]
        numerator = numerator + jnp.einsum(
            "bnqk,bknc->bnqc",
            weights.astype(jnp.bfloat16),
            picked[..., head_size:],
            preferred_element_type=jnp.float32,
        )
        return (numerator, denominator + jnp.sum(weights, axis=-1))

    start_state = (
        jnp.zeros((block_count, items, BLOCK, head_size), jnp.float32),
        jnp.zeros((block_count, items, BLOCK), jnp.float32),
    )
    numerator, denominator = lax.fori_loop(0, slot_total, slot_step, start_state)
    outcome = (numerator / denominator[..., None]).astype(jnp.bfloat16)
    outcome = outcome.transpose(0, 2, 1, 3).reshape(position_span, frame_total, items, head_size)
    temporal_out = lax.all_to_all(outcome, "seq", split_axis=1, concat_axis=0, tiled=True)
    spatial = packed[..., 3 * head_size :]
    blocks_frame = positions // BLOCK
    scores = (
        jnp.einsum(
            "fpnc,fqnc->fnpq",
            spatial[..., :head_size],
            spatial[..., head_size : 2 * head_size],
            preferred_element_type=jnp.float32,
        )
        * scale_factor
    )
    keep = spatial_mask.astype(jnp.float32)[:, None, :, None, :, None]
    weights = (
        jnp.exp(scores).reshape(frames_local, pairs_local, blocks_frame, BLOCK, blocks_frame, BLOCK)
        * keep
    )
    weights = weights.reshape(frames_local, pairs_local, positions, positions)
    denominator = jnp.sum(weights, axis=-1)
    numerator = jnp.einsum(
        "fnpq,fqnc->fpnc",
        weights.astype(jnp.bfloat16),
        spatial[..., 2 * head_size :],
        preferred_element_type=jnp.float32,
    )
    spatial_out = (numerator / denominator.transpose(0, 2, 1)[..., None]).astype(jnp.bfloat16)
    attention = jnp.concatenate([temporal_out.transpose(1, 0, 2, 3), spatial_out], axis=-1)
    attention = attention.reshape(row_count, pairs_local * 2 * head_size)
    out_width = w_out.shape[1]
    blocks = lax.axis_size("head") * lax.axis_size("sub")
    gate_slice = lax.dynamic_slice_in_dim(
        modulation[2], lax.axis_index(("head", "sub")) * out_width, out_width, 0
    )
    return mix(attention, whole_out.reshape(blocks, -1, out_width), gate_slice[None, :])

def push(source, target, send_sem, recv_sem, axis, place):
    return pltpu.make_async_remote_copy(
        src_ref=source,
        dst_ref=target,
        send_sem=send_sem,
        recv_sem=recv_sem,
        device_id={axis: place},
        device_id_type=MESH,
    )


def seats(count):
    return (count // 2 - 1, count // 2)


def by_pair_kernel(
    sizes, chunks, pieces, o_chunks,
    tokens, modulation, w_own, o_own, pattern, counts, mask, update,
    held, raw, stage, hfull, wfull, tq, sq, o_all, lists, lists_all, table, own, slots,
    tok_sems, l_sems, w_sems, z_sems, x_sems, c_sems, o_sems, keep_sems, sz_sems, sx_sems, sc_sems, own_sems,
):
    count, parts, heads, subs = sizes
    low, high = seats(count)
    me, group = lax.axis_index("seq"), lax.axis_index("groups")
    head, sub = lax.axis_index("head"), lax.axis_index("sub")
    other = low + high - me
    near = jnp.where(me == low, low - 1, high + 1)
    far = jnp.where(me == low, high + 1, low - 1)
    seated = jnp.logical_or(me == low, me == high)
    ended = jnp.logical_not(seated)
    outward = jnp.where(me == low, 1, 0)
    blocks = heads * subs
    quarter = held.shape[1]
    unit = quarter // chunks
    width = wfull.shape[2]
    half = w_own.shape[0] // parts
    piece = half // pieces
    block = unit * blocks

    barrier = pltpu.get_barrier_semaphore()
    others = 0
    for axis in ("seq", "groups", "head", "sub"):
        size = lax.axis_size(axis)
        for hop in range(1, size):
            partner = lax.rem(lax.axis_index(axis) + hop, size)
            pl.semaphore_signal(barrier, inc=1, device_id={axis: partner}, device_id_type=MESH)
            others += 1

    def rows_of(head_hop, sub_hop, chunk):
        owner = lax.rem(head + heads - head_hop, heads) * subs + lax.rem(sub + subs - sub_hop, subs)
        return pl.ds(pl.multiple_of((chunk * blocks + owner) * unit, unit), unit)

    def fetch(hop, chunk):
        return pltpu.make_async_copy(
            tokens.at[rows_of(hop, 0, chunk)], held.at[hop, pl.ds(chunk * unit, unit)],
            tok_sems.at[hop, chunk],
        )

    for chunk in range(chunks):
        fetch(0, chunk).start()
    raw_copy = pltpu.make_async_copy(w_own, raw, own_sems.at[0])
    raw_copy.start()
    o_copy = pltpu.make_async_copy(o_own, o_all.at[me], own_sems.at[1])
    o_copy.start()

    @pl.when(seated)
    def _():
        for hop in range(1, heads):
            for chunk in range(chunks):
                fetch(hop, chunk).start()

    lists[...] = jnp.zeros_like(lists)
    slots_of = pattern.shape[1]
    lists[0 : pattern.shape[0], 0:slots_of] = pattern[...]
    lists[8 : 8 + mask.shape[0], 0 : mask.shape[1]] = mask[...]
    lists[16:17, 0 : counts.shape[1]] = counts[...]
    gain = 1.0 + modulation[1:2, :]
    shift = modulation[0:1, :]

    def modulate_rows(hop):
        def some(i, carry):
            at = pl.ds(pl.multiple_of(i * 16, 16), 16)
            chunk = i // (unit // 16)
            owner = lax.rem(head + heads - hop, heads) * subs + sub
            start = (chunk * blocks + owner) * unit + lax.rem(i, unit // 16) * 16
            values = held[hop, at, :].astype(jnp.float32)
            centered = values - jnp.mean(values, axis=-1, keepdims=True)
            spread_of = jnp.mean(jnp.square(centered), axis=-1, keepdims=True)
            normed = centered * lax.rsqrt(spread_of + EPSILON)
            hfull[me, pl.ds(pl.multiple_of(start, 16), 16), :] = (normed * gain + shift).astype(hfull.dtype)
            return carry

        for chunk in range(chunks):
            fetch(hop, chunk).wait()
        lax.fori_loop(0, quarter // 16, some, 0, unroll=4)

    modulate_rows(0)
    pl.semaphore_wait(barrier, others)

    def spot(frame, head_hop, sub_hop, chunk):
        return hfull.at[frame, rows_of(head_hop, sub_hop, chunk)]

    def z_push(frame, chunk, place):
        target = spot(frame, 0, 0, chunk)
        return push(target, target, z_sems.at[0, frame, chunk], z_sems.at[1, frame, chunk], "seq", place)

    def x_push(frame, chunk, hop):
        target = spot(frame, 0, 0, chunk)
        return push(
            target, target, x_sems.at[hop, 0, frame, chunk], x_sems.at[hop, 1, frame, chunk],
            "head", lax.rem(head + hop, heads),
        )

    def c_push(frame, chunk, hop, turn):
        target = spot(frame, hop, 0, chunk)
        return push(
            target, target, c_sems.at[hop, turn, 0, frame, chunk], c_sems.at[hop, turn, 1, frame, chunk],
            "sub", lax.rem(sub + turn, subs),
        )

    def l_push(seat):
        return push(lists, lists_all.at[me], l_sems.at[0, seat - low], l_sems.at[1, me], "seq", seat)

    def w_rows(part, step):
        return pl.ds(pl.multiple_of(part * half + step * piece, piece), piece)

    def w_along(seat, source, step):
        return push(
            stage.at[seat - low, pl.ds(step * piece, piece)], wfull.at[source, w_rows(group, step)],
            w_sems.at[0, 0, seat - low, step], w_sems.at[0, 1, source, step], "seq", seat,
        )

    def w_across(source, step, turn):
        target = wfull.at[source, w_rows(group, step)]
        return push(
            target, target, w_sems.at[turn, 0, source, step], w_sems.at[turn, 1, source, step],
            "groups", lax.rem(group + turn, parts),
        )

    outs = LineGather(o_all, o_sems, o_chunks, count, parts)

    for seat in (low, high):
        @pl.when(me != seat)
        def _():
            l_push(seat).start()

    @pl.when(seated)
    def _():
        for chunk in range(chunks):
            z_push(me, chunk, other).start()
            for turn in range(1, subs):
                c_push(me, chunk, 0, turn).start()

    @pl.when(ended)
    def _():
        for chunk in range(chunks):
            z_push(me, chunk, jnp.where(me < low, low, high)).start()

    raw_copy.wait()

    def unpack(i, carry):
        start = pl.multiple_of(i * 64, 64)
        both = raw[pl.ds(pl.multiple_of(group * half + start, 64), 64)]
        first, second = both[:, 0, :], both[:, 1, :]
        stage[0, pl.ds(start, 64), :] = first
        stage[1, pl.ds(start, 64), :] = second
        return carry

    lax.fori_loop(0, half // 64, unpack, 0)

    @pl.when(seated)
    def _():
        for step in range(pieces):
            w_along(other, me, step).start()

    @pl.when(ended)
    def _():
        for seat in (jnp.where(me < low, high, low), jnp.where(me < low, low, high)):
            for step in range(pieces):
                w_along(seat, me, step).start()

    o_copy.wait()

    @pl.when(ended)
    def _():
        for way in (0, 1):
            outs.open_way(way)
        for step in range(1, count):
            for way in (0, 1):
                outs.relay(step, way)

    @pl.when(seated)
    def _():
        for way in (0, 1):
            @pl.when(outward == way)
            def _():
                outs.open_way(way)

        keep = pltpu.make_async_copy(lists, lists_all.at[me], own_sems.at[2])
        keep.start()
        for hop in range(1, heads):
            modulate_rows(hop)
            for chunk in range(chunks):
                for turn in range(1, subs):
                    c_push(me, chunk, hop, turn).start()

        def land(frame, chunk, onward):
            z_push(frame, chunk, other).wait_recv()
            for hop in range(1, heads):
                x_push(frame, chunk, hop).start()
            for turn in range(1, subs):
                c_push(frame, chunk, 0, turn).start()
            if onward:
                z_push(frame, chunk, other).start()

        def crossed(frame, chunk):
            for hop in range(1, heads):
                x_push(frame, chunk, hop).wait_recv()
                for turn in range(1, subs):
                    c_push(frame, chunk, hop, turn).start()

        def gathered(frame, chunk):
            for hop in range(heads):
                for turn in range(1, subs):
                    c_push(frame, chunk, hop, turn).wait_recv()

        def keep_pair(i, carry):
            at = pl.ds(pl.multiple_of(i * 64, 64), 64)
            both = raw[at]
            wfull[me, at, :] = jnp.where(me == low, both[:, 0, :], both[:, 1, :])
            return carry

        land(near, 0, True)
        land(other, 0, False)
        lax.fori_loop(0, w_own.shape[0] // 64, keep_pair, 0)
        for chunk in range(1, chunks):
            land(near, chunk, True)
            land(other, chunk, False)

        def w_land(source, step):
            w_along(me, source, step).wait_recv()
            for turn in range(1, parts):
                w_across(source, step, turn).start()

        marks = [(source, step) for step in range(pieces) for source in (other, far, near)]
        ahead = [(frame, chunk) for chunk in range(chunks) for frame in (near, other)]
        for i in range(max(len(marks), len(ahead))):
            if i < len(ahead):
                crossed(*ahead[i])
            if i < len(marks):
                w_land(*marks[i])

        for source in (near, other, far):
            l_push_from(lists_all, lists, l_sems, source, low, me).wait_recv()
        keep.wait()
        to_table = pltpu.make_async_copy(lists_all, table, own_sems.at[3])
        to_table.start()

        span = unit
        scale = math.log2(math.e) / math.sqrt(own.shape[2] // 2)
        size = own.shape[2] // 2
        total_blocks = tq.shape[0]
        each = total_blocks // count
        window = 2 * WIN + 1

        def project(frame, chunk):
            rows = pl.ds(pl.multiple_of(chunk * block, block), block)
            total = jnp.dot(
                hfull[frame, rows, :], wfull[...].reshape(-1, width), preferred_element_type=jnp.float32
            ).astype(tq.dtype)
            at = pl.ds(pl.multiple_of(frame * span, span), span)
            for i in range(blocks):
                tq[chunk * blocks + i, at, :] = total[i * span : (i + 1) * span, : 3 * size]
            sq[frame, rows, :] = total[:, 3 * size :]

        def project_frame(frame):
            lax.fori_loop(0, chunks, lambda chunk, carry: (project(frame, chunk), carry)[1], 0)

        def soft(q, keys, values, biases):
            scores = lax.dot_general(
                q, keys, (((1,), (1,)), ((), ())), preferred_element_type=jnp.float32
            )
            parts_of = []
            sums = None
            for i, bias in enumerate(biases):
                weight = jnp.exp2(scores[:, i * BLOCK : (i + 1) * BLOCK] * scale + bias)
                sums = weight if sums is None else sums + weight
                parts_of.append(weight.astype(jnp.bfloat16))
            numerator = jnp.dot(
                jnp.concatenate(parts_of, axis=1), values, preferred_element_type=jnp.float32
            )
            return (numerator / jnp.sum(sums, axis=-1, keepdims=True)).astype(own.dtype)

        def temporal(chunk):
            def query(i, carry):
                b = chunk * blocks + i
                device, row = b // each, lax.rem(b, each)
                start = jnp.clip(b - WIN, 0, total_blocks - window)
                used = table[device, 16, row]
                biases = []
                for w in range(window):
                    times = 0
                    for j in range(slots_of):
                        hit = jnp.logical_and(j < used, table[device, row, j] == start + w)
                        times = times + jnp.where(hit, 1, 0)
                    bias = jnp.float32(-jnp.inf)
                    for m in range(1, slots_of + 1):
                        bias = jnp.where(times == m, jnp.float32(math.log2(m)), bias)
                    biases.append(bias)
                near_by = pl.ds(start, window)
                result = soft(
                    tq[b, :, :size],
                    tq[near_by, :, size : 2 * size].reshape(-1, size),
                    tq[near_by, :, 2 * size :].reshape(-1, size),
                    biases,
                )
                at = pl.ds(pl.multiple_of(b * span, span), span)
                for f in range(count):
                    own[f, at, :size] = result[f * span : (f + 1) * span]
                return carry

            lax.fori_loop(0, blocks, query, 0)

        def spatial(frame):
            per = sq.shape[1] // BLOCK

            def query(i, carry):
                at = pl.ds(pl.multiple_of(i * BLOCK, BLOCK), BLOCK)
                biases = [
                    jnp.where(table[frame, 8 + i, j] > 0, jnp.float32(0), jnp.float32(-jnp.inf))
                    for j in range(per)
                ]
                own[frame, at, size:] = soft(
                    sq[frame, at, :size], sq[frame, :, size : 2 * size], sq[frame, :, 2 * size :], biases
                )
                return carry

            lax.fori_loop(0, per, query, 0)

        def send(frame, chunk):
            out_push(own, slots, sz_sems, me, frame, chunk, block, low).start()

        def settle(chunk):
            send(near, chunk)
            send(other, chunk)
            keep_out(own, slots, keep_sems, me, chunk, block, low).start()

        early = (me, near, other)
        for chunk in range(chunks + 1):
            if chunk < chunks:
                land(far, chunk, False)
            if chunk:
                crossed(far, chunk - 1)
            if chunk == 0:
                for source in (other, near, far):
                    for step in range(pieces):
                        for turn in range(1, parts):
                            w_across(source, step, turn).wait_recv()
                for earlier in range(chunks):
                    gathered(me, earlier)
                    gathered(near, earlier)
                    gathered(other, earlier)
                to_table.wait()
            if chunk < len(early):
                project_frame(early[chunk])
            if chunk and chunk <= len(early):
                spatial(early[chunk - 1])
            if chunk:
                gathered(far, chunk - 1)
                project(far, chunk - 1)
            if chunk == chunks - 2:
                for way in (0, 1):
                    @pl.when(outward != way)
                    def _():
                        outs.open_way(way)
            if chunk == chunks - 1:
                for way in (0, 1):
                    @pl.when(outward != way)
                    def _():
                        outs.relay(1, way)
            if chunk >= max(2, len(early)):
                for ready in range(chunk - 2 if chunk > max(2, len(early)) else 0, chunk - 1):
                    temporal(ready)
                    settle(ready)
        temporal(chunks - 1)
        settle(chunks - 1)
        spatial(far)
        for chunk in range(chunks):
            send(far, chunk)
        for way in (0, 1):
            @pl.when(outward == way)
            def _():
                outs.relay(1, way)
                outs.relay(2, way)

    columns_of = own.shape[2]

    def item(hop, turn, seat, chunk):
        return out_spot(slots, hop, turn, seat, chunk, block, low, columns_of)

    def to_head(hop, seat, chunk):
        return push(
            item(0, 0, seat, chunk), item(hop, 0, seat, chunk),
            sx_sems.at[hop, 0, seat - low, chunk], sx_sems.at[hop, 1, seat - low, chunk],
            "head", lax.rem(head + hop, heads),
        )

    def to_sub(hop, turn, seat, chunk):
        return push(
            item(hop, 0, seat, chunk), item(hop, turn, seat, chunk),
            sc_sems.at[hop, turn, 0, seat - low, chunk], sc_sems.at[hop, turn, 1, seat - low, chunk],
            "sub", lax.rem(sub + turn, subs),
        )

    def arrive(chunk, seat):
        @pl.when(me == seat)
        def _():
            keep_out(own, slots, keep_sems, seat, chunk, block, low).wait()

        @pl.when(me != seat)
        def _():
            out_push(own, slots, sz_sems, seat, me, chunk, block, low).wait_recv()

        for hop in range(1, heads):
            to_head(hop, seat, chunk).start()
        for turn in range(1, subs):
            to_sub(0, turn, seat, chunk).start()

    def pass_on(chunk, seat):
        for hop in range(1, heads):
            to_head(hop, seat, chunk).wait_recv()
            for turn in range(1, subs):
                to_sub(hop, turn, seat, chunk).start()

    columns = pl.ds(pl.multiple_of((head * subs + sub) * update.shape[1], 128), update.shape[1])
    gate = modulation[2:3, columns]

    def finish(chunk):
        for seat in (low, high):
            for hop in range(heads):
                for turn in range(1, subs):
                    to_sub(hop, turn, seat, chunk).wait_recv()
        rows = slice(chunk * block, (chunk + 1) * block)
        total = None
        for hop in range(heads):
            for turn in range(subs):
                owner = lax.rem(head + heads - hop, heads) * subs + lax.rem(sub + subs - turn, subs)
                product = jnp.dot(slots[hop, turn, rows, :], o_all[owner], preferred_element_type=jnp.float32)
                total = product if total is None else total + product
        update[rows, :] = (gate * total).astype(update.dtype)

    listed = [(chunk, seat) for chunk in range(chunks) for seat in (low, high)]
    for n, (chunk, seat) in enumerate(listed):
        arrive(chunk, seat)
        if n:
            pass_on(*listed[n - 1])
        if n == 2:
            for step in range(1, count):
                for way in (0, 1):
                    @pl.when(outs.present(step, way))
                    def _():
                        outs.complete(outs.shard_of(step, way))
        if chunk and seat == high:
            finish(chunk - 1)
    pass_on(*listed[-1])
    finish(chunks - 1)

    for seat in (low, high):
        @pl.when(me != seat)
        def _():
            l_push(seat).wait_send()
            for step in range(pieces):
                w_along(seat, me, step).wait_send()

    @pl.when(ended)
    def _():
        for chunk in range(chunks):
            z_push(me, chunk, jnp.where(me < low, low, high)).wait_send()

    @pl.when(seated)
    def _():
        for chunk in range(chunks):
            z_push(me, chunk, other).wait_send()
            z_push(near, chunk, other).wait_send()
            for frame in (me, near, other, far):
                for hop in range(heads):
                    for turn in range(1, subs):
                        c_push(frame, chunk, hop, turn).wait_send()
            for frame in (near, other, far):
                for hop in range(1, heads):
                    x_push(frame, chunk, hop).wait_send()
                out_push(own, slots, sz_sems, me, frame, chunk, block, low).wait_send()
        for source in (near, other, far):
            for step in range(pieces):
                for turn in range(1, parts):
                    w_across(source, step, turn).wait_send()

    for way in (0, 1):
        outs.close_way(way)
    for step in range(1, count):
        for way in (0, 1):
            outs.close_sends(step, way)
    for chunk in range(chunks):
        for seat in (low, high):
            for hop in range(1, heads):
                to_head(hop, seat, chunk).wait_send()
            for hop in range(heads):
                for turn in range(1, subs):
                    to_sub(hop, turn, seat, chunk).wait_send()


def l_push_from(lists_all, lists, l_sems, source, low, me):
    return push(lists, lists_all.at[source], l_sems.at[0, me - low], l_sems.at[1, source], "seq", me)


def out_spot(slots, hop, turn, seat, chunk, block, low, columns):
    at = (seat - low) * columns
    at = pl.ds(pl.multiple_of(at, columns), columns)
    return slots.at[hop, turn, pl.ds(chunk * block, block), at]


def out_push(own, slots, sems, seat, frame, chunk, block, low):
    return push(
        own.at[frame, pl.ds(chunk * block, block)],
        out_spot(slots, 0, 0, seat, chunk, block, low, own.shape[2]),
        sems.at[0, frame, chunk], sems.at[1, seat, chunk], "seq", frame,
    )


def keep_out(own, slots, sems, seat, chunk, block, low):
    return pltpu.make_async_copy(
        own.at[seat, pl.ds(chunk * block, block)],
        out_spot(slots, 0, 0, seat, chunk, block, low, own.shape[2]),
        sems.at[chunk],
    )


class LineGather:
    def __init__(self, slots, sems, chunks, count, parts):
        self.slots, self.chunks = slots, chunks
        self.sems, self.count, self.parts = sems, count, parts
        self.me = lax.axis_index("seq")
        self.group = lax.axis_index("groups")
        self.size = slots.shape[1] // (parts * chunks)

    def rows(self, group, chunk):
        start = (group * self.chunks + chunk) * self.size
        return pl.ds(pl.multiple_of(start, self.size), self.size)

    def along(self, shard, chunk, way):
        rows = self.rows(self.group, chunk)
        return push(
            self.slots.at[shard, rows], self.slots.at[shard, rows],
            self.sems.at[way, 0, shard, chunk], self.sems.at[way, 1, shard, chunk],
            "seq", self.me + (1 if way == 0 else -1),
        )

    def across(self, shard, chunk, hop):
        rows = self.rows(self.group, chunk)
        return push(
            self.slots.at[shard, rows], self.slots.at[shard, rows],
            self.sems.at[1 + hop, 0, shard, chunk], self.sems.at[1 + hop, 1, shard, chunk],
            "groups", lax.rem(self.group + hop, self.parts),
        )

    def onward(self, way):
        return self.me < self.count - 1 if way == 0 else self.me > 0

    def shard_of(self, step, way):
        return self.me - step if way == 0 else self.me + step

    def present(self, step, way):
        return self.me >= step if way == 0 else self.me + step < self.count

    def open_way(self, way):
        @pl.when(self.onward(way))
        def _():
            for chunk in range(self.chunks):
                self.along(self.me, chunk, way).start()

    def relay(self, step, way):
        shard = self.shard_of(step, way)

        @pl.when(self.present(step, way))
        def _():
            for chunk in range(self.chunks):
                self.along(shard, chunk, way).wait_recv()

                @pl.when(self.onward(way))
                def _():
                    self.along(shard, chunk, way).start()

                for hop in range(1, self.parts):
                    self.across(shard, chunk, hop).start()

    def complete(self, shard):
        for chunk in range(self.chunks):
            for hop in range(1, self.parts):
                self.across(shard, chunk, hop).wait_recv()

    def close_sends(self, step, way):
        shard = self.shard_of(step, way)

        @pl.when(self.present(step, way))
        def _():
            for chunk in range(self.chunks):
                @pl.when(self.onward(way))
                def _():
                    self.along(shard, chunk, way).wait_send()

                for hop in range(1, self.parts):
                    self.across(shard, chunk, hop).wait_send()

    def close_way(self, way):
        @pl.when(self.onward(way))
        def _():
            for chunk in range(self.chunks):
                self.along(self.me, chunk, way).wait_send()


def by_pair(tokens, modulation, w_own, o_own, pattern, counts, mask):
    sizes = tuple(lax.axis_size(axis) for axis in ("seq", "groups", "head", "sub"))
    count, parts, heads, subs = sizes
    rows, depth = tokens.shape
    width = w_own.shape[2]
    blocks = heads * subs
    quarter = rows // blocks
    chunks = rows // BLOCK
    pieces = 2
    o_chunks = 2
    columns = width // 3
    seated = len(seats(count))
    vmem = pl.BlockSpec(memory_space=pltpu.VMEM)
    whole = pl.BlockSpec(memory_space=pl.ANY)
    dma = pltpu.SemaphoreType.DMA
    kept = jnp.bfloat16
    return pl.pallas_call(
        functools.partial(by_pair_kernel, sizes, chunks, pieces, o_chunks),
        out_shape=jax.ShapeDtypeStruct((rows, o_own.shape[1]), kept),
        in_specs=[whole, vmem, whole, whole, vmem, vmem, vmem],
        out_specs=vmem,
        scratch_shapes=[
            pltpu.VMEM((heads, quarter, depth), kept),
            pltpu.VMEM(w_own.shape, kept),
            pltpu.VMEM((seated, w_own.shape[0] // parts, width), kept),
            pltpu.VMEM((count, rows, depth), kept),
            pltpu.VMEM((count, w_own.shape[0], width), kept),
            pltpu.VMEM((count * rows // BLOCK, BLOCK, width // 2), kept),
            pltpu.VMEM((count, rows, width // 2), kept),
            pltpu.VMEM((count,) + o_own.shape, kept),
            pltpu.VMEM((24, 128), jnp.int32),
            pltpu.VMEM((count, 24, 128), jnp.int32),
            pltpu.SMEM((count, 24, 128), jnp.int32),
            pltpu.VMEM((count, rows, columns), kept),
            pltpu.VMEM((heads, subs, rows, seated * columns), kept),
            dma((heads, chunks)),
            dma((2, count)),
            dma((parts, 2, count, pieces)),
            dma((2, count, chunks)),
            dma((heads, 2, count, chunks)),
            dma((heads, subs, 2, count, chunks)),
            dma((1 + parts, 2, count, o_chunks)),
            dma((chunks,)),
            dma((2, count, chunks)),
            dma((heads, 2, seated, chunks)),
            dma((heads, subs, 2, seated, chunks)),
            dma((4,)),
        ],
        compiler_params=pltpu.CompilerParams(
            collective_id=2, has_side_effects=True, vmem_limit_bytes=60 * 1024 * 1024
        ),
        name="by_pair",
    )(tokens, modulation, w_own, o_own, pattern, counts, mask)


def shards_by_pair(tokens, modulation, w_qkv, w_out, pattern, counts, spatial_mask):
    return by_pair(tokens, modulation, w_qkv, w_out, pattern, counts[None, :], spatial_mask[0])


def one_pair_each(count, blocks, parts, tokens, w_qkv, w_out, pattern, spatial_mask):
    rows, frames = tokens.shape[0], spatial_mask.shape[0]
    return (
        count == blocks == 4
        and w_qkv.shape[1] == len(seats(count))
        and frames == 1
        and rows == BLOCK * pattern.shape[0] == BLOCK * spatial_mask.shape[1]
        and pattern.shape[0] < 8
        and BLOCK % (16 * count) == 0
        and w_qkv.shape[0] % (128 * parts) == 0
        and w_out.shape[0] % (32 * parts) == 0
    )


def shards_any(*args):
    tokens, _, w_qkv, w_out, pattern, _, spatial_mask = args
    blocks = lax.axis_size("head") * lax.axis_size("sub")
    sizes = lax.axis_size("seq"), blocks, lax.axis_size("groups")
    if one_pair_each(*sizes, tokens, w_qkv, w_out, pattern, spatial_mask):
        return shards_by_pair(*args)
    return shards(*args)


def solution(mesh):
    return jax.shard_map(
        shards_any,
        mesh=mesh,
        in_specs=(
            P(("groups", "seq"), None),
            P(),
            P("seq", ("head", "sub"), None),
            P("seq", ("head", "sub")),
            P(("groups", "seq"), None),
            P(("groups", "seq")),
            P(("groups", "seq"), None, None),
        ),
        out_specs=P(("groups", "seq"), ("head", "sub")),
        check_vma=False,
    )
```

```python
import functools
import math

import jax
import jax.numpy as jnp
from jax import lax
from jax.experimental import pallas as pl
from jax.experimental.pallas import tpu as pltpu
from jax.sharding import PartitionSpec as P

BLOCK = 128
WIN = 2


EPSILON = 1e-06


def with_halo(cells, sides, width):
    for axis, dim in sides:
        count = lax.axis_size(axis)
        ends = count - 1
        head = lax.slice_in_dim(cells, 0, width, axis=dim)
        tail = lax.slice_in_dim(cells, cells.shape[dim] - width, cells.shape[dim], axis=dim)
        cells = jnp.concatenate(
            [
                lax.ppermute(tail, axis, [(i, (i + 1) % count) for i in range(ends)]),
                cells,
                lax.ppermute(head, axis, [((i + 1) % count, i) for i in range(ends)]),
            ],
            axis=dim,
        )
    return cells


MESH = pl.DeviceIdType.MESH


def pieces_of(rows, most=4):
    for count in range(most, 0, -1):
        if rows % (16 * count) == 0:
            return count
    return 1


class ShardLine:
    def __init__(self, own, slots, sems, chunks, count, parts):
        self.own, self.slots, self.chunks = own, slots, chunks
        self.sems, self.count, self.parts = sems, count, parts
        self.me = lax.axis_index("seq")
        self.group = lax.axis_index("groups")
        self.size = own.shape[0] // (parts * chunks)

    def rows(self, group, chunk):
        start = (group * self.chunks + chunk) * self.size
        return pl.ds(pl.multiple_of(start, self.size), self.size)

    def along(self, shard, chunk, way, own):
        rows = self.rows(self.group, chunk)
        source = self.own.at[rows] if own else self.slots.at[shard, rows]
        return pltpu.make_async_remote_copy(
            src_ref=source,
            dst_ref=self.slots.at[shard, rows],
            send_sem=self.sems.at[way, 0, shard, chunk],
            recv_sem=self.sems.at[way, 1, shard, chunk],
            device_id={"seq": self.me + (1 if way == 0 else -1)},
            device_id_type=MESH,
        )

    def across(self, shard, chunk, hop):
        rows = self.rows(self.group, chunk)
        return pltpu.make_async_remote_copy(
            src_ref=self.slots.at[shard, rows],
            dst_ref=self.slots.at[shard, rows],
            send_sem=self.sems.at[1 + hop, 0, shard, chunk],
            recv_sem=self.sems.at[1 + hop, 1, shard, chunk],
            device_id={"groups": lax.rem(self.group + hop, self.parts)},
            device_id_type=MESH,
        )

    def open_line(self):
        for chunk in range(self.chunks):
            for way in (0, 1):
                @pl.when(self.onward(way))
                def _():
                    self.along(self.me, chunk, way, True).start()

    def onward(self, way):
        return self.me < self.count - 1 if way == 0 else self.me > 0

    def shard_of(self, step, way):
        return self.me - step if way == 0 else self.me + step

    def present(self, step, way):
        return self.me >= step if way == 0 else self.me + step < self.count

    def relay(self, step):
        for chunk in range(self.chunks):
            for way in (0, 1):
                shard = self.shard_of(step, way)

                @pl.when(self.present(step, way))
                def _():
                    self.along(shard, chunk, way, False).wait_recv()

                    @pl.when(self.onward(way))
                    def _():
                        self.along(shard, chunk, way, False).start()

                    for hop in range(1, self.parts):
                        self.across(shard, chunk, hop).start()

    def complete(self, shard):
        for chunk in range(self.chunks):
            for hop in range(1, self.parts):
                self.across(shard, chunk, hop).wait_recv()

    def close_sends(self, step):
        for chunk in range(self.chunks):
            for way in (0, 1):
                shard = self.shard_of(step, way)

                @pl.when(self.present(step, way))
                def _():
                    @pl.when(self.onward(way))
                    def _():
                        self.along(shard, chunk, way, False).wait_send()

                    for hop in range(1, self.parts):
                        self.across(shard, chunk, hop).wait_send()

    def close_own(self):
        for chunk in range(self.chunks):
            for way in (0, 1):
                @pl.when(self.onward(way))
                def _():
                    self.along(self.me, chunk, way, True).wait_send()


def project_kernel(count, parts, q_chunks, o_chunks, hidden, w_own, o_own, qkv, o_all, slots, total, q_sems, o_sems, own_sem):
    me = lax.axis_index("seq")
    group = lax.axis_index("groups")
    barrier = pltpu.get_barrier_semaphore()

    @pl.when(me > 0)
    def _():
        pl.semaphore_signal(barrier, inc=1, device_id={"seq": me - 1}, device_id_type=MESH)

    @pl.when(me < count - 1)
    def _():
        pl.semaphore_signal(barrier, inc=1, device_id={"seq": me + 1}, device_id_type=MESH)

    for hop in range(1, parts):
        pl.semaphore_signal(
            barrier, inc=1, device_id={"groups": lax.rem(group + hop, parts)}, device_id_type=MESH
        )
    neighbours = jnp.where(me > 0, 1, 0) + jnp.where(me < count - 1, 1, 0) + (parts - 1)
    pl.semaphore_wait(barrier, neighbours)

    line = ShardLine(w_own, slots, q_sems, q_chunks, count, parts)
    outs = ShardLine(o_own, o_all, o_sems, o_chunks, count, parts)
    line.open_line()
    keep = pltpu.make_async_copy(o_own, o_all.at[me], own_sem)
    keep.start()
    tile = 256

    def add(shard, block, first):
        def column(j, carry):
            at = pl.ds(pl.multiple_of(j * tile, tile), tile)
            product = jnp.dot(hidden[shard], block[:, at], preferred_element_type=jnp.float32)
            total[:, at] = product if first else total[:, at] + product
            return carry

        lax.fori_loop(0, total.shape[1] // tile, column, 0)

    def finish(step):
        for way in (0, 1):
            shard = line.shard_of(step, way)

            @pl.when(line.present(step, way))
            def _():
                line.complete(shard)
                add(shard, slots.at[shard], False)

    add(me, w_own, True)

    def q_step(step, carry):
        line.relay(step)

        @pl.when(step > 1)
        def _():
            finish(step - 1)

        return carry

    lax.fori_loop(1, count, q_step, 0)
    outs.open_line()
    finish(count - 1)
    qkv[...] = total[...].astype(qkv.dtype)

    def o_step(step, carry):
        outs.relay(step)
        return carry

    lax.fori_loop(1, count, o_step, 0)

    def last(step, carry):
        line.close_sends(step)
        outs.close_sends(step)
        for way in (0, 1):
            shard = outs.shard_of(step, way)

            @pl.when(outs.present(step, way))
            def _():
                outs.complete(shard)

        return carry

    lax.fori_loop(1, count, last, 0)
    line.close_own()
    outs.close_own()
    keep.wait()


def project(hidden, w_own, o_own):
    count, parts = lax.axis_size("seq"), lax.axis_size("groups")
    rows, depth = hidden.shape
    hidden = hidden.reshape(rows, count, depth // count).transpose(1, 0, 2)
    width = w_own.shape[1]
    most = 4 if count <= 8 else 1
    q_chunks = pieces_of(w_own.shape[0] // parts, most)
    o_chunks = pieces_of(o_own.shape[0] // parts, most)
    vmem = pl.BlockSpec(memory_space=pltpu.VMEM)
    return pl.pallas_call(
        functools.partial(project_kernel, count, parts, q_chunks, o_chunks),
        out_shape=[
            jax.ShapeDtypeStruct((rows, width), jnp.bfloat16),
            jax.ShapeDtypeStruct((count,) + o_own.shape, jnp.bfloat16),
        ],
        in_specs=[vmem] * 3,
        out_specs=[vmem, pl.BlockSpec(memory_space=pl.ANY)],
        scratch_shapes=[
            pltpu.VMEM((count,) + w_own.shape, jnp.bfloat16),
            pltpu.VMEM((rows, width), jnp.float32),
            pltpu.SemaphoreType.DMA((1 + parts, 2, count, q_chunks)),
            pltpu.SemaphoreType.DMA((1 + parts, 2, count, o_chunks)),
            pltpu.SemaphoreType.DMA,
        ],
        compiler_params=pltpu.CompilerParams(
            collective_id=0, has_side_effects=True, vmem_limit_bytes=48 * 1024 * 1024
        ),
        name="project",
    )(hidden, w_own, o_own)


def mix_kernel(heads, subs, chunks, attn, w_all, gate, update, slots, total, x_sems, c_sems):
    head, sub = lax.axis_index("head"), lax.axis_index("sub")
    barrier = pltpu.get_barrier_semaphore()
    for hop in range(1, heads):
        pl.semaphore_signal(
            barrier, inc=1, device_id={"head": lax.rem(head + hop, heads)}, device_id_type=MESH
        )
    for hop in range(1, subs):
        pl.semaphore_signal(
            barrier, inc=1, device_id={"sub": lax.rem(sub + hop, subs)}, device_id_type=MESH
        )
    pl.semaphore_wait(barrier, heads + subs - 2)
    size = attn.shape[0] // chunks

    def to_head(hop, chunk):
        rows = pl.ds(chunk * size, size)
        return pltpu.make_async_remote_copy(
            src_ref=attn.at[rows],
            dst_ref=slots.at[hop, 0, rows],
            send_sem=x_sems.at[hop, 0, chunk],
            recv_sem=x_sems.at[hop, 1, chunk],
            device_id={"head": lax.rem(head + hop, heads)},
            device_id_type=MESH,
        )

    def to_sub(hop, turn, chunk):
        rows = pl.ds(chunk * size, size)
        return pltpu.make_async_remote_copy(
            src_ref=attn.at[rows] if hop == 0 else slots.at[hop, 0, rows],
            dst_ref=slots.at[hop, turn, rows],
            send_sem=c_sems.at[hop, turn, 0, chunk],
            recv_sem=c_sems.at[hop, turn, 1, chunk],
            device_id={"sub": lax.rem(sub + turn, subs)},
            device_id_type=MESH,
        )

    for chunk in range(chunks):
        for hop in range(1, heads):
            to_head(hop, chunk).start()
        for turn in range(1, subs):
            to_sub(0, turn, chunk).start()

    def add(chunk, hop, turn, first):
        rows = slice(chunk * size, (chunk + 1) * size)
        owner = lax.rem(head + heads - hop, heads) * subs + lax.rem(sub + subs - turn, subs)
        block = attn[rows, :] if hop == 0 and turn == 0 else slots[hop, turn, rows, :]
        product = jnp.dot(block, w_all[owner], preferred_element_type=jnp.float32)
        total[rows, :] = product if first else total[rows, :] + product

    for chunk in range(chunks):
        add(chunk, 0, 0, True)
    for chunk in range(chunks):
        for turn in range(1, subs):
            to_sub(0, turn, chunk).wait_recv()
            add(chunk, 0, turn, False)
    for chunk in range(chunks):
        for hop in range(1, heads):
            to_head(hop, chunk).wait_recv()
            for turn in range(1, subs):
                to_sub(hop, turn, chunk).start()
            add(chunk, hop, 0, False)
    for chunk in range(chunks):
        for hop in range(1, heads):
            for turn in range(1, subs):
                to_sub(hop, turn, chunk).wait_recv()
                add(chunk, hop, turn, False)
        rows = slice(chunk * size, (chunk + 1) * size)
        update[rows, :] = (gate[...] * total[rows, :]).astype(update.dtype)
    for chunk in range(chunks):
        for hop in range(1, heads):
            to_head(hop, chunk).wait_send()
        for hop in range(heads):
            for turn in range(1, subs):
                to_sub(hop, turn, chunk).wait_send()


def mix(attention, w_all, gate):
    heads, subs = lax.axis_size("head"), lax.axis_size("sub")
    rows, width = attention.shape
    chunks = pieces_of(rows, 2)
    vmem = pl.BlockSpec(memory_space=pltpu.VMEM)
    return pl.pallas_call(
        functools.partial(mix_kernel, heads, subs, chunks),
        out_shape=jax.ShapeDtypeStruct((rows, w_all.shape[-1]), jnp.bfloat16),
        in_specs=[vmem] * 3,
        out_specs=vmem,
        scratch_shapes=[
            pltpu.VMEM((heads, subs, rows, width), jnp.bfloat16),
            pltpu.VMEM((rows, w_all.shape[-1]), jnp.float32),
            pltpu.SemaphoreType.DMA((heads, 2, chunks)),
            pltpu.SemaphoreType.DMA((heads, subs, 2, chunks)),
        ],
        compiler_params=pltpu.CompilerParams(
            collective_id=1, has_side_effects=True, vmem_limit_bytes=40 * 1024 * 1024
        ),
        name="mix",
    )(attention, w_all, gate)


def modulate(tokens, modulation):
    values = tokens.astype(jnp.float32)
    center = jnp.mean(values, axis=-1, keepdims=True)
    spread = jnp.mean(jnp.square(values - center), axis=-1, keepdims=True)
    normed = (values - center) * lax.rsqrt(spread + EPSILON)
    return (normed * (1.0 + modulation[1]) + modulation[0]).astype(jnp.bfloat16)


def shards(tokens, modulation, w_qkv, w_out, pattern, counts, spatial_mask):
    row_count, feature_width = tokens.shape
    pairs_local = w_qkv.shape[1]
    head_size = w_qkv.shape[2] // 6
    frames_local = spatial_mask.shape[0]
    positions = row_count // frames_local
    slot_total = pattern.shape[1]
    scale_factor = 1.0 / math.sqrt(head_size)
    hidden = modulate(tokens, modulation)
    projected, whole_out = project(hidden, w_qkv.reshape(w_qkv.shape[0], -1), w_out)
    packed = projected.reshape(
        frames_local, positions, pairs_local, 6 * head_size
    )
    temporal_in = packed[..., : 3 * head_size].transpose(1, 0, 2, 3)
    received = lax.all_to_all(temporal_in, "seq", split_axis=0, concat_axis=1, tiled=True)
    position_span, frame_total, items, _ = received.shape
    relaid = received.reshape(position_span * frame_total, items, 3 * head_size)
    extended = with_halo(relaid[:, :, head_size:], (("seq", 0),), WIN * BLOCK)
    block_count = position_span * frame_total // BLOCK
    key_table = extended.reshape(block_count + 2 * WIN, BLOCK, items, 2 * head_size)
    queries = relaid[:, :, :head_size].reshape(block_count, BLOCK, items, head_size)
    offsets = pattern - (lax.axis_index("seq") * block_count - WIN)

    def slot_step(slot_index, state_pair):
        numerator, denominator = state_pair
        chosen = lax.dynamic_index_in_dim(offsets, slot_index, 1, keepdims=False)
        picked = jnp.take(key_table, chosen, axis=0)
        scores = (
            jnp.einsum(
                "bqnc,bknc->bnqk",
                queries,
                picked[..., :head_size],
                preferred_element_type=jnp.float32,
            )
            * scale_factor
        )
        alive = (slot_index < counts).astype(jnp.float32)
        weights = jnp.exp(scores) * alive[:, None, None, None]
        numerator = numerator + jnp.einsum(
            "bnqk,bknc->bnqc",
            weights.astype(jnp.bfloat16),
            picked[..., head_size:],
            preferred_element_type=jnp.float32,
        )
        return (numerator, denominator + jnp.sum(weights, axis=-1))

    start_state = (
        jnp.zeros((block_count, items, BLOCK, head_size), jnp.float32),
        jnp.zeros((block_count, items, BLOCK), jnp.float32),
    )
    numerator, denominator = lax.fori_loop(0, slot_total, slot_step, start_state)
    outcome = (numerator / denominator[..., None]).astype(jnp.bfloat16)
    outcome = outcome.transpose(0, 2, 1, 3).reshape(position_span, frame_total, items, head_size)
    temporal_out = lax.all_to_all(outcome, "seq", split_axis=1, concat_axis=0, tiled=True)
    spatial = packed[..., 3 * head_size :]
    blocks_frame = positions // BLOCK
    scores = (
        jnp.einsum(
            "fpnc,fqnc->fnpq",
            spatial[..., :head_size],
            spatial[..., head_size : 2 * head_size],
            preferred_element_type=jnp.float32,
        )
        * scale_factor
    )
    keep = spatial_mask.astype(jnp.float32)[:, None, :, None, :, None]
    weights = (
        jnp.exp(scores).reshape(frames_local, pairs_local, blocks_frame, BLOCK, blocks_frame, BLOCK)
        * keep
    )
    weights = weights.reshape(frames_local, pairs_local, positions, positions)
    denominator = jnp.sum(weights, axis=-1)
    numerator = jnp.einsum(
        "fnpq,fqnc->fpnc",
        weights.astype(jnp.bfloat16),
        spatial[..., 2 * head_size :],
        preferred_element_type=jnp.float32,
    )
    spatial_out = (numerator / denominator.transpose(0, 2, 1)[..., None]).astype(jnp.bfloat16)
    attention = jnp.concatenate([temporal_out.transpose(1, 0, 2, 3), spatial_out], axis=-1)
    attention = attention.reshape(row_count, pairs_local * 2 * head_size)
    out_width = w_out.shape[1]
    blocks = lax.axis_size("head") * lax.axis_size("sub")
    gate_slice = lax.dynamic_slice_in_dim(
        modulation[2], lax.axis_index(("head", "sub")) * out_width, out_width, 0
    )
    return mix(attention, whole_out.reshape(blocks, -1, out_width), gate_slice[None, :])

def push(source, target, send_sem, recv_sem, axis, place):
    return pltpu.make_async_remote_copy(
        src_ref=source,
        dst_ref=target,
        send_sem=send_sem,
        recv_sem=recv_sem,
        device_id={axis: place},
        device_id_type=MESH,
    )


def seats(count):
    return (count // 2 - 1, count // 2)


def by_pair_kernel(
    sizes, chunks, pieces, o_chunks,
    tokens, modulation, w_own, o_own, pattern, counts, mask, update,
    held, raw, stage, passing, partial, hfull, wfull, tq, sq, o_all, lists, lists_all, table, own, slots,
    tok_sems, l_sems, w_sems, p_sems, z_sems, x_sems, c_sems, o_sems, keep_sems, sz_sems, sx_sems, sc_sems, own_sems,
):
    count, parts, heads, subs = sizes
    low, high = seats(count)
    me, group = lax.axis_index("seq"), lax.axis_index("groups")
    head, sub = lax.axis_index("head"), lax.axis_index("sub")
    other = low + high - me
    near = jnp.where(me == low, low - 1, high + 1)
    far = jnp.where(me == low, high + 1, low - 1)
    seated = jnp.logical_or(me == low, me == high)
    ended = jnp.logical_not(seated)
    outward = jnp.where(me == low, 1, 0)
    blocks = heads * subs
    quarter = held.shape[1]
    unit = quarter // chunks
    width = wfull.shape[2]
    half = w_own.shape[0] // parts
    piece = half // pieces
    block = unit * blocks

    barrier = pltpu.get_barrier_semaphore()
    others = 0
    for axis in ("seq", "groups", "head", "sub"):
        size = lax.axis_size(axis)
        for hop in range(1, size):
            partner = lax.rem(lax.axis_index(axis) + hop, size)
            pl.semaphore_signal(barrier, inc=1, device_id={axis: partner}, device_id_type=MESH)
            others += 1

    def rows_of(head_hop, sub_hop, chunk):
        owner = lax.rem(head + heads - head_hop, heads) * subs + lax.rem(sub + subs - sub_hop, subs)
        return pl.ds(pl.multiple_of((chunk * blocks + owner) * unit, unit), unit)

    def fetch(hop, chunk):
        return pltpu.make_async_copy(
            tokens.at[rows_of(hop, 0, chunk)], held.at[hop, pl.ds(chunk * unit, unit)],
            tok_sems.at[hop, chunk],
        )

    for chunk in range(chunks):
        fetch(0, chunk).start()
    raw_copy = pltpu.make_async_copy(w_own, raw, own_sems.at[0])
    raw_copy.start()
    o_copy = pltpu.make_async_copy(o_own, o_all.at[me], own_sems.at[1])
    o_copy.start()

    @pl.when(seated)
    def _():
        for hop in range(1, heads):
            for chunk in range(chunks):
                fetch(hop, chunk).start()

    lists[...] = jnp.zeros_like(lists)
    slots_of = pattern.shape[1]
    lists[0 : pattern.shape[0], 0:slots_of] = pattern[...]
    lists[8 : 8 + mask.shape[0], 0 : mask.shape[1]] = mask[...]
    lists[16:17, 0 : counts.shape[1]] = counts[...]
    gain = 1.0 + modulation[1:2, :]
    shift = modulation[0:1, :]

    def modulate_rows(hop, first, last):
        def some(i, carry):
            at = pl.ds(pl.multiple_of(i * 16, 16), 16)
            chunk = i // (unit // 16)
            owner = lax.rem(head + heads - hop, heads) * subs + sub
            start = (chunk * blocks + owner) * unit + lax.rem(i, unit // 16) * 16
            values = held[hop, at, :].astype(jnp.float32)
            centered = values - jnp.mean(values, axis=-1, keepdims=True)
            spread_of = jnp.mean(jnp.square(centered), axis=-1, keepdims=True)
            normed = centered * lax.rsqrt(spread_of + EPSILON)
            hfull[me, pl.ds(pl.multiple_of(start, 16), 16), :] = (normed * gain + shift).astype(hfull.dtype)
            return carry

        for chunk in range(first, last):
            fetch(hop, chunk).wait()
        lax.fori_loop(first * unit // 16, last * unit // 16, some, 0, unroll=2)

    modulate_rows(0, 0, 1)
    pl.semaphore_wait(barrier, others)

    def spot(frame, head_hop, sub_hop, chunk):
        return hfull.at[frame, rows_of(head_hop, sub_hop, chunk)]

    def z_push(frame, chunk, place):
        target = spot(frame, 0, 0, chunk)
        return push(target, target, z_sems.at[0, frame, chunk], z_sems.at[1, frame, chunk], "seq", place)

    def x_push(frame, chunk, hop):
        target = spot(frame, 0, 0, chunk)
        return push(
            target, target, x_sems.at[hop, 0, frame, chunk], x_sems.at[hop, 1, frame, chunk],
            "head", lax.rem(head + hop, heads),
        )

    def c_push(frame, chunk, hop, turn):
        target = spot(frame, hop, 0, chunk)
        return push(
            target, target, c_sems.at[hop, turn, 0, frame, chunk], c_sems.at[hop, turn, 1, frame, chunk],
            "sub", lax.rem(sub + turn, subs),
        )

    def l_push(seat):
        return push(lists, lists_all.at[me], l_sems.at[0, seat - low], l_sems.at[1, me], "seq", seat)

    def w_rows(part, step):
        return pl.ds(pl.multiple_of(part * half + step * piece, piece), piece)

    def w_along(seat, source, step):
        return push(
            stage.at[seat - low, pl.ds(step * piece, piece)], wfull.at[source, w_rows(group, step)],
            w_sems.at[0, 0, seat - low, step], w_sems.at[0, 1, source, step], "seq", seat,
        )

    def w_hand(step, place):
        return push(
            stage.at[jnp.where(me < low, high, low) - low, pl.ds(step * piece, piece)],
            passing.at[pl.ds(step * piece, piece)],
            p_sems.at[0, step], p_sems.at[1, step], "seq", place,
        )

    def w_pass(source, step):
        return push(
            passing.at[pl.ds(step * piece, piece)], wfull.at[source, w_rows(group, step)],
            w_sems.at[0, 0, me - low, step], w_sems.at[0, 1, source, step], "seq", other,
        )

    def w_across(source, step, turn):
        target = wfull.at[source, w_rows(group, step)]
        return push(
            target, target, w_sems.at[turn, 0, source, step], w_sems.at[turn, 1, source, step],
            "groups", lax.rem(group + turn, parts),
        )

    outs = LineGather(o_all, o_sems, o_chunks, count, parts)

    for seat in (low, high):
        @pl.when(me != seat)
        def _():
            l_push(seat).start()

    columns_of = own.shape[2]

    def item(hop, turn, seat, chunk):
        return out_spot(slots, hop, turn, seat, chunk, block, low, columns_of)

    def to_head(hop, seat, chunk, source=None):
        return push(
            item(0, 0, seat, chunk) if source is None else source, item(hop, 0, seat, chunk),
            sx_sems.at[hop, 0, seat - low, chunk], sx_sems.at[hop, 1, seat - low, chunk],
            "head", lax.rem(head + hop, heads),
        )

    def to_sub(hop, turn, seat, chunk, source=None):
        return push(
            item(hop, 0, seat, chunk) if source is None else source, item(hop, turn, seat, chunk),
            sc_sems.at[hop, turn, 0, seat - low, chunk], sc_sems.at[hop, turn, 1, seat - low, chunk],
            "sub", lax.rem(sub + turn, subs),
        )

    toward = jnp.where(me < low, low, high)

    def relay_out(step, pieces_of_it, outgoing):
        for way in (0, 1):
            @pl.when((outward == way) == outgoing)
            def _():
                outs.relay(step, way, pieces_of_it)

    o_first, o_last = tuple(range(o_chunks // 2)), tuple(range(o_chunks // 2, o_chunks))

    def z_out(first, last):
        @pl.when(seated)
        def _():
            for chunk in range(first, last):
                z_push(me, chunk, other).start()

        @pl.when(ended)
        def _():
            for chunk in range(first, last):
                z_push(me, chunk, toward).start()

    z_out(0, 1)
    raw_copy.wait()

    def unpack(i, carry):
        start = pl.multiple_of(i * 64, 64)
        both = raw[pl.ds(pl.multiple_of(group * half + start, 64), 64)]
        first, second = both[:, 0, :], both[:, 1, :]
        stage[0, pl.ds(start, 64), :] = first
        stage[1, pl.ds(start, 64), :] = second
        return carry

    lax.fori_loop(0, half // 64, unpack, 0)

    @pl.when(ended)
    def _():
        for step in range(pieces):
            w_hand(step, toward).start()

    @pl.when(seated)
    def _():
        for step in range(pieces):
            w_along(other, me, step).start()

    modulate_rows(0, 1, chunks)
    o_copy.wait()

    @pl.when(ended)
    def _():
        z_out(1, chunks)
        for step in range(pieces):
            w_along(toward, me, step).start()
        for way in (0, 1):
            outs.open_way(way)
        for way in (0, 1):
            outs.relay(1, way)

    @pl.when(seated)
    def _():
        for way in (0, 1):
            @pl.when(outward == way)
            def _():
                outs.open_way(way)

        keep = pltpu.make_async_copy(lists, lists_all.at[me], own_sems.at[2])
        keep.start()
        for chunk in range(chunks):
            for turn in range(1, subs):
                c_push(me, chunk, 0, turn).start()
        for hop in range(1, heads):
            modulate_rows(hop, 0, chunks)
            for chunk in range(chunks):
                for turn in range(1, subs):
                    c_push(me, chunk, hop, turn).start()

        def land(frame, chunk):
            z_push(frame, chunk, other).wait_recv()
            for hop in range(1, heads):
                x_push(frame, chunk, hop).start()
            for turn in range(1, subs):
                c_push(frame, chunk, 0, turn).start()

        def crossed(frame, chunk):
            for hop in range(1, heads):
                x_push(frame, chunk, hop).wait_recv()
                for turn in range(1, subs):
                    c_push(frame, chunk, hop, turn).start()

        def gathered(frame, chunk):
            for hop in range(heads):
                for turn in range(1, subs):
                    c_push(frame, chunk, hop, turn).wait_recv()

        def keep_pair(i, carry):
            at = pl.ds(pl.multiple_of(i * 64, 64), 64)
            both = raw[at]
            wfull[me, at, :] = jnp.where(me == low, both[:, 0, :], both[:, 1, :])
            return carry

        def w_land(source, step):
            w_along(me, source, step).wait_recv()
            for turn in range(1, parts):
                w_across(source, step, turn).start()

        span = unit
        scale = math.log2(math.e) / math.sqrt(own.shape[2] // 2)
        size = own.shape[2] // 2
        total_blocks = tq.shape[0]
        each = total_blocks // count
        window = 2 * WIN + 1

        depth = wfull.shape[1]

        def first_part(frame, slot):
            def some_rows(chunk, carry):
                rows = pl.ds(pl.multiple_of(chunk * block, block), block)
                partial[slot, rows, :] = jnp.dot(
                    hfull[frame, rows, low * depth : (high + 1) * depth],
                    wfull[low : high + 1].reshape(-1, width), preferred_element_type=jnp.float32,
                )
                return carry

            lax.fori_loop(0, chunks, some_rows, 0)

        def keep_qkv(frame, chunk, total):
            at = pl.ds(pl.multiple_of(frame * span, span), span)
            for i in range(blocks):
                tq[chunk * blocks + i, at, :] = total[i * span : (i + 1) * span, : 3 * size]
            sq[frame, pl.ds(pl.multiple_of(chunk * block, block), block), :] = total[:, 3 * size :]

        land(near, 0)
        land(other, 0)
        for step in range(pieces):
            w_hand(step, other).wait_recv()
            w_pass(near, step).start()
            w_land(other, step)
        for chunk in range(1, chunks):
            z_push(me, chunk, other).start()
        z_push(near, 0, other).start()
        crossed(near, 0)
        crossed(other, 0)
        lax.fori_loop(0, w_own.shape[0] // 64, keep_pair, 0)
        rest = max(pieces, chunks - 1)
        for i in range(rest):
            if i + 1 < chunks:
                land(near, i + 1)
                z_push(near, i + 1, other).start()
            if i < pieces:
                w_land(far, i)
        for way in (0, 1):
            @pl.when(outward != way)
            def _():
                outs.open_way(way)
        def crossed_w(source):
            for step in range(pieces):
                for turn in range(1, parts):
                    w_across(source, step, turn).wait_recv()

        def all_in(frame):
            for chunk in range(chunks):
                gathered(frame, chunk)

        crossed_w(other)
        all_in(me)
        first_part(me, 0)
        for i in range(rest):
            if i + 1 < chunks:
                land(other, i + 1)
            if i < pieces:
                w_land(near, i)
            if i + 1 < chunks:
                crossed(near, i + 1)
            if i == rest - 1:
                all_in(near)
                first_part(near, 1)
        for i in range(1, chunks):
            crossed(other, i)
        land(far, 0)
        all_in(other)
        first_part(other, 2)

        for source in (near, other, far):
            l_push_from(lists_all, lists, l_sems, source, low, me).wait_recv()
        keep.wait()
        to_table = pltpu.make_async_copy(lists_all, table, own_sems.at[3])
        to_table.start()

        def project(frame, chunk):
            rows = pl.ds(pl.multiple_of(chunk * block, block), block)
            total = jnp.dot(
                hfull[frame, rows, :], wfull[...].reshape(-1, width), preferred_element_type=jnp.float32
            ).astype(tq.dtype)
            keep_qkv(frame, chunk, total)

        def project_frame(frame, slot):
            def last_part(chunk, carry):
                rows = pl.ds(pl.multiple_of(chunk * block, block), block)
                total = partial[slot, rows, :]
                for source in (0, count - 1):
                    at = slice(source * depth, (source + 1) * depth)
                    total = total + jnp.dot(
                        hfull[frame, rows, at], wfull[source], preferred_element_type=jnp.float32
                    )
                keep_qkv(frame, chunk, total.astype(tq.dtype))
                return carry

            lax.fori_loop(0, chunks, last_part, 0)

        def soft(q, keys, values, biases):
            scores = lax.dot_general(
                q, keys, (((1,), (1,)), ((), ())), preferred_element_type=jnp.float32
            )
            parts_of = []
            sums = None
            for i, bias in enumerate(biases):
                weight = jnp.exp2(scores[:, i * BLOCK : (i + 1) * BLOCK] * scale + bias)
                sums = weight if sums is None else sums + weight
                parts_of.append(weight.astype(jnp.bfloat16))
            numerator = jnp.dot(
                jnp.concatenate(parts_of, axis=1), values, preferred_element_type=jnp.float32
            )
            return (numerator / jnp.sum(sums, axis=-1, keepdims=True)).astype(own.dtype)

        def temporal(chunk):
            def query(i, carry):
                b = chunk * blocks + i
                device, row = b // each, lax.rem(b, each)
                start = jnp.clip(b - WIN, 0, total_blocks - window)
                used = table[device, 16, row]
                biases = []
                for w in range(window):
                    times = 0
                    for j in range(slots_of):
                        hit = jnp.logical_and(j < used, table[device, row, j] == start + w)
                        times = times + jnp.where(hit, 1, 0)
                    bias = jnp.float32(-jnp.inf)
                    for m in range(1, slots_of + 1):
                        bias = jnp.where(times == m, jnp.float32(math.log2(m)), bias)
                    biases.append(bias)
                near_by = pl.ds(start, window)
                result = soft(
                    tq[b, :, :size],
                    tq[near_by, :, size : 2 * size].reshape(-1, size),
                    tq[near_by, :, 2 * size :].reshape(-1, size),
                    biases,
                )
                at = pl.ds(pl.multiple_of(b * span, span), span)
                for f in range(count):
                    own[f, at, :size] = result[f * span : (f + 1) * span]
                return carry

            lax.fori_loop(0, blocks, query, 0)

        def spatial(frame):
            per = sq.shape[1] // BLOCK

            def query(i, carry):
                at = pl.ds(pl.multiple_of(i * BLOCK, BLOCK), BLOCK)
                biases = [
                    jnp.where(table[frame, 8 + i, j] > 0, jnp.float32(0), jnp.float32(-jnp.inf))
                    for j in range(per)
                ]
                own[frame, at, size:] = soft(
                    sq[frame, at, :size], sq[frame, :, size : 2 * size], sq[frame, :, 2 * size :], biases
                )
                return carry

            lax.fori_loop(0, per, query, 0)

        def send(frame, chunk):
            out_push(own, slots, sz_sems, me, frame, chunk, block, low).start()

        def settle(chunk):
            send(near, chunk)
            send(other, chunk)
            keep_out(own, slots, keep_sems, me, chunk, block, low).start()
            mine = own.at[me, pl.ds(chunk * block, block)]
            for hop in range(1, heads):
                to_head(hop, me, chunk, mine).start()
            for turn in range(1, subs):
                to_sub(0, turn, me, chunk, mine).start()

        early = (me, near, other)
        for chunk in range(chunks + 1):
            if 0 < chunk < chunks:
                land(far, chunk)
            if chunk and chunk < chunks:
                crossed(far, chunk - 1)
            if chunk == 0:
                crossed_w(far)
                crossed_w(near)
                to_table.wait()
            if chunk < len(early):
                project_frame(early[chunk], chunk)
            if chunk and chunk <= len(early):
                spatial(early[chunk - 1])
            if chunk:
                gathered(far, chunk - 1)
                project(far, chunk - 1)
            if chunk == 1:
                relay_out(1, None, False)
            if chunk == chunks - 1:
                relay_out(1, o_first, True)
                crossed(far, chunks - 1)
                for ready in range(chunks - 2):
                    temporal(ready)
                    settle(ready)
                relay_out(1, o_last, True)
        for ready in (chunks - 2, chunks - 1):
            temporal(ready)
            settle(ready)
        relay_out(2, o_first, True)
        spatial(far)
        for chunk in range(chunks):
            send(far, chunk)
        relay_out(2, o_last, True)

    def arrive(chunk, seat):
        out_push(own, slots, sz_sems, seat, me, chunk, block, low).wait_recv()
        for hop in range(1, heads):
            to_head(hop, seat, chunk).start()
        for turn in range(1, subs):
            to_sub(0, turn, seat, chunk).start()

    def pass_on(chunk, seat):
        for hop in range(1, heads):
            to_head(hop, seat, chunk).wait_recv()
            for turn in range(1, subs):
                to_sub(hop, turn, seat, chunk).start()

    columns = pl.ds(pl.multiple_of((head * subs + sub) * update.shape[1], 128), update.shape[1])
    gate = modulation[2:3, columns]

    def finish(chunk):
        for seat in (low, high):
            for hop in range(heads):
                for turn in range(1, subs):
                    to_sub(hop, turn, seat, chunk).wait_recv()
        rows = slice(chunk * block, (chunk + 1) * block)
        total = None
        for hop in range(heads):
            for turn in range(subs):
                owner = lax.rem(head + heads - hop, heads) * subs + lax.rem(sub + subs - turn, subs)
                product = jnp.dot(slots[hop, turn, rows, :], o_all[owner], preferred_element_type=jnp.float32)
                total = product if total is None else total + product
        update[rows, :] = (gate * total).astype(update.dtype)

    nearer = jnp.where(seated, me, toward)
    farther = low + high - nearer
    def relay_end(step, pieces_of_it):
        for way in (0, 1):
            outs.relay(step, way, pieces_of_it)

    @pl.when(ended)
    def _():
        relay_end(2, None)
        for chunk in range(chunks):
            arrive(chunk, nearer)
            if chunk:
                pass_on(chunk - 1, nearer)
            if chunk == chunks // 2 - 1:
                relay_end(3, o_first)
        pass_on(chunks - 1, nearer)

    @pl.when(seated)
    def _():
        for chunk in range(chunks):
            pass_on(chunk, nearer)

    for chunk in range(chunks):
        arrive(chunk, farther)
        if chunk:
            pass_on(chunk - 1, farther)
        if chunk < len(o_last):
            @pl.when(ended)
            def _():
                relay_end(3, o_last[chunk : chunk + 1])

    pass_on(chunks - 1, farther)

    @pl.when(seated)
    def _():
        for chunk in range(chunks):
            keep_out(own, slots, keep_sems, me, chunk, block, low).wait()

    for step in range(1, count):
        for way in (0, 1):
            @pl.when(outs.present(step, way))
            def _():
                outs.complete(outs.shard_of(step, way))
    for chunk in range(chunks):
        finish(chunk)

    for seat in (low, high):
        @pl.when(me != seat)
        def _():
            l_push(seat).wait_send()

    @pl.when(ended)
    def _():
        for step in range(pieces):
            w_hand(step, toward).wait_send()
            w_along(toward, me, step).wait_send()
        for chunk in range(chunks):
            z_push(me, chunk, jnp.where(me < low, low, high)).wait_send()

    @pl.when(seated)
    def _():
        for step in range(pieces):
            w_along(other, me, step).wait_send()
            w_pass(near, step).wait_send()
        for chunk in range(chunks):
            z_push(me, chunk, other).wait_send()
            z_push(near, chunk, other).wait_send()
            for frame in (me, near, other, far):
                for hop in range(heads):
                    for turn in range(1, subs):
                        c_push(frame, chunk, hop, turn).wait_send()
            for frame in (near, other, far):
                for hop in range(1, heads):
                    x_push(frame, chunk, hop).wait_send()
                out_push(own, slots, sz_sems, me, frame, chunk, block, low).wait_send()
        for source in (near, other, far):
            for step in range(pieces):
                for turn in range(1, parts):
                    w_across(source, step, turn).wait_send()

    for way in (0, 1):
        outs.close_way(way)
    for step in range(1, count):
        for way in (0, 1):
            outs.close_sends(step, way)
    for chunk in range(chunks):
        for seat in (low, high):
            for hop in range(1, heads):
                to_head(hop, seat, chunk).wait_send()
            for hop in range(heads):
                for turn in range(1, subs):
                    to_sub(hop, turn, seat, chunk).wait_send()


def l_push_from(lists_all, lists, l_sems, source, low, me):
    return push(lists, lists_all.at[source], l_sems.at[0, me - low], l_sems.at[1, source], "seq", me)


def out_spot(slots, hop, turn, seat, chunk, block, low, columns):
    at = (seat - low) * columns
    at = pl.ds(pl.multiple_of(at, columns), columns)
    return slots.at[hop, turn, pl.ds(chunk * block, block), at]


def out_push(own, slots, sems, seat, frame, chunk, block, low):
    return push(
        own.at[frame, pl.ds(chunk * block, block)],
        out_spot(slots, 0, 0, seat, chunk, block, low, own.shape[2]),
        sems.at[0, frame, chunk], sems.at[1, seat, chunk], "seq", frame,
    )


def keep_out(own, slots, sems, seat, chunk, block, low):
    return pltpu.make_async_copy(
        own.at[seat, pl.ds(chunk * block, block)],
        out_spot(slots, 0, 0, seat, chunk, block, low, own.shape[2]),
        sems.at[chunk],
    )


class LineGather:
    def __init__(self, slots, sems, chunks, count, parts):
        self.slots, self.chunks = slots, chunks
        self.sems, self.count, self.parts = sems, count, parts
        self.me = lax.axis_index("seq")
        self.group = lax.axis_index("groups")
        self.size = slots.shape[1] // (parts * chunks)

    def rows(self, group, chunk):
        start = (group * self.chunks + chunk) * self.size
        return pl.ds(pl.multiple_of(start, self.size), self.size)

    def along(self, shard, chunk, way):
        rows = self.rows(self.group, chunk)
        return push(
            self.slots.at[shard, rows], self.slots.at[shard, rows],
            self.sems.at[way, 0, shard, chunk], self.sems.at[way, 1, shard, chunk],
            "seq", self.me + (1 if way == 0 else -1),
        )

    def across(self, shard, chunk, hop):
        rows = self.rows(self.group, chunk)
        return push(
            self.slots.at[shard, rows], self.slots.at[shard, rows],
            self.sems.at[1 + hop, 0, shard, chunk], self.sems.at[1 + hop, 1, shard, chunk],
            "groups", lax.rem(self.group + hop, self.parts),
        )

    def onward(self, way):
        return self.me < self.count - 1 if way == 0 else self.me > 0

    def shard_of(self, step, way):
        return self.me - step if way == 0 else self.me + step

    def present(self, step, way):
        return self.me >= step if way == 0 else self.me + step < self.count

    def open_way(self, way):
        @pl.when(self.onward(way))
        def _():
            for chunk in range(self.chunks):
                self.along(self.me, chunk, way).start()

    def relay(self, step, way, chunks=None):
        shard = self.shard_of(step, way)

        @pl.when(self.present(step, way))
        def _():
            for chunk in range(self.chunks) if chunks is None else chunks:
                self.along(shard, chunk, way).wait_recv()

                @pl.when(self.onward(way))
                def _():
                    self.along(shard, chunk, way).start()

                for hop in range(1, self.parts):
                    self.across(shard, chunk, hop).start()

    def complete(self, shard):
        for chunk in range(self.chunks):
            for hop in range(1, self.parts):
                self.across(shard, chunk, hop).wait_recv()

    def close_sends(self, step, way):
        shard = self.shard_of(step, way)

        @pl.when(self.present(step, way))
        def _():
            for chunk in range(self.chunks):
                @pl.when(self.onward(way))
                def _():
                    self.along(shard, chunk, way).wait_send()

                for hop in range(1, self.parts):
                    self.across(shard, chunk, hop).wait_send()

    def close_way(self, way):
        @pl.when(self.onward(way))
        def _():
            for chunk in range(self.chunks):
                self.along(self.me, chunk, way).wait_send()


def by_pair(tokens, modulation, w_own, o_own, pattern, counts, mask):
    sizes = tuple(lax.axis_size(axis) for axis in ("seq", "groups", "head", "sub"))
    count, parts, heads, subs = sizes
    rows, depth = tokens.shape
    width = w_own.shape[2]
    blocks = heads * subs
    quarter = rows // blocks
    chunks = rows // BLOCK
    pieces = 3
    o_chunks = 4
    columns = width // 3
    seated = len(seats(count))
    vmem = pl.BlockSpec(memory_space=pltpu.VMEM)
    whole = pl.BlockSpec(memory_space=pl.ANY)
    dma = pltpu.SemaphoreType.DMA
    kept = jnp.bfloat16
    return pl.pallas_call(
        functools.partial(by_pair_kernel, sizes, chunks, pieces, o_chunks),
        out_shape=jax.ShapeDtypeStruct((rows, o_own.shape[1]), kept),
        in_specs=[whole, vmem, whole, whole, vmem, vmem, vmem],
        out_specs=vmem,
        scratch_shapes=[
            pltpu.VMEM((heads, quarter, depth), kept),
            pltpu.VMEM(w_own.shape, kept),
            pltpu.VMEM((seated, w_own.shape[0] // parts, width), kept),
            pltpu.VMEM((w_own.shape[0] // parts, width), kept),
            pltpu.VMEM((count - 1, rows, width), jnp.float32),
            pltpu.VMEM((count, rows, depth), kept),
            pltpu.VMEM((count, w_own.shape[0], width), kept),
            pltpu.VMEM((count * rows // BLOCK, BLOCK, width // 2), kept),
            pltpu.VMEM((count, rows, width // 2), kept),
            pltpu.VMEM((count,) + o_own.shape, kept),
            pltpu.VMEM((24, 128), jnp.int32),
            pltpu.VMEM((count, 24, 128), jnp.int32),
            pltpu.SMEM((count, 24, 128), jnp.int32),
            pltpu.VMEM((count, rows, columns), kept),
            pltpu.VMEM((heads, subs, rows, seated * columns), kept),
            dma((heads, chunks)),
            dma((2, count)),
            dma((parts, 2, count, pieces)),
            dma((2, pieces)),
            dma((2, count, chunks)),
            dma((heads, 2, count, chunks)),
            dma((heads, subs, 2, count, chunks)),
            dma((1 + parts, 2, count, o_chunks)),
            dma((chunks,)),
            dma((2, count, chunks)),
            dma((heads, 2, seated, chunks)),
            dma((heads, subs, 2, seated, chunks)),
            dma((4,)),
        ],
        compiler_params=pltpu.CompilerParams(
            collective_id=2, has_side_effects=True, vmem_limit_bytes=60 * 1024 * 1024
        ),
        name="by_pair",
    )(tokens, modulation, w_own, o_own, pattern, counts, mask)


def shards_by_pair(tokens, modulation, w_qkv, w_out, pattern, counts, spatial_mask):
    return by_pair(tokens, modulation, w_qkv, w_out, pattern, counts[None, :], spatial_mask[0])


def one_pair_each(count, blocks, parts, tokens, w_qkv, w_out, pattern, spatial_mask):
    rows, frames = tokens.shape[0], spatial_mask.shape[0]
    return (
        count == blocks == 4
        and w_qkv.shape[1] == len(seats(count))
        and frames == 1
        and rows == BLOCK * pattern.shape[0] == BLOCK * spatial_mask.shape[1]
        and pattern.shape[0] < 8
        and BLOCK % (16 * count) == 0
        and w_qkv.shape[0] % (192 * parts) == 0
        and w_out.shape[0] % (64 * parts) == 0
    )


def shards_any(*args):
    tokens, _, w_qkv, w_out, pattern, _, spatial_mask = args
    blocks = lax.axis_size("head") * lax.axis_size("sub")
    sizes = lax.axis_size("seq"), blocks, lax.axis_size("groups")
    if one_pair_each(*sizes, tokens, w_qkv, w_out, pattern, spatial_mask):
        return shards_by_pair(*args)
    return shards(*args)


def solution(mesh):
    return jax.shard_map(
        shards_any,
        mesh=mesh,
        in_specs=(
            P(("groups", "seq"), None),
            P(),
            P("seq", ("head", "sub"), None),
            P("seq", ("head", "sub")),
            P(("groups", "seq"), None),
            P(("groups", "seq")),
            P(("groups", "seq"), None, None),
        ),
        out_specs=P(("groups", "seq"), ("head", "sub")),
        check_vma=False,
    )
```

```python
import functools
import math

import jax
import jax.numpy as jnp
from jax import lax
from jax.experimental import pallas as pl
from jax.experimental.pallas import tpu as pltpu
from jax.sharding import PartitionSpec as P

BLOCK = 128
WIN = 2


EPSILON = 1e-06


def with_halo(cells, sides, width):
    for axis, dim in sides:
        count = lax.axis_size(axis)
        ends = count - 1
        head = lax.slice_in_dim(cells, 0, width, axis=dim)
        tail = lax.slice_in_dim(cells, cells.shape[dim] - width, cells.shape[dim], axis=dim)
        cells = jnp.concatenate(
            [
                lax.ppermute(tail, axis, [(i, (i + 1) % count) for i in range(ends)]),
                cells,
                lax.ppermute(head, axis, [((i + 1) % count, i) for i in range(ends)]),
            ],
            axis=dim,
        )
    return cells


MESH = pl.DeviceIdType.MESH


def pieces_of(rows, most=4):
    for count in range(most, 0, -1):
        if rows % (16 * count) == 0:
            return count
    return 1


class ShardLine:
    def __init__(self, own, slots, sems, chunks, count, parts):
        self.own, self.slots, self.chunks = own, slots, chunks
        self.sems, self.count, self.parts = sems, count, parts
        self.me = lax.axis_index("seq")
        self.group = lax.axis_index("groups")
        self.size = own.shape[0] // (parts * chunks)

    def rows(self, group, chunk):
        start = (group * self.chunks + chunk) * self.size
        return pl.ds(pl.multiple_of(start, self.size), self.size)

    def along(self, shard, chunk, way, own):
        rows = self.rows(self.group, chunk)
        source = self.own.at[rows] if own else self.slots.at[shard, rows]
        return pltpu.make_async_remote_copy(
            src_ref=source,
            dst_ref=self.slots.at[shard, rows],
            send_sem=self.sems.at[way, 0, shard, chunk],
            recv_sem=self.sems.at[way, 1, shard, chunk],
            device_id={"seq": self.me + (1 if way == 0 else -1)},
            device_id_type=MESH,
        )

    def across(self, shard, chunk, hop):
        rows = self.rows(self.group, chunk)
        return pltpu.make_async_remote_copy(
            src_ref=self.slots.at[shard, rows],
            dst_ref=self.slots.at[shard, rows],
            send_sem=self.sems.at[1 + hop, 0, shard, chunk],
            recv_sem=self.sems.at[1 + hop, 1, shard, chunk],
            device_id={"groups": lax.rem(self.group + hop, self.parts)},
            device_id_type=MESH,
        )

    def open_line(self):
        for chunk in range(self.chunks):
            for way in (0, 1):
                @pl.when(self.onward(way))
                def _():
                    self.along(self.me, chunk, way, True).start()

    def onward(self, way):
        return self.me < self.count - 1 if way == 0 else self.me > 0

    def shard_of(self, step, way):
        return self.me - step if way == 0 else self.me + step

    def present(self, step, way):
        return self.me >= step if way == 0 else self.me + step < self.count

    def relay(self, step):
        for chunk in range(self.chunks):
            for way in (0, 1):
                shard = self.shard_of(step, way)

                @pl.when(self.present(step, way))
                def _():
                    self.along(shard, chunk, way, False).wait_recv()

                    @pl.when(self.onward(way))
                    def _():
                        self.along(shard, chunk, way, False).start()

                    for hop in range(1, self.parts):
                        self.across(shard, chunk, hop).start()

    def complete(self, shard):
        for chunk in range(self.chunks):
            for hop in range(1, self.parts):
                self.across(shard, chunk, hop).wait_recv()

    def close_sends(self, step):
        for chunk in range(self.chunks):
            for way in (0, 1):
                shard = self.shard_of(step, way)

                @pl.when(self.present(step, way))
                def _():
                    @pl.when(self.onward(way))
                    def _():
                        self.along(shard, chunk, way, False).wait_send()

                    for hop in range(1, self.parts):
                        self.across(shard, chunk, hop).wait_send()

    def close_own(self):
        for chunk in range(self.chunks):
            for way in (0, 1):
                @pl.when(self.onward(way))
                def _():
                    self.along(self.me, chunk, way, True).wait_send()


def project_kernel(count, parts, q_chunks, o_chunks, hidden, w_own, o_own, qkv, o_all, slots, total, q_sems, o_sems, own_sem):
    me = lax.axis_index("seq")
    group = lax.axis_index("groups")
    barrier = pltpu.get_barrier_semaphore()

    @pl.when(me > 0)
    def _():
        pl.semaphore_signal(barrier, inc=1, device_id={"seq": me - 1}, device_id_type=MESH)

    @pl.when(me < count - 1)
    def _():
        pl.semaphore_signal(barrier, inc=1, device_id={"seq": me + 1}, device_id_type=MESH)

    for hop in range(1, parts):
        pl.semaphore_signal(
            barrier, inc=1, device_id={"groups": lax.rem(group + hop, parts)}, device_id_type=MESH
        )
    neighbours = jnp.where(me > 0, 1, 0) + jnp.where(me < count - 1, 1, 0) + (parts - 1)
    pl.semaphore_wait(barrier, neighbours)

    line = ShardLine(w_own, slots, q_sems, q_chunks, count, parts)
    outs = ShardLine(o_own, o_all, o_sems, o_chunks, count, parts)
    line.open_line()
    keep = pltpu.make_async_copy(o_own, o_all.at[me], own_sem)
    keep.start()
    tile = 256

    def add(shard, block, first):
        def column(j, carry):
            at = pl.ds(pl.multiple_of(j * tile, tile), tile)
            product = jnp.dot(hidden[shard], block[:, at], preferred_element_type=jnp.float32)
            total[:, at] = product if first else total[:, at] + product
            return carry

        lax.fori_loop(0, total.shape[1] // tile, column, 0)

    def finish(step):
        for way in (0, 1):
            shard = line.shard_of(step, way)

            @pl.when(line.present(step, way))
            def _():
                line.complete(shard)
                add(shard, slots.at[shard], False)

    add(me, w_own, True)

    def q_step(step, carry):
        line.relay(step)

        @pl.when(step > 1)
        def _():
            finish(step - 1)

        return carry

    lax.fori_loop(1, count, q_step, 0)
    outs.open_line()
    finish(count - 1)
    qkv[...] = total[...].astype(qkv.dtype)

    def o_step(step, carry):
        outs.relay(step)
        return carry

    lax.fori_loop(1, count, o_step, 0)

    def last(step, carry):
        line.close_sends(step)
        outs.close_sends(step)
        for way in (0, 1):
            shard = outs.shard_of(step, way)

            @pl.when(outs.present(step, way))
            def _():
                outs.complete(shard)

        return carry

    lax.fori_loop(1, count, last, 0)
    line.close_own()
    outs.close_own()
    keep.wait()


def project(hidden, w_own, o_own):
    count, parts = lax.axis_size("seq"), lax.axis_size("groups")
    rows, depth = hidden.shape
    hidden = hidden.reshape(rows, count, depth // count).transpose(1, 0, 2)
    width = w_own.shape[1]
    most = 4 if count <= 8 else 1
    q_chunks = pieces_of(w_own.shape[0] // parts, most)
    o_chunks = pieces_of(o_own.shape[0] // parts, most)
    vmem = pl.BlockSpec(memory_space=pltpu.VMEM)
    return pl.pallas_call(
        functools.partial(project_kernel, count, parts, q_chunks, o_chunks),
        out_shape=[
            jax.ShapeDtypeStruct((rows, width), jnp.bfloat16),
            jax.ShapeDtypeStruct((count,) + o_own.shape, jnp.bfloat16),
        ],
        in_specs=[vmem] * 3,
        out_specs=[vmem, pl.BlockSpec(memory_space=pl.ANY)],
        scratch_shapes=[
            pltpu.VMEM((count,) + w_own.shape, jnp.bfloat16),
            pltpu.VMEM((rows, width), jnp.float32),
            pltpu.SemaphoreType.DMA((1 + parts, 2, count, q_chunks)),
            pltpu.SemaphoreType.DMA((1 + parts, 2, count, o_chunks)),
            pltpu.SemaphoreType.DMA,
        ],
        compiler_params=pltpu.CompilerParams(
            collective_id=0, has_side_effects=True, vmem_limit_bytes=48 * 1024 * 1024
        ),
        name="project",
    )(hidden, w_own, o_own)


def mix_kernel(heads, subs, chunks, attn, w_all, gate, update, slots, total, x_sems, c_sems):
    head, sub = lax.axis_index("head"), lax.axis_index("sub")
    barrier = pltpu.get_barrier_semaphore()
    for hop in range(1, heads):
        pl.semaphore_signal(
            barrier, inc=1, device_id={"head": lax.rem(head + hop, heads)}, device_id_type=MESH
        )
    for hop in range(1, subs):
        pl.semaphore_signal(
            barrier, inc=1, device_id={"sub": lax.rem(sub + hop, subs)}, device_id_type=MESH
        )
    pl.semaphore_wait(barrier, heads + subs - 2)
    size = attn.shape[0] // chunks

    def to_head(hop, chunk):
        rows = pl.ds(chunk * size, size)
        return pltpu.make_async_remote_copy(
            src_ref=attn.at[rows],
            dst_ref=slots.at[hop, 0, rows],
            send_sem=x_sems.at[hop, 0, chunk],
            recv_sem=x_sems.at[hop, 1, chunk],
            device_id={"head": lax.rem(head + hop, heads)},
            device_id_type=MESH,
        )

    def to_sub(hop, turn, chunk):
        rows = pl.ds(chunk * size, size)
        return pltpu.make_async_remote_copy(
            src_ref=attn.at[rows] if hop == 0 else slots.at[hop, 0, rows],
            dst_ref=slots.at[hop, turn, rows],
            send_sem=c_sems.at[hop, turn, 0, chunk],
            recv_sem=c_sems.at[hop, turn, 1, chunk],
            device_id={"sub": lax.rem(sub + turn, subs)},
            device_id_type=MESH,
        )

    for chunk in range(chunks):
        for hop in range(1, heads):
            to_head(hop, chunk).start()
        for turn in range(1, subs):
            to_sub(0, turn, chunk).start()

    def add(chunk, hop, turn, first):
        rows = slice(chunk * size, (chunk + 1) * size)
        owner = lax.rem(head + heads - hop, heads) * subs + lax.rem(sub + subs - turn, subs)
        block = attn[rows, :] if hop == 0 and turn == 0 else slots[hop, turn, rows, :]
        product = jnp.dot(block, w_all[owner], preferred_element_type=jnp.float32)
        total[rows, :] = product if first else total[rows, :] + product

    for chunk in range(chunks):
        add(chunk, 0, 0, True)
    for chunk in range(chunks):
        for turn in range(1, subs):
            to_sub(0, turn, chunk).wait_recv()
            add(chunk, 0, turn, False)
    for chunk in range(chunks):
        for hop in range(1, heads):
            to_head(hop, chunk).wait_recv()
            for turn in range(1, subs):
                to_sub(hop, turn, chunk).start()
            add(chunk, hop, 0, False)
    for chunk in range(chunks):
        for hop in range(1, heads):
            for turn in range(1, subs):
                to_sub(hop, turn, chunk).wait_recv()
                add(chunk, hop, turn, False)
        rows = slice(chunk * size, (chunk + 1) * size)
        update[rows, :] = (gate[...] * total[rows, :]).astype(update.dtype)
    for chunk in range(chunks):
        for hop in range(1, heads):
            to_head(hop, chunk).wait_send()
        for hop in range(heads):
            for turn in range(1, subs):
                to_sub(hop, turn, chunk).wait_send()


def mix(attention, w_all, gate):
    heads, subs = lax.axis_size("head"), lax.axis_size("sub")
    rows, width = attention.shape
    chunks = pieces_of(rows, 2)
    vmem = pl.BlockSpec(memory_space=pltpu.VMEM)
    return pl.pallas_call(
        functools.partial(mix_kernel, heads, subs, chunks),
        out_shape=jax.ShapeDtypeStruct((rows, w_all.shape[-1]), jnp.bfloat16),
        in_specs=[vmem] * 3,
        out_specs=vmem,
        scratch_shapes=[
            pltpu.VMEM((heads, subs, rows, width), jnp.bfloat16),
            pltpu.VMEM((rows, w_all.shape[-1]), jnp.float32),
            pltpu.SemaphoreType.DMA((heads, 2, chunks)),
            pltpu.SemaphoreType.DMA((heads, subs, 2, chunks)),
        ],
        compiler_params=pltpu.CompilerParams(
            collective_id=1, has_side_effects=True, vmem_limit_bytes=40 * 1024 * 1024
        ),
        name="mix",
    )(attention, w_all, gate)


def modulate(tokens, modulation):
    values = tokens.astype(jnp.float32)
    center = jnp.mean(values, axis=-1, keepdims=True)
    spread = jnp.mean(jnp.square(values - center), axis=-1, keepdims=True)
    normed = (values - center) * lax.rsqrt(spread + EPSILON)
    return (normed * (1.0 + modulation[1]) + modulation[0]).astype(jnp.bfloat16)


def shards(tokens, modulation, w_qkv, w_out, pattern, counts, spatial_mask):
    row_count, feature_width = tokens.shape
    pairs_local = w_qkv.shape[1]
    head_size = w_qkv.shape[2] // 6
    frames_local = spatial_mask.shape[0]
    positions = row_count // frames_local
    slot_total = pattern.shape[1]
    scale_factor = 1.0 / math.sqrt(head_size)
    hidden = modulate(tokens, modulation)
    projected, whole_out = project(hidden, w_qkv.reshape(w_qkv.shape[0], -1), w_out)
    packed = projected.reshape(
        frames_local, positions, pairs_local, 6 * head_size
    )
    temporal_in = packed[..., : 3 * head_size].transpose(1, 0, 2, 3)
    received = lax.all_to_all(temporal_in, "seq", split_axis=0, concat_axis=1, tiled=True)
    position_span, frame_total, items, _ = received.shape
    relaid = received.reshape(position_span * frame_total, items, 3 * head_size)
    extended = with_halo(relaid[:, :, head_size:], (("seq", 0),), WIN * BLOCK)
    block_count = position_span * frame_total // BLOCK
    key_table = extended.reshape(block_count + 2 * WIN, BLOCK, items, 2 * head_size)
    queries = relaid[:, :, :head_size].reshape(block_count, BLOCK, items, head_size)
    offsets = pattern - (lax.axis_index("seq") * block_count - WIN)

    def slot_step(slot_index, state_pair):
        numerator, denominator = state_pair
        chosen = lax.dynamic_index_in_dim(offsets, slot_index, 1, keepdims=False)
        picked = jnp.take(key_table, chosen, axis=0)
        scores = (
            jnp.einsum(
                "bqnc,bknc->bnqk",
                queries,
                picked[..., :head_size],
                preferred_element_type=jnp.float32,
            )
            * scale_factor
        )
        alive = (slot_index < counts).astype(jnp.float32)
        weights = jnp.exp(scores) * alive[:, None, None, None]
        numerator = numerator + jnp.einsum(
            "bnqk,bknc->bnqc",
            weights.astype(jnp.bfloat16),
            picked[..., head_size:],
            preferred_element_type=jnp.float32,
        )
        return (numerator, denominator + jnp.sum(weights, axis=-1))

    start_state = (
        jnp.zeros((block_count, items, BLOCK, head_size), jnp.float32),
        jnp.zeros((block_count, items, BLOCK), jnp.float32),
    )
    numerator, denominator = lax.fori_loop(0, slot_total, slot_step, start_state)
    outcome = (numerator / denominator[..., None]).astype(jnp.bfloat16)
    outcome = outcome.transpose(0, 2, 1, 3).reshape(position_span, frame_total, items, head_size)
    temporal_out = lax.all_to_all(outcome, "seq", split_axis=1, concat_axis=0, tiled=True)
    spatial = packed[..., 3 * head_size :]
    blocks_frame = positions // BLOCK
    scores = (
        jnp.einsum(
            "fpnc,fqnc->fnpq",
            spatial[..., :head_size],
            spatial[..., head_size : 2 * head_size],
            preferred_element_type=jnp.float32,
        )
        * scale_factor
    )
    keep = spatial_mask.astype(jnp.float32)[:, None, :, None, :, None]
    weights = (
        jnp.exp(scores).reshape(frames_local, pairs_local, blocks_frame, BLOCK, blocks_frame, BLOCK)
        * keep
    )
    weights = weights.reshape(frames_local, pairs_local, positions, positions)
    denominator = jnp.sum(weights, axis=-1)
    numerator = jnp.einsum(
        "fnpq,fqnc->fpnc",
        weights.astype(jnp.bfloat16),
        spatial[..., 2 * head_size :],
        preferred_element_type=jnp.float32,
    )
    spatial_out = (numerator / denominator.transpose(0, 2, 1)[..., None]).astype(jnp.bfloat16)
    attention = jnp.concatenate([temporal_out.transpose(1, 0, 2, 3), spatial_out], axis=-1)
    attention = attention.reshape(row_count, pairs_local * 2 * head_size)
    out_width = w_out.shape[1]
    blocks = lax.axis_size("head") * lax.axis_size("sub")
    gate_slice = lax.dynamic_slice_in_dim(
        modulation[2], lax.axis_index(("head", "sub")) * out_width, out_width, 0
    )
    return mix(attention, whole_out.reshape(blocks, -1, out_width), gate_slice[None, :])

def push(source, target, send_sem, recv_sem, axis, place):
    return pltpu.make_async_remote_copy(
        src_ref=source,
        dst_ref=target,
        send_sem=send_sem,
        recv_sem=recv_sem,
        device_id={axis: place},
        device_id_type=MESH,
    )


def seats(count):
    return (count // 2 - 1, count // 2)


def by_pair_kernel(
    sizes, chunks, pieces, o_chunks,
    tokens, modulation, w_own, o_own, pattern, counts, mask, update,
    held, raw, stage, passing, partial, hfull, wfull, tq, sq, o_all, lists, lists_all, table, own, slots,
    tok_sems, l_sems, w_sems, p_sems, z_sems, x_sems, c_sems, o_sems, keep_sems, sz_sems, sx_sems, sc_sems, own_sems,
):
    count, parts, heads, subs = sizes
    low, high = seats(count)
    me, group = lax.axis_index("seq"), lax.axis_index("groups")
    head, sub = lax.axis_index("head"), lax.axis_index("sub")
    other = low + high - me
    near = jnp.where(me == low, low - 1, high + 1)
    far = jnp.where(me == low, high + 1, low - 1)
    seated = jnp.logical_or(me == low, me == high)
    ended = jnp.logical_not(seated)
    outward = jnp.where(me == low, 1, 0)
    blocks = heads * subs
    quarter = held.shape[1]
    unit = quarter // chunks
    width = wfull.shape[2]
    half = w_own.shape[0] // parts
    piece = half // pieces
    block = unit * blocks

    barrier = pltpu.get_barrier_semaphore()
    others = 0
    for axis in ("seq", "groups", "head", "sub"):
        size = lax.axis_size(axis)
        for hop in range(1, size):
            partner = lax.rem(lax.axis_index(axis) + hop, size)
            pl.semaphore_signal(barrier, inc=1, device_id={axis: partner}, device_id_type=MESH)
            others += 1

    def rows_of(head_hop, sub_hop, chunk):
        owner = lax.rem(head + heads - head_hop, heads) * subs + lax.rem(sub + subs - sub_hop, subs)
        return pl.ds(pl.multiple_of((chunk * blocks + owner) * unit, unit), unit)

    def fetch(hop, chunk):
        return pltpu.make_async_copy(
            tokens.at[rows_of(hop, 0, chunk)], held.at[hop, pl.ds(chunk * unit, unit)],
            tok_sems.at[hop, chunk],
        )

    for chunk in range(chunks):
        fetch(0, chunk).start()
    raw_copy = pltpu.make_async_copy(w_own, raw, own_sems.at[0])
    raw_copy.start()
    o_copy = pltpu.make_async_copy(o_own, o_all.at[me], own_sems.at[1])
    o_copy.start()

    @pl.when(seated)
    def _():
        for hop in range(1, heads):
            for chunk in range(chunks):
                fetch(hop, chunk).start()

    lists[...] = jnp.zeros_like(lists)
    slots_of = pattern.shape[1]
    lists[0 : pattern.shape[0], 0:slots_of] = pattern[...]
    lists[8 : 8 + mask.shape[0], 0 : mask.shape[1]] = mask[...]
    lists[16:17, 0 : counts.shape[1]] = counts[...]
    gain = 1.0 + modulation[1:2, :]
    shift = modulation[0:1, :]

    def modulate_rows(hop, first, last):
        def some(i, carry):
            at = pl.ds(pl.multiple_of(i * 16, 16), 16)
            chunk = i // (unit // 16)
            owner = lax.rem(head + heads - hop, heads) * subs + sub
            start = (chunk * blocks + owner) * unit + lax.rem(i, unit // 16) * 16
            values = held[hop, at, :].astype(jnp.float32)
            centered = values - jnp.mean(values, axis=-1, keepdims=True)
            spread_of = jnp.mean(jnp.square(centered), axis=-1, keepdims=True)
            normed = centered * lax.rsqrt(spread_of + EPSILON)
            hfull[me, pl.ds(pl.multiple_of(start, 16), 16), :] = (normed * gain + shift).astype(hfull.dtype)
            return carry

        for chunk in range(first, last):
            fetch(hop, chunk).wait()
        lax.fori_loop(first * unit // 16, last * unit // 16, some, 0, unroll=2)

    modulate_rows(0, 0, 1)
    pl.semaphore_wait(barrier, others)

    def spot(frame, head_hop, sub_hop, chunk):
        return hfull.at[frame, rows_of(head_hop, sub_hop, chunk)]

    def z_push(frame, chunk, place):
        target = spot(frame, 0, 0, chunk)
        return push(target, target, z_sems.at[0, frame, chunk], z_sems.at[1, frame, chunk], "seq", place)

    def x_push(frame, chunk, hop):
        target = spot(frame, 0, 0, chunk)
        return push(
            target, target, x_sems.at[hop, 0, frame, chunk], x_sems.at[hop, 1, frame, chunk],
            "head", lax.rem(head + hop, heads),
        )

    def c_push(frame, chunk, hop, turn):
        target = spot(frame, hop, 0, chunk)
        return push(
            target, target, c_sems.at[hop, turn, 0, frame, chunk], c_sems.at[hop, turn, 1, frame, chunk],
            "sub", lax.rem(sub + turn, subs),
        )

    def l_push(seat):
        return push(lists, lists_all.at[me], l_sems.at[0, seat - low], l_sems.at[1, me], "seq", seat)

    def w_rows(part, step):
        return pl.ds(pl.multiple_of(part * half + step * piece, piece), piece)

    def w_along(seat, source, step):
        return push(
            stage.at[seat - low, pl.ds(step * piece, piece)], wfull.at[source, w_rows(group, step)],
            w_sems.at[0, 0, seat - low, step], w_sems.at[0, 1, source, step], "seq", seat,
        )

    def w_hand(step, place):
        return push(
            stage.at[jnp.where(me < low, high, low) - low, pl.ds(step * piece, piece)],
            passing.at[pl.ds(step * piece, piece)],
            p_sems.at[0, step], p_sems.at[1, step], "seq", place,
        )

    def w_pass(source, step):
        return push(
            passing.at[pl.ds(step * piece, piece)], wfull.at[source, w_rows(group, step)],
            w_sems.at[0, 0, me - low, step], w_sems.at[0, 1, source, step], "seq", other,
        )

    def w_across(source, step, turn):
        target = wfull.at[source, w_rows(group, step)]
        return push(
            target, target, w_sems.at[turn, 0, source, step], w_sems.at[turn, 1, source, step],
            "groups", lax.rem(group + turn, parts),
        )

    outs = LineGather(o_all, o_sems, o_chunks, count, parts)

    for seat in (low, high):
        @pl.when(me != seat)
        def _():
            l_push(seat).start()

    columns_of = own.shape[2]

    def item(hop, turn, seat, chunk):
        return out_spot(slots, hop, turn, seat, chunk, block, low, columns_of)

    def to_head(hop, seat, chunk, source=None):
        return push(
            item(0, 0, seat, chunk) if source is None else source, item(hop, 0, seat, chunk),
            sx_sems.at[hop, 0, seat - low, chunk], sx_sems.at[hop, 1, seat - low, chunk],
            "head", lax.rem(head + hop, heads),
        )

    def to_sub(hop, turn, seat, chunk, source=None):
        return push(
            item(hop, 0, seat, chunk) if source is None else source, item(hop, turn, seat, chunk),
            sc_sems.at[hop, turn, 0, seat - low, chunk], sc_sems.at[hop, turn, 1, seat - low, chunk],
            "sub", lax.rem(sub + turn, subs),
        )

    toward = jnp.where(me < low, low, high)

    def relay_out(step, pieces_of_it, outgoing):
        for way in (0, 1):
            @pl.when((outward == way) == outgoing)
            def _():
                outs.relay(step, way, pieces_of_it)

    o_first, o_last = tuple(range(o_chunks // 2)), tuple(range(o_chunks // 2, o_chunks))

    def z_out(first, last):
        @pl.when(seated)
        def _():
            for chunk in range(first, last):
                z_push(me, chunk, other).start()

        @pl.when(ended)
        def _():
            for chunk in range(first, last):
                z_push(me, chunk, toward).start()

    z_out(0, 1)
    raw_copy.wait()

    def unpack(i, carry):
        start = pl.multiple_of(i * 64, 64)
        both = raw[pl.ds(pl.multiple_of(group * half + start, 64), 64)]
        first, second = both[:, 0, :], both[:, 1, :]
        stage[0, pl.ds(start, 64), :] = first
        stage[1, pl.ds(start, 64), :] = second
        return carry

    lax.fori_loop(0, half // 64, unpack, 0)

    @pl.when(ended)
    def _():
        for step in range(pieces):
            w_hand(step, toward).start()

    @pl.when(seated)
    def _():
        for step in range(pieces):
            w_along(other, me, step).start()

    modulate_rows(0, 1, chunks)
    o_copy.wait()

    @pl.when(ended)
    def _():
        z_out(1, chunks)
        for step in range(pieces):
            w_along(toward, me, step).start()
        for way in (0, 1):
            outs.open_way(way)
        for way in (0, 1):
            outs.relay(1, way)

    @pl.when(seated)
    def _():
        for way in (0, 1):
            @pl.when(outward == way)
            def _():
                outs.open_way(way)

        keep = pltpu.make_async_copy(lists, lists_all.at[me], own_sems.at[2])
        keep.start()
        for chunk in range(chunks):
            for turn in range(1, subs):
                c_push(me, chunk, 0, turn).start()
        for hop in range(1, heads):
            modulate_rows(hop, 0, chunks)
            for chunk in range(chunks):
                for turn in range(1, subs):
                    c_push(me, chunk, hop, turn).start()

        def land(frame, chunk):
            z_push(frame, chunk, other).wait_recv()
            for hop in range(1, heads):
                x_push(frame, chunk, hop).start()
            for turn in range(1, subs):
                c_push(frame, chunk, 0, turn).start()

        def crossed(frame, chunk):
            for hop in range(1, heads):
                x_push(frame, chunk, hop).wait_recv()
                for turn in range(1, subs):
                    c_push(frame, chunk, hop, turn).start()

        def gathered(frame, chunk):
            for hop in range(heads):
                for turn in range(1, subs):
                    c_push(frame, chunk, hop, turn).wait_recv()

        def keep_pair(i, carry):
            at = pl.ds(pl.multiple_of(i * 64, 64), 64)
            both = raw[at]
            wfull[me, at, :] = jnp.where(me == low, both[:, 0, :], both[:, 1, :])
            return carry

        def w_land(source, step):
            w_along(me, source, step).wait_recv()
            for turn in range(1, parts):
                w_across(source, step, turn).start()

        span = unit
        scale = math.log2(math.e) / math.sqrt(own.shape[2] // 2)
        size = own.shape[2] // 2
        total_blocks = tq.shape[0]
        each = total_blocks // count
        window = 2 * WIN + 1

        depth = wfull.shape[1]

        def first_part(frame, slot):
            def some_rows(chunk, carry):
                rows = pl.ds(pl.multiple_of(chunk * block, block), block)
                partial[slot, rows, :] = jnp.dot(
                    hfull[frame, rows, low * depth : (high + 1) * depth],
                    wfull[low : high + 1].reshape(-1, width), preferred_element_type=jnp.float32,
                )
                return carry

            lax.fori_loop(0, chunks, some_rows, 0)

        def keep_qkv(frame, chunk, total):
            at = pl.ds(pl.multiple_of(frame * span, span), span)
            for i in range(blocks):
                tq[chunk * blocks + i, at, :] = total[i * span : (i + 1) * span, : 3 * size]
            sq[frame, pl.ds(pl.multiple_of(chunk * block, block), block), :] = total[:, 3 * size :]

        land(near, 0)
        land(other, 0)
        for step in range(pieces):
            w_hand(step, other).wait_recv()
            w_pass(near, step).start()
            w_land(other, step)
        for chunk in range(1, chunks):
            z_push(me, chunk, other).start()
        z_push(near, 0, other).start()
        crossed(near, 0)
        crossed(other, 0)
        lax.fori_loop(0, w_own.shape[0] // 64, keep_pair, 0)
        rest = max(pieces, chunks - 1)
        for i in range(rest):
            if i + 1 < chunks:
                land(near, i + 1)
                z_push(near, i + 1, other).start()
            if i < pieces:
                w_land(far, i)
        for way in (0, 1):
            @pl.when(outward != way)
            def _():
                outs.open_way(way)
        def crossed_w(source):
            for step in range(pieces):
                for turn in range(1, parts):
                    w_across(source, step, turn).wait_recv()

        def all_in(frame):
            for chunk in range(chunks):
                gathered(frame, chunk)

        crossed_w(other)
        all_in(me)
        first_part(me, 0)
        for i in range(rest):
            if i + 1 < chunks:
                land(other, i + 1)
            if i < pieces:
                w_land(near, i)
            if i + 1 < chunks:
                crossed(near, i + 1)
            if i == rest - 1:
                all_in(near)
                first_part(near, 1)
        for i in range(1, chunks):
            crossed(other, i)
        land(far, 0)
        all_in(other)
        first_part(other, 2)

        for source in (near, other, far):
            l_push_from(lists_all, lists, l_sems, source, low, me).wait_recv()
        keep.wait()
        to_table = pltpu.make_async_copy(lists_all, table, own_sems.at[3])
        to_table.start()

        def project(frame, chunk):
            rows = pl.ds(pl.multiple_of(chunk * block, block), block)
            total = jnp.dot(
                hfull[frame, rows, :], wfull[...].reshape(-1, width), preferred_element_type=jnp.float32
            ).astype(tq.dtype)
            keep_qkv(frame, chunk, total)

        def project_frame(frame, slot):
            def last_part(chunk, carry):
                rows = pl.ds(pl.multiple_of(chunk * block, block), block)
                total = partial[slot, rows, :]
                for source in (0, count - 1):
                    at = slice(source * depth, (source + 1) * depth)
                    total = total + jnp.dot(
                        hfull[frame, rows, at], wfull[source], preferred_element_type=jnp.float32
                    )
                keep_qkv(frame, chunk, total.astype(tq.dtype))
                return carry

            lax.fori_loop(0, chunks, last_part, 0)

        def soft(q, keys, values, biases):
            scores = lax.dot_general(
                q, keys, (((1,), (1,)), ((), ())), preferred_element_type=jnp.float32
            )
            parts_of = []
            sums = None
            for i, bias in enumerate(biases):
                weight = jnp.exp2(scores[:, i * BLOCK : (i + 1) * BLOCK] * scale + bias)
                sums = weight if sums is None else sums + weight
                parts_of.append(weight.astype(jnp.bfloat16))
            numerator = jnp.dot(
                jnp.concatenate(parts_of, axis=1), values, preferred_element_type=jnp.float32
            )
            return (numerator / jnp.sum(sums, axis=-1, keepdims=True)).astype(own.dtype)

        def temporal(chunk):
            def query(i, carry):
                b = chunk * blocks + i
                device, row = b // each, lax.rem(b, each)
                start = jnp.clip(b - WIN, 0, total_blocks - window)
                used = table[device, 16, row]
                biases = []
                for w in range(window):
                    times = 0
                    for j in range(slots_of):
                        hit = jnp.logical_and(j < used, table[device, row, j] == start + w)
                        times = times + jnp.where(hit, 1, 0)
                    bias = jnp.float32(-jnp.inf)
                    for m in range(1, slots_of + 1):
                        bias = jnp.where(times == m, jnp.float32(math.log2(m)), bias)
                    biases.append(bias)
                near_by = pl.ds(start, window)
                result = soft(
                    tq[b, :, :size],
                    tq[near_by, :, size : 2 * size].reshape(-1, size),
                    tq[near_by, :, 2 * size :].reshape(-1, size),
                    biases,
                )
                at = pl.ds(pl.multiple_of(b * span, span), span)
                for f in range(count):
                    own[f, at, :size] = result[f * span : (f + 1) * span]
                return carry

            lax.fori_loop(0, blocks, query, 0)

        def spatial(frame):
            per = sq.shape[1] // BLOCK

            def query(i, carry):
                at = pl.ds(pl.multiple_of(i * BLOCK, BLOCK), BLOCK)
                biases = [
                    jnp.where(table[frame, 8 + i, j] > 0, jnp.float32(0), jnp.float32(-jnp.inf))
                    for j in range(per)
                ]
                own[frame, at, size:] = soft(
                    sq[frame, at, :size], sq[frame, :, size : 2 * size], sq[frame, :, 2 * size :], biases
                )
                return carry

            lax.fori_loop(0, per, query, 0)

        def send(frame, chunk):
            out_push(own, slots, sz_sems, me, frame, chunk, block, low).start()

        def settle(chunk):
            send(near, chunk)
            send(other, chunk)
            keep_out(own, slots, keep_sems, me, chunk, block, low).start()
            mine = own.at[me, pl.ds(chunk * block, block)]
            for hop in range(1, heads):
                to_head(hop, me, chunk, mine).start()
            for turn in range(1, subs):
                to_sub(0, turn, me, chunk, mine).start()

        early = (me, near, other)
        for chunk in range(chunks + 1):
            if 0 < chunk < chunks:
                land(far, chunk)
            if chunk and chunk < chunks:
                crossed(far, chunk - 1)
            if chunk == chunks - 2:
                relay_out(1, o_first[:1], True)
            if chunk == 0:
                crossed_w(far)
                crossed_w(near)
                to_table.wait()
            if chunk < len(early):
                project_frame(early[chunk], chunk)
            if chunk and chunk <= len(early):
                spatial(early[chunk - 1])
            if chunk:
                gathered(far, chunk - 1)
                project(far, chunk - 1)
            if chunk == chunks - 2:
                relay_out(1, o_first[1:], True)
            if chunk == 1:
                relay_out(1, None, False)
            if chunk == chunks - 1:
                for ready in range(chunks - 2):
                    temporal(ready)
                    settle(ready)
                    relay_out(1, o_last[ready : ready + 1], True)
                crossed(far, chunks - 1)
        temporal(chunks - 2)
        settle(chunks - 2)
        relay_out(2, o_first, True)
        temporal(chunks - 1)
        settle(chunks - 1)
        spatial(far)
        for chunk in range(chunks):
            send(far, chunk)
        relay_out(2, o_last, True)

    def arrive(chunk, seat):
        out_push(own, slots, sz_sems, seat, me, chunk, block, low).wait_recv()
        for hop in range(1, heads):
            to_head(hop, seat, chunk).start()
        for turn in range(1, subs):
            to_sub(0, turn, seat, chunk).start()

    def pass_on(chunk, seat):
        for hop in range(1, heads):
            to_head(hop, seat, chunk).wait_recv()
            for turn in range(1, subs):
                to_sub(hop, turn, seat, chunk).start()

    columns = pl.ds(pl.multiple_of((head * subs + sub) * update.shape[1], 128), update.shape[1])
    gate = modulation[2:3, columns]

    def finish(chunk):
        for seat in (low, high):
            for hop in range(heads):
                for turn in range(1, subs):
                    to_sub(hop, turn, seat, chunk).wait_recv()
        rows = slice(chunk * block, (chunk + 1) * block)
        total = None
        for hop in range(heads):
            for turn in range(subs):
                owner = lax.rem(head + heads - hop, heads) * subs + lax.rem(sub + subs - turn, subs)
                product = jnp.dot(slots[hop, turn, rows, :], o_all[owner], preferred_element_type=jnp.float32)
                total = product if total is None else total + product
        update[rows, :] = (gate * total).astype(update.dtype)

    nearer = jnp.where(seated, me, toward)
    farther = low + high - nearer
    def relay_end(step, pieces_of_it):
        for way in (0, 1):
            outs.relay(step, way, pieces_of_it)

    @pl.when(ended)
    def _():
        relay_end(2, o_first)
        for chunk in range(chunks):
            arrive(chunk, nearer)
            if chunk == chunks // 2 - 1:
                relay_end(2, o_last)
                relay_end(3, o_first)

    for chunk in range(chunks):
        arrive(chunk, farther)
        if chunk % 2:
            @pl.when(ended)
            def _():
                relay_end(3, o_last[chunk // 2 :: chunks // 2])

    for seat in (nearer, farther):
        for chunk in range(chunks):
            pass_on(chunk, seat)

    @pl.when(seated)
    def _():
        for chunk in range(chunks):
            keep_out(own, slots, keep_sems, me, chunk, block, low).wait()

    for step in range(1, count):
        for way in (0, 1):
            @pl.when(outs.present(step, way))
            def _():
                outs.complete(outs.shard_of(step, way))
    for chunk in range(chunks):
        finish(chunk)

    for seat in (low, high):
        @pl.when(me != seat)
        def _():
            l_push(seat).wait_send()

    @pl.when(ended)
    def _():
        for step in range(pieces):
            w_hand(step, toward).wait_send()
            w_along(toward, me, step).wait_send()
        for chunk in range(chunks):
            z_push(me, chunk, jnp.where(me < low, low, high)).wait_send()

    @pl.when(seated)
    def _():
        for step in range(pieces):
            w_along(other, me, step).wait_send()
            w_pass(near, step).wait_send()
        for chunk in range(chunks):
            z_push(me, chunk, other).wait_send()
            z_push(near, chunk, other).wait_send()
            for frame in (me, near, other, far):
                for hop in range(heads):
                    for turn in range(1, subs):
                        c_push(frame, chunk, hop, turn).wait_send()
            for frame in (near, other, far):
                for hop in range(1, heads):
                    x_push(frame, chunk, hop).wait_send()
                out_push(own, slots, sz_sems, me, frame, chunk, block, low).wait_send()
        for source in (near, other, far):
            for step in range(pieces):
                for turn in range(1, parts):
                    w_across(source, step, turn).wait_send()

    for way in (0, 1):
        outs.close_way(way)
    for step in range(1, count):
        for way in (0, 1):
            outs.close_sends(step, way)
    for chunk in range(chunks):
        for seat in (low, high):
            for hop in range(1, heads):
                to_head(hop, seat, chunk).wait_send()
            for hop in range(heads):
                for turn in range(1, subs):
                    to_sub(hop, turn, seat, chunk).wait_send()


def l_push_from(lists_all, lists, l_sems, source, low, me):
    return push(lists, lists_all.at[source], l_sems.at[0, me - low], l_sems.at[1, source], "seq", me)


def out_spot(slots, hop, turn, seat, chunk, block, low, columns):
    at = (seat - low) * columns
    at = pl.ds(pl.multiple_of(at, columns), columns)
    return slots.at[hop, turn, pl.ds(chunk * block, block), at]


def out_push(own, slots, sems, seat, frame, chunk, block, low):
    return push(
        own.at[frame, pl.ds(chunk * block, block)],
        out_spot(slots, 0, 0, seat, chunk, block, low, own.shape[2]),
        sems.at[0, frame, chunk], sems.at[1, seat, chunk], "seq", frame,
    )


def keep_out(own, slots, sems, seat, chunk, block, low):
    return pltpu.make_async_copy(
        own.at[seat, pl.ds(chunk * block, block)],
        out_spot(slots, 0, 0, seat, chunk, block, low, own.shape[2]),
        sems.at[chunk],
    )


class LineGather:
    def __init__(self, slots, sems, chunks, count, parts):
        self.slots, self.chunks = slots, chunks
        self.sems, self.count, self.parts = sems, count, parts
        self.me = lax.axis_index("seq")
        self.group = lax.axis_index("groups")
        self.size = slots.shape[1] // (parts * chunks)

    def rows(self, group, chunk):
        start = (group * self.chunks + chunk) * self.size
        return pl.ds(pl.multiple_of(start, self.size), self.size)

    def along(self, shard, chunk, way):
        rows = self.rows(self.group, chunk)
        return push(
            self.slots.at[shard, rows], self.slots.at[shard, rows],
            self.sems.at[way, 0, shard, chunk], self.sems.at[way, 1, shard, chunk],
            "seq", self.me + (1 if way == 0 else -1),
        )

    def across(self, shard, chunk, hop):
        rows = self.rows(self.group, chunk)
        return push(
            self.slots.at[shard, rows], self.slots.at[shard, rows],
            self.sems.at[1 + hop, 0, shard, chunk], self.sems.at[1 + hop, 1, shard, chunk],
            "groups", lax.rem(self.group + hop, self.parts),
        )

    def onward(self, way):
        return self.me < self.count - 1 if way == 0 else self.me > 0

    def shard_of(self, step, way):
        return self.me - step if way == 0 else self.me + step

    def present(self, step, way):
        return self.me >= step if way == 0 else self.me + step < self.count

    def open_way(self, way, chunks=None):
        @pl.when(self.onward(way))
        def _():
            for chunk in range(self.chunks) if chunks is None else chunks:
                self.along(self.me, chunk, way).start()

    def relay(self, step, way, chunks=None):
        shard = self.shard_of(step, way)

        @pl.when(self.present(step, way))
        def _():
            for chunk in range(self.chunks) if chunks is None else chunks:
                self.along(shard, chunk, way).wait_recv()

                @pl.when(self.onward(way))
                def _():
                    self.along(shard, chunk, way).start()

                for hop in range(1, self.parts):
                    self.across(shard, chunk, hop).start()

    def complete(self, shard):
        for chunk in range(self.chunks):
            for hop in range(1, self.parts):
                self.across(shard, chunk, hop).wait_recv()

    def close_sends(self, step, way):
        shard = self.shard_of(step, way)

        @pl.when(self.present(step, way))
        def _():
            for chunk in range(self.chunks):
                @pl.when(self.onward(way))
                def _():
                    self.along(shard, chunk, way).wait_send()

                for hop in range(1, self.parts):
                    self.across(shard, chunk, hop).wait_send()

    def close_way(self, way):
        @pl.when(self.onward(way))
        def _():
            for chunk in range(self.chunks):
                self.along(self.me, chunk, way).wait_send()


def by_pair(tokens, modulation, w_own, o_own, pattern, counts, mask):
    sizes = tuple(lax.axis_size(axis) for axis in ("seq", "groups", "head", "sub"))
    count, parts, heads, subs = sizes
    rows, depth = tokens.shape
    width = w_own.shape[2]
    blocks = heads * subs
    quarter = rows // blocks
    chunks = rows // BLOCK
    pieces = 3
    o_chunks = 4
    columns = width // 3
    seated = len(seats(count))
    vmem = pl.BlockSpec(memory_space=pltpu.VMEM)
    whole = pl.BlockSpec(memory_space=pl.ANY)
    dma = pltpu.SemaphoreType.DMA
    kept = jnp.bfloat16
    return pl.pallas_call(
        functools.partial(by_pair_kernel, sizes, chunks, pieces, o_chunks),
        out_shape=jax.ShapeDtypeStruct((rows, o_own.shape[1]), kept),
        in_specs=[whole, vmem, whole, whole, vmem, vmem, vmem],
        out_specs=vmem,
        scratch_shapes=[
            pltpu.VMEM((heads, quarter, depth), kept),
            pltpu.VMEM(w_own.shape, kept),
            pltpu.VMEM((seated, w_own.shape[0] // parts, width), kept),
            pltpu.VMEM((w_own.shape[0] // parts, width), kept),
            pltpu.VMEM((count - 1, rows, width), jnp.float32),
            pltpu.VMEM((count, rows, depth), kept),
            pltpu.VMEM((count, w_own.shape[0], width), kept),
            pltpu.VMEM((count * rows // BLOCK, BLOCK, width // 2), kept),
            pltpu.VMEM((count, rows, width // 2), kept),
            pltpu.VMEM((count,) + o_own.shape, kept),
            pltpu.VMEM((24, 128), jnp.int32),
            pltpu.VMEM((count, 24, 128), jnp.int32),
            pltpu.SMEM((count, 24, 128), jnp.int32),
            pltpu.VMEM((count, rows, columns), kept),
            pltpu.VMEM((heads, subs, rows, seated * columns), kept),
            dma((heads, chunks)),
            dma((2, count)),
            dma((parts, 2, count, pieces)),
            dma((2, pieces)),
            dma((2, count, chunks)),
            dma((heads, 2, count, chunks)),
            dma((heads, subs, 2, count, chunks)),
            dma((1 + parts, 2, count, o_chunks)),
            dma((chunks,)),
            dma((2, count, chunks)),
            dma((heads, 2, seated, chunks)),
            dma((heads, subs, 2, seated, chunks)),
            dma((4,)),
        ],
        compiler_params=pltpu.CompilerParams(
            collective_id=2, has_side_effects=True, vmem_limit_bytes=60 * 1024 * 1024
        ),
        name="by_pair",
    )(tokens, modulation, w_own, o_own, pattern, counts, mask)


def shards_by_pair(tokens, modulation, w_qkv, w_out, pattern, counts, spatial_mask):
    return by_pair(tokens, modulation, w_qkv, w_out, pattern, counts[None, :], spatial_mask[0])


def one_pair_each(count, blocks, parts, tokens, w_qkv, w_out, pattern, spatial_mask):
    rows, frames = tokens.shape[0], spatial_mask.shape[0]
    return (
        count == blocks == 4
        and w_qkv.shape[1] == len(seats(count))
        and frames == 1
        and rows == BLOCK * pattern.shape[0] == BLOCK * spatial_mask.shape[1]
        and pattern.shape[0] < 8
        and BLOCK % (16 * count) == 0
        and w_qkv.shape[0] % (192 * parts) == 0
        and w_out.shape[0] % (64 * parts) == 0
    )


def shards_any(*args):
    tokens, _, w_qkv, w_out, pattern, _, spatial_mask = args
    blocks = lax.axis_size("head") * lax.axis_size("sub")
    sizes = lax.axis_size("seq"), blocks, lax.axis_size("groups")
    if one_pair_each(*sizes, tokens, w_qkv, w_out, pattern, spatial_mask):
        return shards_by_pair(*args)
    return shards(*args)


def solution(mesh):
    return jax.shard_map(
        shards_any,
        mesh=mesh,
        in_specs=(
            P(("groups", "seq"), None),
            P(),
            P("seq", ("head", "sub"), None),
            P("seq", ("head", "sub")),
            P(("groups", "seq"), None),
            P(("groups", "seq")),
            P(("groups", "seq"), None, None),
        ),
        out_specs=P(("groups", "seq"), ("head", "sub")),
        check_vma=False,
    )
```

```python
import functools
import math

import jax
import jax.numpy as jnp
from jax import lax
from jax.experimental import pallas as pl
from jax.experimental.pallas import tpu as pltpu
from jax.sharding import PartitionSpec as P

BLOCK = 128
WIN = 2


EPSILON = 1e-06


def with_halo(cells, sides, width):
    for axis, dim in sides:
        count = lax.axis_size(axis)
        ends = count - 1
        head = lax.slice_in_dim(cells, 0, width, axis=dim)
        tail = lax.slice_in_dim(cells, cells.shape[dim] - width, cells.shape[dim], axis=dim)
        cells = jnp.concatenate(
            [
                lax.ppermute(tail, axis, [(i, (i + 1) % count) for i in range(ends)]),
                cells,
                lax.ppermute(head, axis, [((i + 1) % count, i) for i in range(ends)]),
            ],
            axis=dim,
        )
    return cells


MESH = pl.DeviceIdType.MESH


def pieces_of(rows, most=4):
    for count in range(most, 0, -1):
        if rows % (16 * count) == 0:
            return count
    return 1


class ShardLine:
    def __init__(self, own, slots, sems, chunks, count, parts):
        self.own, self.slots, self.chunks = own, slots, chunks
        self.sems, self.count, self.parts = sems, count, parts
        self.me = lax.axis_index("seq")
        self.group = lax.axis_index("groups")
        self.size = own.shape[0] // (parts * chunks)

    def rows(self, group, chunk):
        start = (group * self.chunks + chunk) * self.size
        return pl.ds(pl.multiple_of(start, self.size), self.size)

    def along(self, shard, chunk, way, own):
        rows = self.rows(self.group, chunk)
        source = self.own.at[rows] if own else self.slots.at[shard, rows]
        return pltpu.make_async_remote_copy(
            src_ref=source,
            dst_ref=self.slots.at[shard, rows],
            send_sem=self.sems.at[way, 0, shard, chunk],
            recv_sem=self.sems.at[way, 1, shard, chunk],
            device_id={"seq": self.me + (1 if way == 0 else -1)},
            device_id_type=MESH,
        )

    def across(self, shard, chunk, hop):
        rows = self.rows(self.group, chunk)
        return pltpu.make_async_remote_copy(
            src_ref=self.slots.at[shard, rows],
            dst_ref=self.slots.at[shard, rows],
            send_sem=self.sems.at[1 + hop, 0, shard, chunk],
            recv_sem=self.sems.at[1 + hop, 1, shard, chunk],
            device_id={"groups": lax.rem(self.group + hop, self.parts)},
            device_id_type=MESH,
        )

    def open_line(self):
        for chunk in range(self.chunks):
            for way in (0, 1):
                @pl.when(self.onward(way))
                def _():
                    self.along(self.me, chunk, way, True).start()

    def onward(self, way):
        return self.me < self.count - 1 if way == 0 else self.me > 0

    def shard_of(self, step, way):
        return self.me - step if way == 0 else self.me + step

    def present(self, step, way):
        return self.me >= step if way == 0 else self.me + step < self.count

    def relay(self, step):
        for chunk in range(self.chunks):
            for way in (0, 1):
                shard = self.shard_of(step, way)

                @pl.when(self.present(step, way))
                def _():
                    self.along(shard, chunk, way, False).wait_recv()

                    @pl.when(self.onward(way))
                    def _():
                        self.along(shard, chunk, way, False).start()

                    for hop in range(1, self.parts):
                        self.across(shard, chunk, hop).start()

    def complete(self, shard):
        for chunk in range(self.chunks):
            for hop in range(1, self.parts):
                self.across(shard, chunk, hop).wait_recv()

    def close_sends(self, step):
        for chunk in range(self.chunks):
            for way in (0, 1):
                shard = self.shard_of(step, way)

                @pl.when(self.present(step, way))
                def _():
                    @pl.when(self.onward(way))
                    def _():
                        self.along(shard, chunk, way, False).wait_send()

                    for hop in range(1, self.parts):
                        self.across(shard, chunk, hop).wait_send()

    def close_own(self):
        for chunk in range(self.chunks):
            for way in (0, 1):
                @pl.when(self.onward(way))
                def _():
                    self.along(self.me, chunk, way, True).wait_send()


def project_kernel(count, parts, q_chunks, o_chunks, hidden, w_own, o_own, qkv, o_all, slots, total, q_sems, o_sems, own_sem):
    me = lax.axis_index("seq")
    group = lax.axis_index("groups")
    barrier = pltpu.get_barrier_semaphore()

    @pl.when(me > 0)
    def _():
        pl.semaphore_signal(barrier, inc=1, device_id={"seq": me - 1}, device_id_type=MESH)

    @pl.when(me < count - 1)
    def _():
        pl.semaphore_signal(barrier, inc=1, device_id={"seq": me + 1}, device_id_type=MESH)

    for hop in range(1, parts):
        pl.semaphore_signal(
            barrier, inc=1, device_id={"groups": lax.rem(group + hop, parts)}, device_id_type=MESH
        )
    neighbours = jnp.where(me > 0, 1, 0) + jnp.where(me < count - 1, 1, 0) + (parts - 1)
    pl.semaphore_wait(barrier, neighbours)

    line = ShardLine(w_own, slots, q_sems, q_chunks, count, parts)
    outs = ShardLine(o_own, o_all, o_sems, o_chunks, count, parts)
    line.open_line()
    keep = pltpu.make_async_copy(o_own, o_all.at[me], own_sem)
    keep.start()
    tile = 256

    def add(shard, block, first):
        def column(j, carry):
            at = pl.ds(pl.multiple_of(j * tile, tile), tile)
            product = jnp.dot(hidden[shard], block[:, at], preferred_element_type=jnp.float32)
            total[:, at] = product if first else total[:, at] + product
            return carry

        lax.fori_loop(0, total.shape[1] // tile, column, 0)

    def finish(step):
        for way in (0, 1):
            shard = line.shard_of(step, way)

            @pl.when(line.present(step, way))
            def _():
                line.complete(shard)
                add(shard, slots.at[shard], False)

    add(me, w_own, True)

    def q_step(step, carry):
        line.relay(step)

        @pl.when(step > 1)
        def _():
            finish(step - 1)

        return carry

    lax.fori_loop(1, count, q_step, 0)
    outs.open_line()
    finish(count - 1)
    qkv[...] = total[...].astype(qkv.dtype)

    def o_step(step, carry):
        outs.relay(step)
        return carry

    lax.fori_loop(1, count, o_step, 0)

    def last(step, carry):
        line.close_sends(step)
        outs.close_sends(step)
        for way in (0, 1):
            shard = outs.shard_of(step, way)

            @pl.when(outs.present(step, way))
            def _():
                outs.complete(shard)

        return carry

    lax.fori_loop(1, count, last, 0)
    line.close_own()
    outs.close_own()
    keep.wait()


def project(hidden, w_own, o_own):
    count, parts = lax.axis_size("seq"), lax.axis_size("groups")
    rows, depth = hidden.shape
    hidden = hidden.reshape(rows, count, depth // count).transpose(1, 0, 2)
    width = w_own.shape[1]
    most = 4 if count <= 8 else 1
    q_chunks = pieces_of(w_own.shape[0] // parts, most)
    o_chunks = pieces_of(o_own.shape[0] // parts, most)
    vmem = pl.BlockSpec(memory_space=pltpu.VMEM)
    return pl.pallas_call(
        functools.partial(project_kernel, count, parts, q_chunks, o_chunks),
        out_shape=[
            jax.ShapeDtypeStruct((rows, width), jnp.bfloat16),
            jax.ShapeDtypeStruct((count,) + o_own.shape, jnp.bfloat16),
        ],
        in_specs=[vmem] * 3,
        out_specs=[vmem, pl.BlockSpec(memory_space=pl.ANY)],
        scratch_shapes=[
            pltpu.VMEM((count,) + w_own.shape, jnp.bfloat16),
            pltpu.VMEM((rows, width), jnp.float32),
            pltpu.SemaphoreType.DMA((1 + parts, 2, count, q_chunks)),
            pltpu.SemaphoreType.DMA((1 + parts, 2, count, o_chunks)),
            pltpu.SemaphoreType.DMA,
        ],
        compiler_params=pltpu.CompilerParams(
            collective_id=0, has_side_effects=True, vmem_limit_bytes=48 * 1024 * 1024
        ),
        name="project",
    )(hidden, w_own, o_own)


def mix_kernel(heads, subs, chunks, attn, w_all, gate, update, slots, total, x_sems, c_sems):
    head, sub = lax.axis_index("head"), lax.axis_index("sub")
    barrier = pltpu.get_barrier_semaphore()
    for hop in range(1, heads):
        pl.semaphore_signal(
            barrier, inc=1, device_id={"head": lax.rem(head + hop, heads)}, device_id_type=MESH
        )
    for hop in range(1, subs):
        pl.semaphore_signal(
            barrier, inc=1, device_id={"sub": lax.rem(sub + hop, subs)}, device_id_type=MESH
        )
    pl.semaphore_wait(barrier, heads + subs - 2)
    size = attn.shape[0] // chunks

    def to_head(hop, chunk):
        rows = pl.ds(chunk * size, size)
        return pltpu.make_async_remote_copy(
            src_ref=attn.at[rows],
            dst_ref=slots.at[hop, 0, rows],
            send_sem=x_sems.at[hop, 0, chunk],
            recv_sem=x_sems.at[hop, 1, chunk],
            device_id={"head": lax.rem(head + hop, heads)},
            device_id_type=MESH,
        )

    def to_sub(hop, turn, chunk):
        rows = pl.ds(chunk * size, size)
        return pltpu.make_async_remote_copy(
            src_ref=attn.at[rows] if hop == 0 else slots.at[hop, 0, rows],
            dst_ref=slots.at[hop, turn, rows],
            send_sem=c_sems.at[hop, turn, 0, chunk],
            recv_sem=c_sems.at[hop, turn, 1, chunk],
            device_id={"sub": lax.rem(sub + turn, subs)},
            device_id_type=MESH,
        )

    for chunk in range(chunks):
        for hop in range(1, heads):
            to_head(hop, chunk).start()
        for turn in range(1, subs):
            to_sub(0, turn, chunk).start()

    def add(chunk, hop, turn, first):
        rows = slice(chunk * size, (chunk + 1) * size)
        owner = lax.rem(head + heads - hop, heads) * subs + lax.rem(sub + subs - turn, subs)
        block = attn[rows, :] if hop == 0 and turn == 0 else slots[hop, turn, rows, :]
        product = jnp.dot(block, w_all[owner], preferred_element_type=jnp.float32)
        total[rows, :] = product if first else total[rows, :] + product

    for chunk in range(chunks):
        add(chunk, 0, 0, True)
    for chunk in range(chunks):
        for turn in range(1, subs):
            to_sub(0, turn, chunk).wait_recv()
            add(chunk, 0, turn, False)
    for chunk in range(chunks):
        for hop in range(1, heads):
            to_head(hop, chunk).wait_recv()
            for turn in range(1, subs):
                to_sub(hop, turn, chunk).start()
            add(chunk, hop, 0, False)
    for chunk in range(chunks):
        for hop in range(1, heads):
            for turn in range(1, subs):
                to_sub(hop, turn, chunk).wait_recv()
                add(chunk, hop, turn, False)
        rows = slice(chunk * size, (chunk + 1) * size)
        update[rows, :] = (gate[...] * total[rows, :]).astype(update.dtype)
    for chunk in range(chunks):
        for hop in range(1, heads):
            to_head(hop, chunk).wait_send()
        for hop in range(heads):
            for turn in range(1, subs):
                to_sub(hop, turn, chunk).wait_send()


def mix(attention, w_all, gate):
    heads, subs = lax.axis_size("head"), lax.axis_size("sub")
    rows, width = attention.shape
    chunks = pieces_of(rows, 2)
    vmem = pl.BlockSpec(memory_space=pltpu.VMEM)
    return pl.pallas_call(
        functools.partial(mix_kernel, heads, subs, chunks),
        out_shape=jax.ShapeDtypeStruct((rows, w_all.shape[-1]), jnp.bfloat16),
        in_specs=[vmem] * 3,
        out_specs=vmem,
        scratch_shapes=[
            pltpu.VMEM((heads, subs, rows, width), jnp.bfloat16),
            pltpu.VMEM((rows, w_all.shape[-1]), jnp.float32),
            pltpu.SemaphoreType.DMA((heads, 2, chunks)),
            pltpu.SemaphoreType.DMA((heads, subs, 2, chunks)),
        ],
        compiler_params=pltpu.CompilerParams(
            collective_id=1, has_side_effects=True, vmem_limit_bytes=40 * 1024 * 1024
        ),
        name="mix",
    )(attention, w_all, gate)


def modulate(tokens, modulation):
    values = tokens.astype(jnp.float32)
    center = jnp.mean(values, axis=-1, keepdims=True)
    spread = jnp.mean(jnp.square(values - center), axis=-1, keepdims=True)
    normed = (values - center) * lax.rsqrt(spread + EPSILON)
    return (normed * (1.0 + modulation[1]) + modulation[0]).astype(jnp.bfloat16)


def shards(tokens, modulation, w_qkv, w_out, pattern, counts, spatial_mask):
    row_count, feature_width = tokens.shape
    pairs_local = w_qkv.shape[1]
    head_size = w_qkv.shape[2] // 6
    frames_local = spatial_mask.shape[0]
    positions = row_count // frames_local
    slot_total = pattern.shape[1]
    scale_factor = 1.0 / math.sqrt(head_size)
    hidden = modulate(tokens, modulation)
    projected, whole_out = project(hidden, w_qkv.reshape(w_qkv.shape[0], -1), w_out)
    packed = projected.reshape(
        frames_local, positions, pairs_local, 6 * head_size
    )
    temporal_in = packed[..., : 3 * head_size].transpose(1, 0, 2, 3)
    received = lax.all_to_all(temporal_in, "seq", split_axis=0, concat_axis=1, tiled=True)
    position_span, frame_total, items, _ = received.shape
    relaid = received.reshape(position_span * frame_total, items, 3 * head_size)
    extended = with_halo(relaid[:, :, head_size:], (("seq", 0),), WIN * BLOCK)
    block_count = position_span * frame_total // BLOCK
    key_table = extended.reshape(block_count + 2 * WIN, BLOCK, items, 2 * head_size)
    queries = relaid[:, :, :head_size].reshape(block_count, BLOCK, items, head_size)
    offsets = pattern - (lax.axis_index("seq") * block_count - WIN)

    def slot_step(slot_index, state_pair):
        numerator, denominator = state_pair
        chosen = lax.dynamic_index_in_dim(offsets, slot_index, 1, keepdims=False)
        picked = jnp.take(key_table, chosen, axis=0)
        scores = (
            jnp.einsum(
                "bqnc,bknc->bnqk",
                queries,
                picked[..., :head_size],
                preferred_element_type=jnp.float32,
            )
            * scale_factor
        )
        alive = (slot_index < counts).astype(jnp.float32)
        weights = jnp.exp(scores) * alive[:, None, None, None]
        numerator = numerator + jnp.einsum(
            "bnqk,bknc->bnqc",
            weights.astype(jnp.bfloat16),
            picked[..., head_size:],
            preferred_element_type=jnp.float32,
        )
        return (numerator, denominator + jnp.sum(weights, axis=-1))

    start_state = (
        jnp.zeros((block_count, items, BLOCK, head_size), jnp.float32),
        jnp.zeros((block_count, items, BLOCK), jnp.float32),
    )
    numerator, denominator = lax.fori_loop(0, slot_total, slot_step, start_state)
    outcome = (numerator / denominator[..., None]).astype(jnp.bfloat16)
    outcome = outcome.transpose(0, 2, 1, 3).reshape(position_span, frame_total, items, head_size)
    temporal_out = lax.all_to_all(outcome, "seq", split_axis=1, concat_axis=0, tiled=True)
    spatial = packed[..., 3 * head_size :]
    blocks_frame = positions // BLOCK
    scores = (
        jnp.einsum(
            "fpnc,fqnc->fnpq",
            spatial[..., :head_size],
            spatial[..., head_size : 2 * head_size],
            preferred_element_type=jnp.float32,
        )
        * scale_factor
    )
    keep = spatial_mask.astype(jnp.float32)[:, None, :, None, :, None]
    weights = (
        jnp.exp(scores).reshape(frames_local, pairs_local, blocks_frame, BLOCK, blocks_frame, BLOCK)
        * keep
    )
    weights = weights.reshape(frames_local, pairs_local, positions, positions)
    denominator = jnp.sum(weights, axis=-1)
    numerator = jnp.einsum(
        "fnpq,fqnc->fpnc",
        weights.astype(jnp.bfloat16),
        spatial[..., 2 * head_size :],
        preferred_element_type=jnp.float32,
    )
    spatial_out = (numerator / denominator.transpose(0, 2, 1)[..., None]).astype(jnp.bfloat16)
    attention = jnp.concatenate([temporal_out.transpose(1, 0, 2, 3), spatial_out], axis=-1)
    attention = attention.reshape(row_count, pairs_local * 2 * head_size)
    out_width = w_out.shape[1]
    blocks = lax.axis_size("head") * lax.axis_size("sub")
    gate_slice = lax.dynamic_slice_in_dim(
        modulation[2], lax.axis_index(("head", "sub")) * out_width, out_width, 0
    )
    return mix(attention, whole_out.reshape(blocks, -1, out_width), gate_slice[None, :])

def push(source, target, send_sem, recv_sem, axis, place):
    return pltpu.make_async_remote_copy(
        src_ref=source,
        dst_ref=target,
        send_sem=send_sem,
        recv_sem=recv_sem,
        device_id={axis: place},
        device_id_type=MESH,
    )


def seats(count):
    return (count // 2 - 1, count // 2)


def by_pair_kernel(
    sizes, chunks, pieces, o_chunks,
    tokens, modulation, w_own, o_own, pattern, counts, mask, update,
    held, raw, stage, passing, partial, hfull, wfull, tq, sq, o_all, lists, lists_all, table, own, slots,
    tok_sems, l_sems, w_sems, p_sems, z_sems, x_sems, c_sems, o_sems, keep_sems, sz_sems, sx_sems, sc_sems, own_sems,
):
    count, parts, heads, subs = sizes
    low, high = seats(count)
    me, group = lax.axis_index("seq"), lax.axis_index("groups")
    head, sub = lax.axis_index("head"), lax.axis_index("sub")
    other = low + high - me
    near = jnp.where(me == low, low - 1, high + 1)
    far = jnp.where(me == low, high + 1, low - 1)
    seated = jnp.logical_or(me == low, me == high)
    ended = jnp.logical_not(seated)
    outward = jnp.where(me == low, 1, 0)
    blocks = heads * subs
    quarter = held.shape[1]
    unit = quarter // chunks
    width = wfull.shape[2]
    half = w_own.shape[0] // parts
    piece = half // pieces
    block = unit * blocks

    barrier = pltpu.get_barrier_semaphore()
    others = 0
    for axis in ("seq", "groups", "head", "sub"):
        size = lax.axis_size(axis)
        for hop in range(1, size):
            partner = lax.rem(lax.axis_index(axis) + hop, size)
            pl.semaphore_signal(barrier, inc=1, device_id={axis: partner}, device_id_type=MESH)
            others += 1

    def rows_of(head_hop, sub_hop, chunk):
        owner = lax.rem(head + heads - head_hop, heads) * subs + lax.rem(sub + subs - sub_hop, subs)
        return pl.ds(pl.multiple_of((chunk * blocks + owner) * unit, unit), unit)

    def fetch(hop, chunk):
        return pltpu.make_async_copy(
            tokens.at[rows_of(hop, 0, chunk)], held.at[hop, pl.ds(chunk * unit, unit)],
            tok_sems.at[hop, chunk],
        )

    for chunk in range(chunks):
        fetch(0, chunk).start()
    raw_copy = pltpu.make_async_copy(w_own, raw, own_sems.at[0])
    raw_copy.start()
    o_copy = pltpu.make_async_copy(o_own, o_all.at[me], own_sems.at[1])
    o_copy.start()

    @pl.when(seated)
    def _():
        for hop in range(1, heads):
            for chunk in range(chunks):
                fetch(hop, chunk).start()

    lists[...] = jnp.zeros_like(lists)
    slots_of = pattern.shape[1]
    lists[0 : pattern.shape[0], 0:slots_of] = pattern[...]
    lists[8 : 8 + mask.shape[0], 0 : mask.shape[1]] = mask[...]
    lists[16:17, 0 : counts.shape[1]] = counts[...]
    gain = 1.0 + modulation[1:2, :]
    shift = modulation[0:1, :]

    def modulate_rows(hop, first, last):
        def some(i, carry):
            at = pl.ds(pl.multiple_of(i * 16, 16), 16)
            chunk = i // (unit // 16)
            owner = lax.rem(head + heads - hop, heads) * subs + sub
            start = (chunk * blocks + owner) * unit + lax.rem(i, unit // 16) * 16
            values = held[hop, at, :].astype(jnp.float32)
            centered = values - jnp.mean(values, axis=-1, keepdims=True)
            spread_of = jnp.mean(jnp.square(centered), axis=-1, keepdims=True)
            normed = centered * lax.rsqrt(spread_of + EPSILON)
            hfull[me, pl.ds(pl.multiple_of(start, 16), 16), :] = (normed * gain + shift).astype(hfull.dtype)
            return carry

        for chunk in range(first, last):
            fetch(hop, chunk).wait()
        lax.fori_loop(first * unit // 16, last * unit // 16, some, 0, unroll=2)

    modulate_rows(0, 0, 1)
    pl.semaphore_wait(barrier, others)

    def spot(frame, head_hop, sub_hop, chunk):
        return hfull.at[frame, rows_of(head_hop, sub_hop, chunk)]

    def z_push(frame, chunk, place):
        target = spot(frame, 0, 0, chunk)
        return push(target, target, z_sems.at[0, frame, chunk], z_sems.at[1, frame, chunk], "seq", place)

    def x_push(frame, chunk, hop):
        target = spot(frame, 0, 0, chunk)
        return push(
            target, target, x_sems.at[hop, 0, frame, chunk], x_sems.at[hop, 1, frame, chunk],
            "head", lax.rem(head + hop, heads),
        )

    def c_push(frame, chunk, hop, turn):
        target = spot(frame, hop, 0, chunk)
        return push(
            target, target, c_sems.at[hop, turn, 0, frame, chunk], c_sems.at[hop, turn, 1, frame, chunk],
            "sub", lax.rem(sub + turn, subs),
        )

    def l_push(seat):
        return push(lists, lists_all.at[me], l_sems.at[0, seat - low], l_sems.at[1, me], "seq", seat)

    def w_rows(part, step):
        return pl.ds(pl.multiple_of(part * half + step * piece, piece), piece)

    def w_along(seat, source, step):
        return push(
            stage.at[seat - low, pl.ds(step * piece, piece)], wfull.at[source, w_rows(group, step)],
            w_sems.at[0, 0, seat - low, step], w_sems.at[0, 1, source, step], "seq", seat,
        )

    def w_hand(step, place):
        return push(
            stage.at[jnp.where(me < low, high, low) - low, pl.ds(step * piece, piece)],
            passing.at[pl.ds(step * piece, piece)],
            p_sems.at[0, step], p_sems.at[1, step], "seq", place,
        )

    def w_pass(source, step):
        return push(
            passing.at[pl.ds(step * piece, piece)], wfull.at[source, w_rows(group, step)],
            w_sems.at[0, 0, me - low, step], w_sems.at[0, 1, source, step], "seq", other,
        )

    def w_across(source, step, turn):
        target = wfull.at[source, w_rows(group, step)]
        return push(
            target, target, w_sems.at[turn, 0, source, step], w_sems.at[turn, 1, source, step],
            "groups", lax.rem(group + turn, parts),
        )

    outs = LineGather(o_all, o_sems, o_chunks, count, parts)

    for seat in (low, high):
        @pl.when(me != seat)
        def _():
            l_push(seat).start()

    columns_of = own.shape[2]

    def item(hop, turn, seat, chunk):
        return out_spot(slots, hop, turn, seat, chunk, block, low, columns_of)

    def to_head(hop, seat, chunk, source=None):
        return push(
            item(0, 0, seat, chunk) if source is None else source, item(hop, 0, seat, chunk),
            sx_sems.at[hop, 0, seat - low, chunk], sx_sems.at[hop, 1, seat - low, chunk],
            "head", lax.rem(head + hop, heads),
        )

    def to_sub(hop, turn, seat, chunk, source=None):
        return push(
            item(hop, 0, seat, chunk) if source is None else source, item(hop, turn, seat, chunk),
            sc_sems.at[hop, turn, 0, seat - low, chunk], sc_sems.at[hop, turn, 1, seat - low, chunk],
            "sub", lax.rem(sub + turn, subs),
        )

    toward = jnp.where(me < low, low, high)

    def relay_out(step, pieces_of_it, outgoing):
        for way in (0, 1):
            @pl.when((outward == way) == outgoing)
            def _():
                outs.relay(step, way, pieces_of_it)

    o_first, o_last = tuple(range(o_chunks // 2)), tuple(range(o_chunks // 2, o_chunks))

    def z_out(first, last):
        @pl.when(seated)
        def _():
            for chunk in range(first, last):
                z_push(me, chunk, other).start()

        @pl.when(ended)
        def _():
            for chunk in range(first, last):
                z_push(me, chunk, toward).start()

    z_out(0, 1)
    raw_copy.wait()

    def unpack(i, carry):
        start = pl.multiple_of(i * 64, 64)
        both = raw[pl.ds(pl.multiple_of(group * half + start, 64), 64)]
        first, second = both[:, 0, :], both[:, 1, :]
        stage[0, pl.ds(start, 64), :] = first
        stage[1, pl.ds(start, 64), :] = second
        return carry

    lax.fori_loop(0, half // 64, unpack, 0)

    @pl.when(ended)
    def _():
        for step in range(pieces):
            w_hand(step, toward).start()

    @pl.when(seated)
    def _():
        for step in range(pieces):
            w_along(other, me, step).start()

    modulate_rows(0, 1, chunks)
    o_copy.wait()

    @pl.when(ended)
    def _():
        z_out(1, chunks)
        for step in range(pieces):
            w_along(toward, me, step).start()
        for way in (0, 1):
            outs.open_way(way)
        for way in (0, 1):
            outs.relay(1, way)

    @pl.when(seated)
    def _():
        for way in (0, 1):
            @pl.when(outward == way)
            def _():
                outs.open_way(way)

        keep = pltpu.make_async_copy(lists, lists_all.at[me], own_sems.at[2])
        keep.start()
        for chunk in range(chunks):
            for turn in range(1, subs):
                c_push(me, chunk, 0, turn).start()
        for hop in range(1, heads):
            modulate_rows(hop, 0, chunks)
            for chunk in range(chunks):
                for turn in range(1, subs):
                    c_push(me, chunk, hop, turn).start()

        def land(frame, chunk):
            z_push(frame, chunk, other).wait_recv()
            for hop in range(1, heads):
                x_push(frame, chunk, hop).start()
            for turn in range(1, subs):
                c_push(frame, chunk, 0, turn).start()

        def crossed(frame, chunk):
            for hop in range(1, heads):
                x_push(frame, chunk, hop).wait_recv()
                for turn in range(1, subs):
                    c_push(frame, chunk, hop, turn).start()

        def gathered(frame, chunk):
            for hop in range(heads):
                for turn in range(1, subs):
                    c_push(frame, chunk, hop, turn).wait_recv()

        def keep_pair(i, carry):
            at = pl.ds(pl.multiple_of(i * 64, 64), 64)
            both = raw[at]
            wfull[me, at, :] = jnp.where(me == low, both[:, 0, :], both[:, 1, :])
            return carry

        def w_land(source, step):
            w_along(me, source, step).wait_recv()
            for turn in range(1, parts):
                w_across(source, step, turn).start()

        span = unit
        scale = math.log2(math.e) / math.sqrt(own.shape[2] // 2)
        size = own.shape[2] // 2
        total_blocks = tq.shape[0]
        each = total_blocks // count
        window = 2 * WIN + 1

        depth = wfull.shape[1]

        def first_part(frame, slot):
            def some_rows(chunk, carry):
                rows = pl.ds(pl.multiple_of(chunk * block, block), block)
                partial[slot, rows, :] = jnp.dot(
                    hfull[frame, rows, low * depth : (high + 1) * depth],
                    wfull[low : high + 1].reshape(-1, width), preferred_element_type=jnp.float32,
                )
                return carry

            lax.fori_loop(0, chunks, some_rows, 0)

        def keep_qkv(frame, chunk, total):
            at = pl.ds(pl.multiple_of(frame * span, span), span)
            for i in range(blocks):
                tq[chunk * blocks + i, at, :] = total[i * span : (i + 1) * span, : 3 * size]
            sq[frame, pl.ds(pl.multiple_of(chunk * block, block), block), :] = total[:, 3 * size :]

        land(near, 0)
        land(other, 0)
        for step in range(pieces):
            w_hand(step, other).wait_recv()
            w_pass(near, step).start()
            w_land(other, step)
        for chunk in range(1, chunks):
            z_push(me, chunk, other).start()
        z_push(near, 0, other).start()
        crossed(near, 0)
        crossed(other, 0)
        lax.fori_loop(0, w_own.shape[0] // 64, keep_pair, 0)
        rest = max(pieces, chunks - 1)
        for i in range(rest):
            if i + 1 < chunks:
                land(near, i + 1)
                z_push(near, i + 1, other).start()
            if i < pieces:
                w_land(far, i)
        for way in (0, 1):
            @pl.when(outward != way)
            def _():
                outs.open_way(way)
        def crossed_w(source):
            for step in range(pieces):
                for turn in range(1, parts):
                    w_across(source, step, turn).wait_recv()

        def all_in(frame):
            for chunk in range(chunks):
                gathered(frame, chunk)

        crossed_w(other)
        all_in(me)
        first_part(me, 0)
        for source in (near, other, far):
            l_push_from(lists_all, lists, l_sems, source, low, me).wait_recv()
        keep.wait()
        to_table = pltpu.make_async_copy(lists_all, table, own_sems.at[3])
        to_table.start()
        for i in range(rest):
            if i + 1 < chunks:
                land(other, i + 1)
            if i < pieces:
                w_land(near, i)
            if i + 1 < chunks:
                crossed(near, i + 1)
            if i == rest - 1:
                all_in(near)
                first_part(near, 1)
        def project(frame, chunk):
            rows = pl.ds(pl.multiple_of(chunk * block, block), block)
            total = jnp.dot(
                hfull[frame, rows, :], wfull[...].reshape(-1, width), preferred_element_type=jnp.float32
            ).astype(tq.dtype)
            keep_qkv(frame, chunk, total)

        def add_part(frame, slot, source):
            at = pl.ds(pl.multiple_of(source * depth, depth), depth)

            def some_rows(chunk, carry):
                rows = pl.ds(pl.multiple_of(chunk * block, block), block)
                partial[slot, rows, :] += jnp.dot(
                    hfull[frame, rows, at], wfull[source], preferred_element_type=jnp.float32
                )
                return carry

            lax.fori_loop(0, chunks, some_rows, 0)

        def project_frame(frame, slot):
            at = pl.ds(pl.multiple_of(near * depth, depth), depth)

            def last_part(chunk, carry):
                rows = pl.ds(pl.multiple_of(chunk * block, block), block)
                total = partial[slot, rows, :] + jnp.dot(
                    hfull[frame, rows, at], wfull[near], preferred_element_type=jnp.float32
                )
                keep_qkv(frame, chunk, total.astype(tq.dtype))
                return carry

            lax.fori_loop(0, chunks, last_part, 0)

        def soft(q, keys, values, biases):
            scores = lax.dot_general(
                q, keys, (((1,), (1,)), ((), ())), preferred_element_type=jnp.float32
            )
            parts_of = []
            sums = None
            for i, bias in enumerate(biases):
                weight = jnp.exp2(scores[:, i * BLOCK : (i + 1) * BLOCK] * scale + bias)
                sums = weight if sums is None else sums + weight
                parts_of.append(weight.astype(jnp.bfloat16))
            numerator = jnp.dot(
                jnp.concatenate(parts_of, axis=1), values, preferred_element_type=jnp.float32
            )
            return (numerator / jnp.sum(sums, axis=-1, keepdims=True)).astype(own.dtype)

        def temporal(chunk):
            def query(i, carry):
                b = chunk * blocks + i
                device, row = b // each, lax.rem(b, each)
                start = jnp.clip(b - WIN, 0, total_blocks - window)
                used = table[device, 16, row]
                biases = []
                for w in range(window):
                    times = 0
                    for j in range(slots_of):
                        hit = jnp.logical_and(j < used, table[device, row, j] == start + w)
                        times = times + jnp.where(hit, 1, 0)
                    bias = jnp.float32(-jnp.inf)
                    for m in range(1, slots_of + 1):
                        bias = jnp.where(times == m, jnp.float32(math.log2(m)), bias)
                    biases.append(bias)
                near_by = pl.ds(start, window)
                result = soft(
                    tq[b, :, :size],
                    tq[near_by, :, size : 2 * size].reshape(-1, size),
                    tq[near_by, :, 2 * size :].reshape(-1, size),
                    biases,
                )
                at = pl.ds(pl.multiple_of(b * span, span), span)
                for f in range(count):
                    own[f, at, :size] = result[f * span : (f + 1) * span]
                return carry

            lax.fori_loop(0, blocks, query, 0)

        def spatial(frame):
            per = sq.shape[1] // BLOCK

            def query(i, carry):
                at = pl.ds(pl.multiple_of(i * BLOCK, BLOCK), BLOCK)
                biases = [
                    jnp.where(table[frame, 8 + i, j] > 0, jnp.float32(0), jnp.float32(-jnp.inf))
                    for j in range(per)
                ]
                own[frame, at, size:] = soft(
                    sq[frame, at, :size], sq[frame, :, size : 2 * size], sq[frame, :, 2 * size :], biases
                )
                return carry

            lax.fori_loop(0, per, query, 0)

        def send(frame, chunk):
            out_push(own, slots, sz_sems, me, frame, chunk, block, low).start()

        def settle(chunk):
            send(near, chunk)
            send(other, chunk)
            keep_out(own, slots, keep_sems, me, chunk, block, low).start()
            mine = own.at[me, pl.ds(chunk * block, block)]
            for hop in range(1, heads):
                to_head(hop, me, chunk, mine).start()
            for turn in range(1, subs):
                to_sub(0, turn, me, chunk, mine).start()

        def far_project(chunk):
            gathered(far, chunk)
            project(far, chunk)

        crossed(other, 1)
        land(far, 0)
        crossed_w(far)
        add_part(me, 0, far)
        crossed(other, 2)
        add_part(near, 1, far)
        crossed(other, 3)
        land(far, 1)
        all_in(other)
        first_part(other, 2)
        add_part(other, 2, far)
        crossed_w(near)
        to_table.wait()
        project_frame(me, 0)
        land(far, 2)
        crossed(far, 0)
        project_frame(near, 1)
        project_frame(other, 2)
        relay_out(1, None, False)
        land(far, 3)
        crossed(far, 1)
        far_project(0)
        far_project(1)
        spatial(me)
        relay_out(1, (0,), True)
        spatial(near)
        spatial(other)
        temporal(0)
        settle(0)
        crossed(far, 2)
        relay_out(1, (1,), True)
        far_project(2)
        temporal(1)
        settle(1)
        relay_out(1, (2,), True)
        crossed(far, 3)
        relay_out(1, (3,), True)
        far_project(3)
        spatial(far)
        send(far, 0)
        send(far, 1)
        relay_out(2, (0,), True)
        temporal(2)
        settle(2)
        send(far, 2)
        relay_out(2, (1,), True)
        temporal(3)
        settle(3)
        send(far, 3)
        relay_out(2, (2, 3), True)

    def arrive(chunk, seat):
        out_push(own, slots, sz_sems, seat, me, chunk, block, low).wait_recv()
        for hop in range(1, heads):
            to_head(hop, seat, chunk).start()
        for turn in range(1, subs):
            to_sub(0, turn, seat, chunk).start()

    def pass_on(chunk, seat):
        for hop in range(1, heads):
            to_head(hop, seat, chunk).wait_recv()
            for turn in range(1, subs):
                to_sub(hop, turn, seat, chunk).start()

    columns = pl.ds(pl.multiple_of((head * subs + sub) * update.shape[1], 128), update.shape[1])
    gate = modulation[2:3, columns]

    def product(shard, chunk):
        hop = lax.rem(head + heads - shard // subs, heads)
        turn = lax.rem(sub + subs - lax.rem(shard, subs), subs)
        rows = pl.ds(pl.multiple_of(chunk * block, block), block)
        return rows, jnp.dot(slots[hop, turn, rows, :], o_all[shard], preferred_element_type=jnp.float32)

    def gather_up(shards):
        def some_rows(chunk, carry):
            total = None
            for shard in shards:
                rows, term = product(shard, chunk)
                total = term if total is None else total + term
            partial[0, rows, :] = total
            return carry

        lax.fori_loop(0, chunks, some_rows, 0)

    def finish(shard):
        def some_rows(chunk, carry):
            rows, term = product(shard, chunk)
            update[rows, :] = (gate * (partial[0, rows, :] + term)).astype(update.dtype)
            return carry

        lax.fori_loop(0, chunks, some_rows, 0)

    nearer = jnp.where(seated, me, toward)
    farther = low + high - nearer
    def relay_end(step, pieces_of_it):
        for way in (0, 1):
            outs.relay(step, way, pieces_of_it)

    @pl.when(ended)
    def _():
        relay_end(2, o_first)
        for chunk in range(chunks):
            arrive(chunk, nearer)
            if chunk == chunks // 2 - 1:
                relay_end(2, o_last)
                relay_end(3, o_first)

    for chunk in range(chunks):
        arrive(chunk, farther)
        if chunk % 2:
            @pl.when(ended)
            def _():
                relay_end(3, o_last[chunk // 2 :: chunks // 2])

    for chunk in range(chunks):
        pass_on(chunk, nearer)

    @pl.when(seated)
    def _():
        for chunk in range(chunks):
            keep_out(own, slots, keep_sems, me, chunk, block, low).wait()

    for chunk in range(chunks):
        pass_on(chunk, farther)
    last = jnp.where(ended, count - 1 - me, far)
    middle = (jnp.where(ended, toward, near), jnp.where(ended, low + high - toward, other))
    for shard in middle:
        outs.complete(shard)
    for chunk in range(chunks):
        for seat in (nearer, farther):
            for hop in range(heads):
                for turn in range(1, subs):
                    to_sub(hop, turn, seat, chunk).wait_recv()
    gather_up((me,) + middle)
    outs.complete(last)
    finish(last)

    for seat in (low, high):
        @pl.when(me != seat)
        def _():
            l_push(seat).wait_send()

    @pl.when(ended)
    def _():
        for step in range(pieces):
            w_hand(step, toward).wait_send()
            w_along(toward, me, step).wait_send()
        for chunk in range(chunks):
            z_push(me, chunk, jnp.where(me < low, low, high)).wait_send()

    @pl.when(seated)
    def _():
        for step in range(pieces):
            w_along(other, me, step).wait_send()
            w_pass(near, step).wait_send()
        for chunk in range(chunks):
            z_push(me, chunk, other).wait_send()
            z_push(near, chunk, other).wait_send()
            for frame in (me, near, other, far):
                for hop in range(heads):
                    for turn in range(1, subs):
                        c_push(frame, chunk, hop, turn).wait_send()
            for frame in (near, other, far):
                for hop in range(1, heads):
                    x_push(frame, chunk, hop).wait_send()
                out_push(own, slots, sz_sems, me, frame, chunk, block, low).wait_send()
        for source in (near, other, far):
            for step in range(pieces):
                for turn in range(1, parts):
                    w_across(source, step, turn).wait_send()

    for way in (0, 1):
        outs.close_way(way)
    for step in range(1, count):
        for way in (0, 1):
            outs.close_sends(step, way)
    for chunk in range(chunks):
        for seat in (low, high):
            for hop in range(1, heads):
                to_head(hop, seat, chunk).wait_send()
            for hop in range(heads):
                for turn in range(1, subs):
                    to_sub(hop, turn, seat, chunk).wait_send()


def l_push_from(lists_all, lists, l_sems, source, low, me):
    return push(lists, lists_all.at[source], l_sems.at[0, me - low], l_sems.at[1, source], "seq", me)


def out_spot(slots, hop, turn, seat, chunk, block, low, columns):
    at = (seat - low) * columns
    at = pl.ds(pl.multiple_of(at, columns), columns)
    return slots.at[hop, turn, pl.ds(chunk * block, block), at]


def out_push(own, slots, sems, seat, frame, chunk, block, low):
    return push(
        own.at[frame, pl.ds(chunk * block, block)],
        out_spot(slots, 0, 0, seat, chunk, block, low, own.shape[2]),
        sems.at[0, frame, chunk], sems.at[1, seat, chunk], "seq", frame,
    )


def keep_out(own, slots, sems, seat, chunk, block, low):
    return pltpu.make_async_copy(
        own.at[seat, pl.ds(chunk * block, block)],
        out_spot(slots, 0, 0, seat, chunk, block, low, own.shape[2]),
        sems.at[chunk],
    )


class LineGather:
    def __init__(self, slots, sems, chunks, count, parts):
        self.slots, self.chunks = slots, chunks
        self.sems, self.count, self.parts = sems, count, parts
        self.me = lax.axis_index("seq")
        self.group = lax.axis_index("groups")
        self.size = slots.shape[1] // (parts * chunks)

    def rows(self, group, chunk):
        start = (group * self.chunks + chunk) * self.size
        return pl.ds(pl.multiple_of(start, self.size), self.size)

    def along(self, shard, chunk, way):
        rows = self.rows(self.group, chunk)
        return push(
            self.slots.at[shard, rows], self.slots.at[shard, rows],
            self.sems.at[way, 0, shard, chunk], self.sems.at[way, 1, shard, chunk],
            "seq", self.me + (1 if way == 0 else -1),
        )

    def across(self, shard, chunk, hop):
        rows = self.rows(self.group, chunk)
        return push(
            self.slots.at[shard, rows], self.slots.at[shard, rows],
            self.sems.at[1 + hop, 0, shard, chunk], self.sems.at[1 + hop, 1, shard, chunk],
            "groups", lax.rem(self.group + hop, self.parts),
        )

    def onward(self, way):
        return self.me < self.count - 1 if way == 0 else self.me > 0

    def shard_of(self, step, way):
        return self.me - step if way == 0 else self.me + step

    def present(self, step, way):
        return self.me >= step if way == 0 else self.me + step < self.count

    def open_way(self, way, chunks=None):
        @pl.when(self.onward(way))
        def _():
            for chunk in range(self.chunks) if chunks is None else chunks:
                self.along(self.me, chunk, way).start()

    def relay(self, step, way, chunks=None):
        shard = self.shard_of(step, way)

        @pl.when(self.present(step, way))
        def _():
            for chunk in range(self.chunks) if chunks is None else chunks:
                self.along(shard, chunk, way).wait_recv()

                @pl.when(self.onward(way))
                def _():
                    self.along(shard, chunk, way).start()

                for hop in range(1, self.parts):
                    self.across(shard, chunk, hop).start()

    def complete(self, shard):
        for chunk in range(self.chunks):
            for hop in range(1, self.parts):
                self.across(shard, chunk, hop).wait_recv()

    def close_sends(self, step, way):
        shard = self.shard_of(step, way)

        @pl.when(self.present(step, way))
        def _():
            for chunk in range(self.chunks):
                @pl.when(self.onward(way))
                def _():
                    self.along(shard, chunk, way).wait_send()

                for hop in range(1, self.parts):
                    self.across(shard, chunk, hop).wait_send()

    def close_way(self, way):
        @pl.when(self.onward(way))
        def _():
            for chunk in range(self.chunks):
                self.along(self.me, chunk, way).wait_send()


def by_pair(tokens, modulation, w_own, o_own, pattern, counts, mask):
    sizes = tuple(lax.axis_size(axis) for axis in ("seq", "groups", "head", "sub"))
    count, parts, heads, subs = sizes
    rows, depth = tokens.shape
    width = w_own.shape[2]
    blocks = heads * subs
    quarter = rows // blocks
    chunks = rows // BLOCK
    pieces = 3
    o_chunks = 4
    columns = width // 3
    seated = len(seats(count))
    vmem = pl.BlockSpec(memory_space=pltpu.VMEM)
    whole = pl.BlockSpec(memory_space=pl.ANY)
    dma = pltpu.SemaphoreType.DMA
    kept = jnp.bfloat16
    return pl.pallas_call(
        functools.partial(by_pair_kernel, sizes, chunks, pieces, o_chunks),
        out_shape=jax.ShapeDtypeStruct((rows, o_own.shape[1]), kept),
        in_specs=[whole, vmem, whole, whole, vmem, vmem, vmem],
        out_specs=vmem,
        scratch_shapes=[
            pltpu.VMEM((heads, quarter, depth), kept),
            pltpu.VMEM(w_own.shape, kept),
            pltpu.VMEM((seated, w_own.shape[0] // parts, width), kept),
            pltpu.VMEM((w_own.shape[0] // parts, width), kept),
            pltpu.VMEM((count - 1, rows, width), jnp.float32),
            pltpu.VMEM((count, rows, depth), kept),
            pltpu.VMEM((count, w_own.shape[0], width), kept),
            pltpu.VMEM((count * rows // BLOCK, BLOCK, width // 2), kept),
            pltpu.VMEM((count, rows, width // 2), kept),
            pltpu.VMEM((count,) + o_own.shape, kept),
            pltpu.VMEM((24, 128), jnp.int32),
            pltpu.VMEM((count, 24, 128), jnp.int32),
            pltpu.SMEM((count, 24, 128), jnp.int32),
            pltpu.VMEM((count, rows, columns), kept),
            pltpu.VMEM((heads, subs, rows, seated * columns), kept),
            dma((heads, chunks)),
            dma((2, count)),
            dma((parts, 2, count, pieces)),
            dma((2, pieces)),
            dma((2, count, chunks)),
            dma((heads, 2, count, chunks)),
            dma((heads, subs, 2, count, chunks)),
            dma((1 + parts, 2, count, o_chunks)),
            dma((chunks,)),
            dma((2, count, chunks)),
            dma((heads, 2, seated, chunks)),
            dma((heads, subs, 2, seated, chunks)),
            dma((4,)),
        ],
        compiler_params=pltpu.CompilerParams(
            collective_id=2, has_side_effects=True, vmem_limit_bytes=60 * 1024 * 1024
        ),
        name="by_pair",
    )(tokens, modulation, w_own, o_own, pattern, counts, mask)


def shards_by_pair(tokens, modulation, w_qkv, w_out, pattern, counts, spatial_mask):
    return by_pair(tokens, modulation, w_qkv, w_out, pattern, counts[None, :], spatial_mask[0])


def one_pair_each(count, blocks, parts, tokens, w_qkv, w_out, pattern, spatial_mask):
    rows, frames = tokens.shape[0], spatial_mask.shape[0]
    return (
        count == blocks == 4
        and w_qkv.shape[1] == len(seats(count))
        and frames == 1
        and rows == BLOCK * pattern.shape[0] == BLOCK * spatial_mask.shape[1]
        and pattern.shape[0] == count
        and BLOCK % (16 * count) == 0
        and w_qkv.shape[0] % (192 * parts) == 0
        and w_out.shape[0] % (64 * parts) == 0
    )


def shards_any(*args):
    tokens, _, w_qkv, w_out, pattern, _, spatial_mask = args
    blocks = lax.axis_size("head") * lax.axis_size("sub")
    sizes = lax.axis_size("seq"), blocks, lax.axis_size("groups")
    if one_pair_each(*sizes, tokens, w_qkv, w_out, pattern, spatial_mask):
        return shards_by_pair(*args)
    return shards(*args)


def solution(mesh):
    return jax.shard_map(
        shards_any,
        mesh=mesh,
        in_specs=(
            P(("groups", "seq"), None),
            P(),
            P("seq", ("head", "sub"), None),
            P("seq", ("head", "sub")),
            P(("groups", "seq"), None),
            P(("groups", "seq")),
            P(("groups", "seq"), None, None),
        ),
        out_specs=P(("groups", "seq"), ("head", "sub")),
        check_vma=False,
    )
```

```python
import functools
import math

import jax
import jax.numpy as jnp
from jax import lax
from jax.experimental import pallas as pl
from jax.experimental.pallas import tpu as pltpu
from jax.sharding import PartitionSpec as P

BLOCK = 128
WIN = 2


EPSILON = 1e-06


def with_halo(cells, sides, width):
    for axis, dim in sides:
        count = lax.axis_size(axis)
        ends = count - 1
        head = lax.slice_in_dim(cells, 0, width, axis=dim)
        tail = lax.slice_in_dim(cells, cells.shape[dim] - width, cells.shape[dim], axis=dim)
        cells = jnp.concatenate(
            [
                lax.ppermute(tail, axis, [(i, (i + 1) % count) for i in range(ends)]),
                cells,
                lax.ppermute(head, axis, [((i + 1) % count, i) for i in range(ends)]),
            ],
            axis=dim,
        )
    return cells


MESH = pl.DeviceIdType.MESH


def pieces_of(rows, most=4):
    for count in range(most, 0, -1):
        if rows % (16 * count) == 0:
            return count
    return 1


class ShardLine:
    def __init__(self, own, slots, sems, chunks, count, parts):
        self.own, self.slots, self.chunks = own, slots, chunks
        self.sems, self.count, self.parts = sems, count, parts
        self.me = lax.axis_index("seq")
        self.group = lax.axis_index("groups")
        self.size = own.shape[0] // (parts * chunks)

    def rows(self, group, chunk):
        start = (group * self.chunks + chunk) * self.size
        return pl.ds(pl.multiple_of(start, self.size), self.size)

    def along(self, shard, chunk, way, own):
        rows = self.rows(self.group, chunk)
        source = self.own.at[rows] if own else self.slots.at[shard, rows]
        return pltpu.make_async_remote_copy(
            src_ref=source,
            dst_ref=self.slots.at[shard, rows],
            send_sem=self.sems.at[way, 0, shard, chunk],
            recv_sem=self.sems.at[way, 1, shard, chunk],
            device_id={"seq": self.me + (1 if way == 0 else -1)},
            device_id_type=MESH,
        )

    def across(self, shard, chunk, hop):
        rows = self.rows(self.group, chunk)
        return pltpu.make_async_remote_copy(
            src_ref=self.slots.at[shard, rows],
            dst_ref=self.slots.at[shard, rows],
            send_sem=self.sems.at[1 + hop, 0, shard, chunk],
            recv_sem=self.sems.at[1 + hop, 1, shard, chunk],
            device_id={"groups": lax.rem(self.group + hop, self.parts)},
            device_id_type=MESH,
        )

    def open_line(self):
        for chunk in range(self.chunks):
            for way in (0, 1):
                @pl.when(self.onward(way))
                def _():
                    self.along(self.me, chunk, way, True).start()

    def onward(self, way):
        return self.me < self.count - 1 if way == 0 else self.me > 0

    def shard_of(self, step, way):
        return self.me - step if way == 0 else self.me + step

    def present(self, step, way):
        return self.me >= step if way == 0 else self.me + step < self.count

    def relay(self, step):
        for chunk in range(self.chunks):
            for way in (0, 1):
                shard = self.shard_of(step, way)

                @pl.when(self.present(step, way))
                def _():
                    self.along(shard, chunk, way, False).wait_recv()

                    @pl.when(self.onward(way))
                    def _():
                        self.along(shard, chunk, way, False).start()

                    for hop in range(1, self.parts):
                        self.across(shard, chunk, hop).start()

    def complete(self, shard):
        for chunk in range(self.chunks):
            for hop in range(1, self.parts):
                self.across(shard, chunk, hop).wait_recv()

    def close_sends(self, step):
        for chunk in range(self.chunks):
            for way in (0, 1):
                shard = self.shard_of(step, way)

                @pl.when(self.present(step, way))
                def _():
                    @pl.when(self.onward(way))
                    def _():
                        self.along(shard, chunk, way, False).wait_send()

                    for hop in range(1, self.parts):
                        self.across(shard, chunk, hop).wait_send()

    def close_own(self):
        for chunk in range(self.chunks):
            for way in (0, 1):
                @pl.when(self.onward(way))
                def _():
                    self.along(self.me, chunk, way, True).wait_send()


def project_kernel(count, parts, q_chunks, o_chunks, hidden, w_own, o_own, qkv, o_all, slots, total, q_sems, o_sems, own_sem):
    me = lax.axis_index("seq")
    group = lax.axis_index("groups")
    barrier = pltpu.get_barrier_semaphore()

    @pl.when(me > 0)
    def _():
        pl.semaphore_signal(barrier, inc=1, device_id={"seq": me - 1}, device_id_type=MESH)

    @pl.when(me < count - 1)
    def _():
        pl.semaphore_signal(barrier, inc=1, device_id={"seq": me + 1}, device_id_type=MESH)

    for hop in range(1, parts):
        pl.semaphore_signal(
            barrier, inc=1, device_id={"groups": lax.rem(group + hop, parts)}, device_id_type=MESH
        )
    neighbours = jnp.where(me > 0, 1, 0) + jnp.where(me < count - 1, 1, 0) + (parts - 1)
    pl.semaphore_wait(barrier, neighbours)

    line = ShardLine(w_own, slots, q_sems, q_chunks, count, parts)
    outs = ShardLine(o_own, o_all, o_sems, o_chunks, count, parts)
    line.open_line()
    keep = pltpu.make_async_copy(o_own, o_all.at[me], own_sem)
    keep.start()
    tile = 256

    def add(shard, block, first):
        def column(j, carry):
            at = pl.ds(pl.multiple_of(j * tile, tile), tile)
            product = jnp.dot(hidden[shard], block[:, at], preferred_element_type=jnp.float32)
            total[:, at] = product if first else total[:, at] + product
            return carry

        lax.fori_loop(0, total.shape[1] // tile, column, 0)

    def finish(step):
        for way in (0, 1):
            shard = line.shard_of(step, way)

            @pl.when(line.present(step, way))
            def _():
                line.complete(shard)
                add(shard, slots.at[shard], False)

    add(me, w_own, True)

    def q_step(step, carry):
        line.relay(step)

        @pl.when(step > 1)
        def _():
            finish(step - 1)

        return carry

    lax.fori_loop(1, count, q_step, 0)
    outs.open_line()
    finish(count - 1)
    qkv[...] = total[...].astype(qkv.dtype)

    def o_step(step, carry):
        outs.relay(step)
        return carry

    lax.fori_loop(1, count, o_step, 0)

    def last(step, carry):
        line.close_sends(step)
        outs.close_sends(step)
        for way in (0, 1):
            shard = outs.shard_of(step, way)

            @pl.when(outs.present(step, way))
            def _():
                outs.complete(shard)

        return carry

    lax.fori_loop(1, count, last, 0)
    line.close_own()
    outs.close_own()
    keep.wait()


def project(hidden, w_own, o_own):
    count, parts = lax.axis_size("seq"), lax.axis_size("groups")
    rows, depth = hidden.shape
    hidden = hidden.reshape(rows, count, depth // count).transpose(1, 0, 2)
    width = w_own.shape[1]
    most = 4 if count <= 8 else 1
    q_chunks = pieces_of(w_own.shape[0] // parts, most)
    o_chunks = pieces_of(o_own.shape[0] // parts, most)
    vmem = pl.BlockSpec(memory_space=pltpu.VMEM)
    return pl.pallas_call(
        functools.partial(project_kernel, count, parts, q_chunks, o_chunks),
        out_shape=[
            jax.ShapeDtypeStruct((rows, width), jnp.bfloat16),
            jax.ShapeDtypeStruct((count,) + o_own.shape, jnp.bfloat16),
        ],
        in_specs=[vmem] * 3,
        out_specs=[vmem, pl.BlockSpec(memory_space=pl.ANY)],
        scratch_shapes=[
            pltpu.VMEM((count,) + w_own.shape, jnp.bfloat16),
            pltpu.VMEM((rows, width), jnp.float32),
            pltpu.SemaphoreType.DMA((1 + parts, 2, count, q_chunks)),
            pltpu.SemaphoreType.DMA((1 + parts, 2, count, o_chunks)),
            pltpu.SemaphoreType.DMA,
        ],
        compiler_params=pltpu.CompilerParams(
            collective_id=0, has_side_effects=True, vmem_limit_bytes=48 * 1024 * 1024
        ),
        name="project",
    )(hidden, w_own, o_own)


def mix_kernel(heads, subs, chunks, attn, w_all, gate, update, slots, total, x_sems, c_sems):
    head, sub = lax.axis_index("head"), lax.axis_index("sub")
    barrier = pltpu.get_barrier_semaphore()
    for hop in range(1, heads):
        pl.semaphore_signal(
            barrier, inc=1, device_id={"head": lax.rem(head + hop, heads)}, device_id_type=MESH
        )
    for hop in range(1, subs):
        pl.semaphore_signal(
            barrier, inc=1, device_id={"sub": lax.rem(sub + hop, subs)}, device_id_type=MESH
        )
    pl.semaphore_wait(barrier, heads + subs - 2)
    size = attn.shape[0] // chunks

    def to_head(hop, chunk):
        rows = pl.ds(chunk * size, size)
        return pltpu.make_async_remote_copy(
            src_ref=attn.at[rows],
            dst_ref=slots.at[hop, 0, rows],
            send_sem=x_sems.at[hop, 0, chunk],
            recv_sem=x_sems.at[hop, 1, chunk],
            device_id={"head": lax.rem(head + hop, heads)},
            device_id_type=MESH,
        )

    def to_sub(hop, turn, chunk):
        rows = pl.ds(chunk * size, size)
        return pltpu.make_async_remote_copy(
            src_ref=attn.at[rows] if hop == 0 else slots.at[hop, 0, rows],
            dst_ref=slots.at[hop, turn, rows],
            send_sem=c_sems.at[hop, turn, 0, chunk],
            recv_sem=c_sems.at[hop, turn, 1, chunk],
            device_id={"sub": lax.rem(sub + turn, subs)},
            device_id_type=MESH,
        )

    for chunk in range(chunks):
        for hop in range(1, heads):
            to_head(hop, chunk).start()
        for turn in range(1, subs):
            to_sub(0, turn, chunk).start()

    def add(chunk, hop, turn, first):
        rows = slice(chunk * size, (chunk + 1) * size)
        owner = lax.rem(head + heads - hop, heads) * subs + lax.rem(sub + subs - turn, subs)
        block = attn[rows, :] if hop == 0 and turn == 0 else slots[hop, turn, rows, :]
        product = jnp.dot(block, w_all[owner], preferred_element_type=jnp.float32)
        total[rows, :] = product if first else total[rows, :] + product

    for chunk in range(chunks):
        add(chunk, 0, 0, True)
    for chunk in range(chunks):
        for turn in range(1, subs):
            to_sub(0, turn, chunk).wait_recv()
            add(chunk, 0, turn, False)
    for chunk in range(chunks):
        for hop in range(1, heads):
            to_head(hop, chunk).wait_recv()
            for turn in range(1, subs):
                to_sub(hop, turn, chunk).start()
            add(chunk, hop, 0, False)
    for chunk in range(chunks):
        for hop in range(1, heads):
            for turn in range(1, subs):
                to_sub(hop, turn, chunk).wait_recv()
                add(chunk, hop, turn, False)
        rows = slice(chunk * size, (chunk + 1) * size)
        update[rows, :] = (gate[...] * total[rows, :]).astype(update.dtype)
    for chunk in range(chunks):
        for hop in range(1, heads):
            to_head(hop, chunk).wait_send()
        for hop in range(heads):
            for turn in range(1, subs):
                to_sub(hop, turn, chunk).wait_send()


def mix(attention, w_all, gate):
    heads, subs = lax.axis_size("head"), lax.axis_size("sub")
    rows, width = attention.shape
    chunks = pieces_of(rows, 2)
    vmem = pl.BlockSpec(memory_space=pltpu.VMEM)
    return pl.pallas_call(
        functools.partial(mix_kernel, heads, subs, chunks),
        out_shape=jax.ShapeDtypeStruct((rows, w_all.shape[-1]), jnp.bfloat16),
        in_specs=[vmem] * 3,
        out_specs=vmem,
        scratch_shapes=[
            pltpu.VMEM((heads, subs, rows, width), jnp.bfloat16),
            pltpu.VMEM((rows, w_all.shape[-1]), jnp.float32),
            pltpu.SemaphoreType.DMA((heads, 2, chunks)),
            pltpu.SemaphoreType.DMA((heads, subs, 2, chunks)),
        ],
        compiler_params=pltpu.CompilerParams(
            collective_id=1, has_side_effects=True, vmem_limit_bytes=40 * 1024 * 1024
        ),
        name="mix",
    )(attention, w_all, gate)


def modulate(tokens, modulation):
    values = tokens.astype(jnp.float32)
    center = jnp.mean(values, axis=-1, keepdims=True)
    spread = jnp.mean(jnp.square(values - center), axis=-1, keepdims=True)
    normed = (values - center) * lax.rsqrt(spread + EPSILON)
    return (normed * (1.0 + modulation[1]) + modulation[0]).astype(jnp.bfloat16)


def shards(tokens, modulation, w_qkv, w_out, pattern, counts, spatial_mask):
    row_count, feature_width = tokens.shape
    pairs_local = w_qkv.shape[1]
    head_size = w_qkv.shape[2] // 6
    frames_local = spatial_mask.shape[0]
    positions = row_count // frames_local
    slot_total = pattern.shape[1]
    scale_factor = 1.0 / math.sqrt(head_size)
    hidden = modulate(tokens, modulation)
    projected, whole_out = project(hidden, w_qkv.reshape(w_qkv.shape[0], -1), w_out)
    packed = projected.reshape(
        frames_local, positions, pairs_local, 6 * head_size
    )
    temporal_in = packed[..., : 3 * head_size].transpose(1, 0, 2, 3)
    received = lax.all_to_all(temporal_in, "seq", split_axis=0, concat_axis=1, tiled=True)
    position_span, frame_total, items, _ = received.shape
    relaid = received.reshape(position_span * frame_total, items, 3 * head_size)
    extended = with_halo(relaid[:, :, head_size:], (("seq", 0),), WIN * BLOCK)
    block_count = position_span * frame_total // BLOCK
    key_table = extended.reshape(block_count + 2 * WIN, BLOCK, items, 2 * head_size)
    queries = relaid[:, :, :head_size].reshape(block_count, BLOCK, items, head_size)
    offsets = pattern - (lax.axis_index("seq") * block_count - WIN)

    def slot_step(slot_index, state_pair):
        numerator, denominator = state_pair
        chosen = lax.dynamic_index_in_dim(offsets, slot_index, 1, keepdims=False)
        picked = jnp.take(key_table, chosen, axis=0)
        scores = (
            jnp.einsum(
                "bqnc,bknc->bnqk",
                queries,
                picked[..., :head_size],
                preferred_element_type=jnp.float32,
            )
            * scale_factor
        )
        alive = (slot_index < counts).astype(jnp.float32)
        weights = jnp.exp(scores) * alive[:, None, None, None]
        numerator = numerator + jnp.einsum(
            "bnqk,bknc->bnqc",
            weights.astype(jnp.bfloat16),
            picked[..., head_size:],
            preferred_element_type=jnp.float32,
        )
        return (numerator, denominator + jnp.sum(weights, axis=-1))

    start_state = (
        jnp.zeros((block_count, items, BLOCK, head_size), jnp.float32),
        jnp.zeros((block_count, items, BLOCK), jnp.float32),
    )
    numerator, denominator = lax.fori_loop(0, slot_total, slot_step, start_state)
    outcome = (numerator / denominator[..., None]).astype(jnp.bfloat16)
    outcome = outcome.transpose(0, 2, 1, 3).reshape(position_span, frame_total, items, head_size)
    temporal_out = lax.all_to_all(outcome, "seq", split_axis=1, concat_axis=0, tiled=True)
    spatial = packed[..., 3 * head_size :]
    blocks_frame = positions // BLOCK
    scores = (
        jnp.einsum(
            "fpnc,fqnc->fnpq",
            spatial[..., :head_size],
            spatial[..., head_size : 2 * head_size],
            preferred_element_type=jnp.float32,
        )
        * scale_factor
    )
    keep = spatial_mask.astype(jnp.float32)[:, None, :, None, :, None]
    weights = (
        jnp.exp(scores).reshape(frames_local, pairs_local, blocks_frame, BLOCK, blocks_frame, BLOCK)
        * keep
    )
    weights = weights.reshape(frames_local, pairs_local, positions, positions)
    denominator = jnp.sum(weights, axis=-1)
    numerator = jnp.einsum(
        "fnpq,fqnc->fpnc",
        weights.astype(jnp.bfloat16),
        spatial[..., 2 * head_size :],
        preferred_element_type=jnp.float32,
    )
    spatial_out = (numerator / denominator.transpose(0, 2, 1)[..., None]).astype(jnp.bfloat16)
    attention = jnp.concatenate([temporal_out.transpose(1, 0, 2, 3), spatial_out], axis=-1)
    attention = attention.reshape(row_count, pairs_local * 2 * head_size)
    out_width = w_out.shape[1]
    blocks = lax.axis_size("head") * lax.axis_size("sub")
    gate_slice = lax.dynamic_slice_in_dim(
        modulation[2], lax.axis_index(("head", "sub")) * out_width, out_width, 0
    )
    return mix(attention, whole_out.reshape(blocks, -1, out_width), gate_slice[None, :])

def push(source, target, send_sem, recv_sem, axis, place):
    return pltpu.make_async_remote_copy(
        src_ref=source,
        dst_ref=target,
        send_sem=send_sem,
        recv_sem=recv_sem,
        device_id={axis: place},
        device_id_type=MESH,
    )


def seats(count):
    return (count // 2 - 1, count // 2)


def by_pair_kernel(
    sizes, chunks, pieces, o_chunks,
    tokens, modulation, w_own, o_own, pattern, counts, mask, update,
    held, raw, stage, passing, partial, hfull, wfull, tq, sq, o_all, lists, lists_all, table, own, slots, result,
    tok_sems, l_sems, w_sems, wa_sems, p_sems, z_sems, x_sems, c_sems, o_sems, oa_sems,
    sz_sems, sx_sems, sc_sems, own_sems, sent,
):
    count, parts, heads, subs = sizes
    low, high = seats(count)
    me, group = lax.axis_index("seq"), lax.axis_index("groups")
    head, sub = lax.axis_index("head"), lax.axis_index("sub")
    other = low + high - me
    near = jnp.where(me == low, low - 1, high + 1)
    far = jnp.where(me == low, high + 1, low - 1)
    seated = jnp.logical_or(me == low, me == high)
    ended = jnp.logical_not(seated)
    outward = jnp.where(me == low, 1, 0)
    blocks = heads * subs
    quarter = held.shape[1]
    unit = quarter // chunks
    width = wfull.shape[2]
    half = w_own.shape[0] // parts
    piece = half // pieces
    block = unit * blocks

    barrier = pltpu.get_barrier_semaphore()
    others = 0
    for axis in ("seq", "groups", "head", "sub"):
        size = lax.axis_size(axis)
        for hop in range(1, size):
            partner = lax.rem(lax.axis_index(axis) + hop, size)
            pl.semaphore_signal(barrier, inc=1, device_id={axis: partner}, device_id_type=MESH)
            others += 1

    def rows_of(head_hop, sub_hop, chunk):
        owner = lax.rem(head + heads - head_hop, heads) * subs + lax.rem(sub + subs - sub_hop, subs)
        return pl.ds(pl.multiple_of((chunk * blocks + owner) * unit, unit), unit)

    def fetch(hop, chunk):
        return pltpu.make_async_copy(
            tokens.at[rows_of(hop, 0, chunk)], held.at[hop, pl.ds(chunk * unit, unit)],
            tok_sems.at[hop, min(chunk, 1) if hop == 0 else 0],
        )

    def fetched(hop, first, last):
        pltpu.make_async_copy(
            tokens.at[pl.ds(first * unit, (last - first) * unit)],
            held.at[hop, pl.ds(first * unit, (last - first) * unit)],
            tok_sems.at[hop, min(first, 1) if hop == 0 else 0],
        ).wait()

    def taken(region, sem):
        push(region, region, sem, sem, "seq", me).wait_recv()

    for chunk in range(chunks):
        fetch(0, chunk).start()
    raw_copy = pltpu.make_async_copy(w_own, raw, own_sems.at[0])
    raw_copy.start()
    o_copy = pltpu.make_async_copy(o_own, o_all.at[me], own_sems.at[1])
    o_copy.start()

    @pl.when(seated)
    def _():
        for hop in range(1, heads):
            for chunk in range(chunks):
                fetch(hop, chunk).start()

    lists[...] = jnp.zeros_like(lists)
    slots_of = pattern.shape[1]
    lists[0 : pattern.shape[0], 0:slots_of] = pattern[...]
    lists[8 : 8 + mask.shape[0], 0 : mask.shape[1]] = mask[...]
    lists[16:17, 0 : counts.shape[1]] = counts[...]
    gain = 1.0 + modulation[1:2, :]
    shift = modulation[0:1, :]

    def modulate_rows(hop, first, last):
        def some(i, carry):
            at = pl.ds(pl.multiple_of(i * 16, 16), 16)
            chunk = i // (unit // 16)
            owner = lax.rem(head + heads - hop, heads) * subs + sub
            start = (chunk * blocks + owner) * unit + lax.rem(i, unit // 16) * 16
            values = held[hop, at, :].astype(jnp.float32)
            centered = values - jnp.mean(values, axis=-1, keepdims=True)
            spread_of = jnp.mean(jnp.square(centered), axis=-1, keepdims=True)
            normed = centered * lax.rsqrt(spread_of + EPSILON)
            hfull[me, pl.ds(pl.multiple_of(start, 16), 16), :] = (normed * gain + shift).astype(hfull.dtype)
            return carry

        fetched(hop, first, last)
        lax.fori_loop(first * unit // 16, last * unit // 16, some, 0, unroll=2)

    modulate_rows(0, 0, 1)
    pl.semaphore_wait(barrier, others)

    def spot(frame, head_hop, sub_hop, chunk):
        return hfull.at[frame, rows_of(head_hop, sub_hop, chunk)]

    def z_push(frame, chunk, place):
        target = spot(frame, 0, 0, chunk)
        return push(target, target, sent.at[1], z_sems.at[frame, chunk], "seq", place)

    def x_push(frame, chunk, hop):
        target = spot(frame, 0, 0, chunk)
        return push(
            target, target, sent.at[2], x_sems.at[frame, chunk],
            "head", lax.rem(head + hop, heads),
        )

    def c_push(frame, chunk, hop, turn):
        target = spot(frame, hop, 0, chunk)
        return push(
            target, target, sent.at[3], c_sems.at[frame, chunk],
            "sub", lax.rem(sub + turn, subs),
        )

    def l_push(seat):
        return push(lists, lists_all.at[me], sent.at[9], l_sems.at[me], "seq", seat)

    def w_rows(part, step):
        return pl.ds(pl.multiple_of(part * half + step * piece, piece), piece)

    def w_along(seat, source, step):
        return push(
            stage.at[seat - low, pl.ds(step * piece, piece)], wfull.at[source, w_rows(group, step)],
            sent.at[0], w_sems.at[source, step], "seq", seat,
        )

    def w_hand(step, place):
        return push(
            stage.at[jnp.where(me < low, high, low) - low, pl.ds(step * piece, piece)],
            passing.at[pl.ds(step * piece, piece)],
            sent.at[0], p_sems.at[step], "seq", place,
        )

    def w_pass(source, step):
        return push(
            passing.at[pl.ds(step * piece, piece)], wfull.at[source, w_rows(group, step)],
            sent.at[0], w_sems.at[source, step], "seq", other,
        )

    def w_across(source, step, turn):
        target = wfull.at[source, w_rows(group, step)]
        return push(
            target, target, sent.at[4], wa_sems.at[source],
            "groups", lax.rem(group + turn, parts),
        )

    outs = LineGather(o_all, o_sems, oa_sems, sent, o_chunks, count, parts)

    for seat in (low, high):
        @pl.when(me != seat)
        def _():
            l_push(seat).start()

    columns_of = own.shape[2]

    def item(hop, turn, seat, chunk):
        return out_spot(slots, hop, turn, seat, chunk, block, low, columns_of)

    def to_head(hop, seat, chunk, source=None):
        return push(
            item(0, 0, seat, chunk) if source is None else source, item(hop, 0, seat, chunk),
            sent.at[7], sx_sems.at[seat - low, chunk],
            "head", lax.rem(head + hop, heads),
        )

    def to_sub(hop, turn, seat, chunk, source=None):
        return push(
            item(hop, 0, seat, chunk) if source is None else source, item(hop, turn, seat, chunk),
            sent.at[8], sc_sems.at[chunk],
            "sub", lax.rem(sub + turn, subs),
        )

    toward = jnp.where(me < low, low, high)

    def relay_out(step, pieces_of_it, outgoing):
        for way in (0, 1):
            @pl.when((outward == way) == outgoing)
            def _():
                outs.relay(step, way, pieces_of_it)

    o_first, o_last = tuple(range(o_chunks // 2)), tuple(range(o_chunks // 2, o_chunks))

    def z_out(first, last):
        @pl.when(seated)
        def _():
            for chunk in range(first, last):
                z_push(me, chunk, other).start()

        @pl.when(ended)
        def _():
            for chunk in range(first, last):
                z_push(me, chunk, toward).start()

    z_out(0, 1)
    raw_copy.wait()

    def unpack(i, carry):
        start = pl.multiple_of(i * 64, 64)
        both = raw[pl.ds(pl.multiple_of(group * half + start, 64), 64)]
        first, second = both[:, 0, :], both[:, 1, :]
        stage[0, pl.ds(start, 64), :] = first
        stage[1, pl.ds(start, 64), :] = second
        return carry

    lax.fori_loop(0, half // 64, unpack, 0)

    @pl.when(ended)
    def _():
        for step in range(pieces):
            w_hand(step, toward).start()

    @pl.when(seated)
    def _():
        for step in range(pieces):
            w_along(other, me, step).start()

    modulate_rows(0, 1, chunks)
    o_copy.wait()

    @pl.when(ended)
    def _():
        z_out(1, chunks)
        for step in range(pieces):
            w_along(toward, me, step).start()
        for way in (0, 1):
            outs.open_way(way)
        for way in (0, 1):
            outs.relay(1, way)

    @pl.when(seated)
    def _():
        for way in (0, 1):
            @pl.when(outward == way)
            def _():
                outs.open_way(way)

        keep = pltpu.make_async_copy(lists, lists_all.at[me], own_sems.at[2])
        keep.start()
        for chunk in range(chunks):
            for turn in range(1, subs):
                c_push(me, chunk, 0, turn).start()
        for hop in range(1, heads):
            modulate_rows(hop, 0, chunks)
            for chunk in range(chunks):
                for turn in range(1, subs):
                    c_push(me, chunk, hop, turn).start()

        def land(frame, chunk):
            z_push(frame, chunk, other).wait_recv()
            for hop in range(1, heads):
                x_push(frame, chunk, hop).start()
            for turn in range(1, subs):
                c_push(frame, chunk, 0, turn).start()

        def crossed(frame, chunk):
            for hop in range(1, heads):
                x_push(frame, chunk, hop).wait_recv()
                for turn in range(1, subs):
                    c_push(frame, chunk, hop, turn).start()

        def gathered(frame, chunk):
            taken(hfull.at[frame, pl.ds(0, heads * (subs - 1) * unit)], c_sems.at[frame, chunk])

        def keep_pair(i, carry):
            at = pl.ds(pl.multiple_of(i * 64, 64), 64)
            both = raw[at]
            wfull[me, at, :] = jnp.where(me == low, both[:, 0, :], both[:, 1, :])
            return carry

        def w_land(source, step):
            w_along(me, source, step).wait_recv()
            for turn in range(1, parts):
                w_across(source, step, turn).start()

        span = unit
        scale = math.log2(math.e) / math.sqrt(own.shape[2] // 2)
        size = own.shape[2] // 2
        total_blocks = tq.shape[0]
        each = total_blocks // count
        window = 2 * WIN + 1

        depth = wfull.shape[1]

        def first_part(frame, slot):
            def some_rows(chunk, carry):
                rows = pl.ds(pl.multiple_of(chunk * block, block), block)
                partial[slot, rows, :] = jnp.dot(
                    hfull[frame, rows, low * depth : (high + 1) * depth],
                    wfull[low : high + 1].reshape(-1, width), preferred_element_type=jnp.float32,
                )
                return carry

            lax.fori_loop(0, chunks, some_rows, 0, unroll=2)

        def keep_qkv(frame, chunk, total):
            at = pl.ds(pl.multiple_of(frame * span, span), span)
            for i in range(blocks):
                tq[chunk * blocks + i, at, :] = total[i * span : (i + 1) * span, : 3 * size]
            sq[frame, pl.ds(pl.multiple_of(chunk * block, block), block), :] = total[:, 3 * size :]

        land(near, 0)
        land(other, 0)
        for step in range(pieces):
            w_hand(step, other).wait_recv()
            w_pass(near, step).start()
            w_land(other, step)
        for chunk in range(1, chunks):
            z_push(me, chunk, other).start()
        z_push(near, 0, other).start()
        crossed(near, 0)
        crossed(other, 0)
        lax.fori_loop(0, w_own.shape[0] // 64, keep_pair, 0)
        rest = max(pieces, chunks - 1)
        for i in range(rest):
            if i + 1 < chunks:
                land(near, i + 1)
                z_push(near, i + 1, other).start()
            if i < pieces:
                w_land(far, i)
        for way in (0, 1):
            @pl.when(outward != way)
            def _():
                outs.open_way(way)
        def crossed_w(source):
            taken(wfull.at[source, pl.ds(0, (parts - 1) * half)], wa_sems.at[source])

        def all_in(frame):
            for chunk in range(chunks):
                gathered(frame, chunk)

        crossed_w(other)
        all_in(me)
        first_part(me, 0)
        for source in (near, other, far):
            taken(lists, l_sems.at[source])
        keep.wait()
        to_table = pltpu.make_async_copy(lists_all, table, own_sems.at[3])
        to_table.start()
        for i in range(rest):
            if i + 1 < chunks:
                land(other, i + 1)
            if i < pieces:
                w_land(near, i)
            if i + 1 < chunks:
                crossed(near, i + 1)
            if i == rest - 1:
                all_in(near)
                first_part(near, 1)
        def project(frame, chunk):
            rows = pl.ds(pl.multiple_of(chunk * block, block), block)
            total = jnp.dot(
                hfull[frame, rows, :], wfull[...].reshape(-1, width), preferred_element_type=jnp.float32
            ).astype(tq.dtype)
            keep_qkv(frame, chunk, total)

        def add_part(frame, slot, source):
            at = pl.ds(pl.multiple_of(source * depth, depth), depth)

            def some_rows(chunk, carry):
                rows = pl.ds(pl.multiple_of(chunk * block, block), block)
                partial[slot, rows, :] += jnp.dot(
                    hfull[frame, rows, at], wfull[source], preferred_element_type=jnp.float32
                )
                return carry

            lax.fori_loop(0, chunks, some_rows, 0, unroll=2)

        def project_frame(frame, slot):
            at = pl.ds(pl.multiple_of(near * depth, depth), depth)

            def last_part(chunk, carry):
                rows = pl.ds(pl.multiple_of(chunk * block, block), block)
                total = partial[slot, rows, :] + jnp.dot(
                    hfull[frame, rows, at], wfull[near], preferred_element_type=jnp.float32
                )
                keep_qkv(frame, chunk, total.astype(tq.dtype))
                return carry

            lax.fori_loop(0, chunks, last_part, 0, unroll=2)

        def soft(q, keys, values, biases):
            scores = lax.dot_general(
                q, keys, (((1,), (1,)), ((), ())), preferred_element_type=jnp.float32
            )
            parts_of = []
            sums = None
            for i, bias in enumerate(biases):
                weight = jnp.exp2(scores[:, i * BLOCK : (i + 1) * BLOCK] * scale + bias)
                sums = weight if sums is None else sums + weight
                parts_of.append(weight.astype(jnp.bfloat16))
            numerator = jnp.dot(
                jnp.concatenate(parts_of, axis=1), values, preferred_element_type=jnp.float32
            )
            return (numerator / jnp.sum(sums, axis=-1, keepdims=True)).astype(own.dtype)

        def temporal(chunk):
            def query(i, carry):
                b = chunk * blocks + i
                device, row = b // each, lax.rem(b, each)
                start = jnp.clip(b - WIN, 0, total_blocks - window)
                used = table[device, 16, row]
                biases = []
                for w in range(window):
                    times = 0
                    for j in range(slots_of):
                        hit = jnp.logical_and(j < used, table[device, row, j] == start + w)
                        times = times + jnp.where(hit, 1, 0)
                    bias = jnp.float32(-jnp.inf)
                    for m in range(1, slots_of + 1):
                        bias = jnp.where(times == m, jnp.float32(math.log2(m)), bias)
                    biases.append(bias)
                near_by = pl.ds(start, window)
                result = soft(
                    tq[b, :, :size],
                    tq[near_by, :, size : 2 * size].reshape(-1, size),
                    tq[near_by, :, 2 * size :].reshape(-1, size),
                    biases,
                )
                at = pl.ds(pl.multiple_of(b * span, span), span)
                for f in range(count):
                    own[f, at, :size] = result[f * span : (f + 1) * span]
                return carry

            lax.fori_loop(0, blocks, query, 0, unroll=True)

        def spatial(frame):
            per = sq.shape[1] // BLOCK

            def query(i, carry):
                at = pl.ds(pl.multiple_of(i * BLOCK, BLOCK), BLOCK)
                biases = [
                    jnp.where(table[frame, 8 + i, j] > 0, jnp.float32(0), jnp.float32(-jnp.inf))
                    for j in range(per)
                ]
                own[frame, at, size:] = soft(
                    sq[frame, at, :size], sq[frame, :, size : 2 * size], sq[frame, :, 2 * size :], biases
                )
                return carry

            lax.fori_loop(0, per, query, 0, unroll=True)

        def send(frame, chunk):
            out_push(own, slots, sz_sems, sent, me, frame, chunk, block, low).start()

        def settle(chunk):
            send(near, chunk)
            send(other, chunk)
            keep_out(own, slots, own_sems.at[4], me, chunk, block, low).start()
            mine = own.at[me, pl.ds(chunk * block, block)]
            for hop in range(1, heads):
                to_head(hop, me, chunk, mine).start()
            for turn in range(1, subs):
                to_sub(0, turn, me, chunk, mine).start()

        def far_project(chunk):
            gathered(far, chunk)
            project(far, chunk)

        crossed(other, 1)
        land(far, 0)
        crossed_w(far)
        add_part(me, 0, far)
        crossed(other, 2)
        add_part(near, 1, far)
        crossed(other, 3)
        land(far, 1)
        all_in(other)
        first_part(other, 2)
        add_part(other, 2, far)
        crossed_w(near)
        to_table.wait()
        project_frame(me, 0)
        land(far, 2)
        crossed(far, 0)
        project_frame(near, 1)
        project_frame(other, 2)
        relay_out(1, None, False)
        land(far, 3)
        crossed(far, 1)
        far_project(0)
        far_project(1)
        spatial(me)
        relay_out(1, (0,), True)
        spatial(near)
        spatial(other)
        temporal(0)
        settle(0)
        crossed(far, 2)
        relay_out(1, (1,), True)
        far_project(2)
        temporal(1)
        settle(1)
        relay_out(1, (2,), True)
        crossed(far, 3)
        relay_out(1, (3,), True)
        far_project(3)
        spatial(far)
        send(far, 0)
        send(far, 1)
        relay_out(2, (0,), True)
        temporal(2)
        settle(2)
        send(far, 2)
        relay_out(2, (1,), True)
        temporal(3)
        settle(3)
        send(far, 3)
        relay_out(2, (2, 3), True)

    def arrive(chunk, seat):
        out_push(own, slots, sz_sems, sent, seat, me, chunk, block, low).wait_recv()
        for hop in range(1, heads):
            to_head(hop, seat, chunk).start()
        for turn in range(1, subs):
            to_sub(0, turn, seat, chunk).start()

    def pass_on(chunk, seat):
        for hop in range(1, heads):
            to_head(hop, seat, chunk).wait_recv()
            for turn in range(1, subs):
                to_sub(hop, turn, seat, chunk).start()

    o_half = o_all.shape[1] // parts
    columns = pl.ds(pl.multiple_of((head * subs + sub) * update.shape[1], 128), update.shape[1])
    gate = modulation[2:3, columns]

    def product(shard, chunk):
        hop = lax.rem(head + heads - shard // subs, heads)
        turn = lax.rem(sub + subs - lax.rem(shard, subs), subs)
        rows = pl.ds(chunk * block, block)
        return rows, jnp.dot(slots[hop, turn, rows, :], o_all[shard], preferred_element_type=jnp.float32)

    def gather_up(shards, chunk):
        total = None
        for shard in shards:
            rows, term = product(shard, chunk)
            total = term if total is None else total + term
        partial[0, rows, :] = total

    def put(chunk):
        rows = pl.ds(chunk * block, block)
        return pltpu.make_async_copy(result.at[rows], update.at[rows], own_sems.at[5])

    def finish(shard, chunk):
        rows, term = product(shard, chunk)
        result[rows, :] = (gate * (partial[0, rows, :] + term)).astype(result.dtype)
        put(chunk).start()

    nearer = jnp.where(seated, me, toward)
    farther = low + high - nearer
    def relay_end(step, pieces_of_it):
        for way in (0, 1):
            outs.relay(step, way, pieces_of_it)

    @pl.when(ended)
    def _():
        relay_end(2, o_first)
        for chunk in range(chunks):
            arrive(chunk, nearer)
            if chunk == chunks // 2 - 1:
                relay_end(2, o_last)
                relay_end(3, o_first)

    for chunk in range(chunks):
        arrive(chunk, farther)
        if chunk % 2:
            @pl.when(ended)
            def _():
                relay_end(3, o_last[chunk // 2 :: chunks // 2])

    for chunk in range(chunks):
        pass_on(chunk, nearer)

    @pl.when(seated)
    def _():
        pltpu.make_async_copy(own.at[0], own.at[0], own_sems.at[4]).wait()

    last = jnp.where(ended, count - 1 - me, far)
    middle = (jnp.where(ended, toward, near), jnp.where(ended, low + high - toward, other))
    for shard in middle:
        outs.complete(shard)

    def add_up(chunk):
        taken(slots.at[pl.ds(0, heads), 0, pl.ds(0, block)], sc_sems.at[chunk])
        gather_up((me,) + middle, chunk)

    for chunk in range(chunks):
        pass_on(chunk, farther)
        if chunk:
            add_up(chunk - 1)
    outs.complete(last)
    for chunk in range(chunks - 1):
        finish(last, chunk)
    add_up(chunks - 1)
    finish(last, chunks - 1)

    taken(stage, sent.at[0])
    taken(slots.at[0, 0], sent.at[7])
    taken(slots.at[0], sent.at[8])
    taken(o_all.at[pl.ds(0, count - 1), pl.ds(0, (parts - 1) * o_half)], sent.at[10])

    @pl.when(ended)
    def _():
        taken(hfull.at[0, pl.ds(0, quarter)], sent.at[1])
        taken(lists_all.at[pl.ds(0, 2)], sent.at[9])
        taken(o_all.at[0, pl.ds(0, o_half)], sent.at[5])

    @pl.when(seated)
    def _():
        taken(hfull.at[0, pl.ds(0, 2 * quarter)], sent.at[1])
        taken(lists, sent.at[9])
        taken(hfull.at[0, pl.ds(0, (count - 1) * quarter)], sent.at[2])
        taken(hfull.at[pl.ds(0, 2)], sent.at[3])
        taken(wfull.at[pl.ds(0, count - 1), pl.ds(0, half)], sent.at[4])
        taken(o_all.at[pl.ds(0, count), pl.ds(0, 5 * o_half // count)], sent.at[5])
        taken(own.at[pl.ds(0, count - 1)], sent.at[6])

    pltpu.make_async_copy(result, update, own_sems.at[5]).wait()


def out_spot(slots, hop, turn, seat, chunk, block, low, columns):
    at = (seat - low) * columns
    at = pl.ds(pl.multiple_of(at, columns), columns)
    return slots.at[hop, turn, pl.ds(chunk * block, block), at]


def out_push(own, slots, sems, sent, seat, frame, chunk, block, low):
    return push(
        own.at[frame, pl.ds(chunk * block, block)],
        out_spot(slots, 0, 0, seat, chunk, block, low, own.shape[2]),
        sent.at[6], sems.at[seat - low, chunk], "seq", frame,
    )


def keep_out(own, slots, sem, seat, chunk, block, low):
    return pltpu.make_async_copy(
        own.at[seat, pl.ds(chunk * block, block)],
        out_spot(slots, 0, 0, seat, chunk, block, low, own.shape[2]),
        sem,
    )


class LineGather:
    def __init__(self, slots, sems, across_sems, sent, chunks, count, parts):
        self.slots, self.chunks = slots, chunks
        self.sems, self.across_sems, self.sent = sems, across_sems, sent
        self.count, self.parts = count, parts
        self.me = lax.axis_index("seq")
        self.group = lax.axis_index("groups")
        self.size = slots.shape[1] // (parts * chunks)

    def rows(self, group, chunk):
        start = (group * self.chunks + chunk) * self.size
        return pl.ds(pl.multiple_of(start, self.size), self.size)

    def along(self, shard, chunk, way):
        rows = self.rows(self.group, chunk)
        return push(
            self.slots.at[shard, rows], self.slots.at[shard, rows],
            self.sent.at[5], self.sems.at[shard, chunk],
            "seq", self.me + (1 if way == 0 else -1),
        )

    def across(self, shard, chunk, hop):
        rows = self.rows(self.group, chunk)
        return push(
            self.slots.at[shard, rows], self.slots.at[shard, rows],
            self.sent.at[10], self.across_sems.at[shard],
            "groups", lax.rem(self.group + hop, self.parts),
        )

    def onward(self, way):
        return self.me < self.count - 1 if way == 0 else self.me > 0

    def shard_of(self, step, way):
        return self.me - step if way == 0 else self.me + step

    def present(self, step, way):
        return self.me >= step if way == 0 else self.me + step < self.count

    def open_way(self, way):
        @pl.when(self.onward(way))
        def _():
            for chunk in range(self.chunks):
                self.along(self.me, chunk, way).start()

    def relay(self, step, way, chunks=None):
        shard = self.shard_of(step, way)

        @pl.when(self.present(step, way))
        def _():
            for chunk in range(self.chunks) if chunks is None else chunks:
                self.along(shard, chunk, way).wait_recv()

                @pl.when(self.onward(way))
                def _():
                    self.along(shard, chunk, way).start()

                for hop in range(1, self.parts):
                    self.across(shard, chunk, hop).start()

    def complete(self, shard):
        region = self.slots.at[shard, pl.ds(0, (self.parts - 1) * self.chunks * self.size)]
        sem = self.across_sems.at[shard]
        push(region, region, sem, sem, "seq", self.me).wait_recv()


def by_pair(tokens, modulation, w_own, o_own, pattern, counts, mask):
    sizes = tuple(lax.axis_size(axis) for axis in ("seq", "groups", "head", "sub"))
    count, parts, heads, subs = sizes
    rows, depth = tokens.shape
    width = w_own.shape[2]
    blocks = heads * subs
    quarter = rows // blocks
    chunks = rows // BLOCK
    pieces = 3
    o_chunks = 4
    columns = width // 3
    seated = len(seats(count))
    vmem = pl.BlockSpec(memory_space=pltpu.VMEM)
    whole = pl.BlockSpec(memory_space=pl.ANY)
    dma = pltpu.SemaphoreType.DMA
    kept = jnp.bfloat16
    return pl.pallas_call(
        functools.partial(by_pair_kernel, sizes, chunks, pieces, o_chunks),
        out_shape=jax.ShapeDtypeStruct((rows, o_own.shape[1]), kept),
        in_specs=[whole, vmem, whole, whole, vmem, vmem, vmem],
        out_specs=whole,
        scratch_shapes=[
            pltpu.VMEM((heads, quarter, depth), kept),
            pltpu.VMEM(w_own.shape, kept),
            pltpu.VMEM((seated, w_own.shape[0] // parts, width), kept),
            pltpu.VMEM((w_own.shape[0] // parts, width), kept),
            pltpu.VMEM((count - 1, rows, width), jnp.float32),
            pltpu.VMEM((count, rows, depth), kept),
            pltpu.VMEM((count, w_own.shape[0], width), kept),
            pltpu.VMEM((count * rows // BLOCK, BLOCK, width // 2), kept),
            pltpu.VMEM((count, rows, width // 2), kept),
            pltpu.VMEM((count,) + o_own.shape, kept),
            pltpu.VMEM((24, 128), jnp.int32),
            pltpu.VMEM((count, 24, 128), jnp.int32),
            pltpu.SMEM((count, 24, 128), jnp.int32),
            pltpu.VMEM((count, rows, columns), kept),
            pltpu.VMEM((heads, subs, rows, seated * columns), kept),
            pltpu.VMEM((rows, o_own.shape[1]), kept),
            dma((heads, 2)),
            dma((count,)),
            dma((count, pieces)),
            dma((count,)),
            dma((pieces,)),
            dma((count, chunks)),
            dma((count, chunks)),
            dma((count, chunks)),
            dma((count, o_chunks)),
            dma((count,)),
            dma((seated, chunks)),
            dma((seated, chunks)),
            dma((chunks,)),
            dma((6,)),
            dma((11,)),
        ],
        compiler_params=pltpu.CompilerParams(
            collective_id=2, has_side_effects=True, vmem_limit_bytes=60 * 1024 * 1024
        ),
        name="by_pair",
    )(tokens, modulation, w_own, o_own, pattern, counts, mask)


def shards_by_pair(tokens, modulation, w_qkv, w_out, pattern, counts, spatial_mask):
    return by_pair(tokens, modulation, w_qkv, w_out, pattern, counts[None, :], spatial_mask[0])


def one_pair_each(count, heads, subs, parts, tokens, w_qkv, w_out, pattern, spatial_mask):
    rows, frames = tokens.shape[0], spatial_mask.shape[0]
    return (
        count == 4
        and heads == subs == parts == 2
        and w_qkv.shape[1] == len(seats(count))
        and frames == 1
        and rows == BLOCK * pattern.shape[0] == BLOCK * spatial_mask.shape[1]
        and pattern.shape[0] == count
        and BLOCK % (16 * count) == 0
        and w_qkv.shape[0] % (192 * parts) == 0
        and w_out.shape[0] % (64 * parts) == 0
    )


def shards_any(*args):
    tokens, _, w_qkv, w_out, pattern, _, spatial_mask = args
    sizes = tuple(lax.axis_size(axis) for axis in ("seq", "head", "sub", "groups"))
    if one_pair_each(*sizes, tokens, w_qkv, w_out, pattern, spatial_mask):
        return shards_by_pair(*args)
    return shards(*args)


def solution(mesh):
    return jax.shard_map(
        shards_any,
        mesh=mesh,
        in_specs=(
            P(("groups", "seq"), None),
            P(),
            P("seq", ("head", "sub"), None),
            P("seq", ("head", "sub")),
            P(("groups", "seq"), None),
            P(("groups", "seq")),
            P(("groups", "seq"), None, None),
        ),
        out_specs=P(("groups", "seq"), ("head", "sub")),
        check_vma=False,
    )
```

```python
import functools
import math

import jax
import jax.numpy as jnp
from jax import lax
from jax.experimental import pallas as pl
from jax.experimental.pallas import tpu as pltpu
from jax.sharding import PartitionSpec as P

BLOCK = 128
WIN = 2


EPSILON = 1e-06


def with_halo(cells, sides, width):
    for axis, dim in sides:
        count = lax.axis_size(axis)
        ends = count - 1
        head = lax.slice_in_dim(cells, 0, width, axis=dim)
        tail = lax.slice_in_dim(cells, cells.shape[dim] - width, cells.shape[dim], axis=dim)
        cells = jnp.concatenate(
            [
                lax.ppermute(tail, axis, [(i, (i + 1) % count) for i in range(ends)]),
                cells,
                lax.ppermute(head, axis, [((i + 1) % count, i) for i in range(ends)]),
            ],
            axis=dim,
        )
    return cells


MESH = pl.DeviceIdType.MESH


def pieces_of(rows, most=4):
    for count in range(most, 0, -1):
        if rows % (16 * count) == 0:
            return count
    return 1


class ShardLine:
    def __init__(self, own, slots, sems, chunks, count, parts):
        self.own, self.slots, self.chunks = own, slots, chunks
        self.sems, self.count, self.parts = sems, count, parts
        self.me = lax.axis_index("seq")
        self.group = lax.axis_index("groups")
        self.size = own.shape[0] // (parts * chunks)

    def rows(self, group, chunk):
        start = (group * self.chunks + chunk) * self.size
        return pl.ds(pl.multiple_of(start, self.size), self.size)

    def along(self, shard, chunk, way, own):
        rows = self.rows(self.group, chunk)
        source = self.own.at[rows] if own else self.slots.at[shard, rows]
        return pltpu.make_async_remote_copy(
            src_ref=source,
            dst_ref=self.slots.at[shard, rows],
            send_sem=self.sems.at[way, 0, shard, chunk],
            recv_sem=self.sems.at[way, 1, shard, chunk],
            device_id={"seq": self.me + (1 if way == 0 else -1)},
            device_id_type=MESH,
        )

    def across(self, shard, chunk, hop):
        rows = self.rows(self.group, chunk)
        return pltpu.make_async_remote_copy(
            src_ref=self.slots.at[shard, rows],
            dst_ref=self.slots.at[shard, rows],
            send_sem=self.sems.at[1 + hop, 0, shard, chunk],
            recv_sem=self.sems.at[1 + hop, 1, shard, chunk],
            device_id={"groups": lax.rem(self.group + hop, self.parts)},
            device_id_type=MESH,
        )

    def open_line(self):
        for chunk in range(self.chunks):
            for way in (0, 1):
                @pl.when(self.onward(way))
                def _():
                    self.along(self.me, chunk, way, True).start()

    def onward(self, way):
        return self.me < self.count - 1 if way == 0 else self.me > 0

    def shard_of(self, step, way):
        return self.me - step if way == 0 else self.me + step

    def present(self, step, way):
        return self.me >= step if way == 0 else self.me + step < self.count

    def relay(self, step):
        for chunk in range(self.chunks):
            for way in (0, 1):
                shard = self.shard_of(step, way)

                @pl.when(self.present(step, way))
                def _():
                    self.along(shard, chunk, way, False).wait_recv()

                    @pl.when(self.onward(way))
                    def _():
                        self.along(shard, chunk, way, False).start()

                    for hop in range(1, self.parts):
                        self.across(shard, chunk, hop).start()

    def complete(self, shard):
        for chunk in range(self.chunks):
            for hop in range(1, self.parts):
                self.across(shard, chunk, hop).wait_recv()

    def close_sends(self, step):
        for chunk in range(self.chunks):
            for way in (0, 1):
                shard = self.shard_of(step, way)

                @pl.when(self.present(step, way))
                def _():
                    @pl.when(self.onward(way))
                    def _():
                        self.along(shard, chunk, way, False).wait_send()

                    for hop in range(1, self.parts):
                        self.across(shard, chunk, hop).wait_send()

    def close_own(self):
        for chunk in range(self.chunks):
            for way in (0, 1):
                @pl.when(self.onward(way))
                def _():
                    self.along(self.me, chunk, way, True).wait_send()


def project_kernel(count, parts, q_chunks, o_chunks, hidden, w_own, o_own, qkv, o_all, slots, total, q_sems, o_sems, own_sem):
    me = lax.axis_index("seq")
    group = lax.axis_index("groups")
    barrier = pltpu.get_barrier_semaphore()

    @pl.when(me > 0)
    def _():
        pl.semaphore_signal(barrier, inc=1, device_id={"seq": me - 1}, device_id_type=MESH)

    @pl.when(me < count - 1)
    def _():
        pl.semaphore_signal(barrier, inc=1, device_id={"seq": me + 1}, device_id_type=MESH)

    for hop in range(1, parts):
        pl.semaphore_signal(
            barrier, inc=1, device_id={"groups": lax.rem(group + hop, parts)}, device_id_type=MESH
        )
    neighbours = jnp.where(me > 0, 1, 0) + jnp.where(me < count - 1, 1, 0) + (parts - 1)
    pl.semaphore_wait(barrier, neighbours)

    line = ShardLine(w_own, slots, q_sems, q_chunks, count, parts)
    outs = ShardLine(o_own, o_all, o_sems, o_chunks, count, parts)
    line.open_line()
    keep = pltpu.make_async_copy(o_own, o_all.at[me], own_sem)
    keep.start()
    tile = 256

    def add(shard, block, first):
        def column(j, carry):
            at = pl.ds(pl.multiple_of(j * tile, tile), tile)
            product = jnp.dot(hidden[shard], block[:, at], preferred_element_type=jnp.float32)
            total[:, at] = product if first else total[:, at] + product
            return carry

        lax.fori_loop(0, total.shape[1] // tile, column, 0)

    def finish(step):
        for way in (0, 1):
            shard = line.shard_of(step, way)

            @pl.when(line.present(step, way))
            def _():
                line.complete(shard)
                add(shard, slots.at[shard], False)

    add(me, w_own, True)

    def q_step(step, carry):
        line.relay(step)

        @pl.when(step > 1)
        def _():
            finish(step - 1)

        return carry

    lax.fori_loop(1, count, q_step, 0)
    outs.open_line()
    finish(count - 1)
    qkv[...] = total[...].astype(qkv.dtype)

    def o_step(step, carry):
        outs.relay(step)
        return carry

    lax.fori_loop(1, count, o_step, 0)

    def last(step, carry):
        line.close_sends(step)
        outs.close_sends(step)
        for way in (0, 1):
            shard = outs.shard_of(step, way)

            @pl.when(outs.present(step, way))
            def _():
                outs.complete(shard)

        return carry

    lax.fori_loop(1, count, last, 0)
    line.close_own()
    outs.close_own()
    keep.wait()


def project(hidden, w_own, o_own):
    count, parts = lax.axis_size("seq"), lax.axis_size("groups")
    rows, depth = hidden.shape
    hidden = hidden.reshape(rows, count, depth // count).transpose(1, 0, 2)
    width = w_own.shape[1]
    most = 4 if count <= 8 else 1
    q_chunks = pieces_of(w_own.shape[0] // parts, most)
    o_chunks = pieces_of(o_own.shape[0] // parts, most)
    vmem = pl.BlockSpec(memory_space=pltpu.VMEM)
    return pl.pallas_call(
        functools.partial(project_kernel, count, parts, q_chunks, o_chunks),
        out_shape=[
            jax.ShapeDtypeStruct((rows, width), jnp.bfloat16),
            jax.ShapeDtypeStruct((count,) + o_own.shape, jnp.bfloat16),
        ],
        in_specs=[vmem] * 3,
        out_specs=[vmem, pl.BlockSpec(memory_space=pl.ANY)],
        scratch_shapes=[
            pltpu.VMEM((count,) + w_own.shape, jnp.bfloat16),
            pltpu.VMEM((rows, width), jnp.float32),
            pltpu.SemaphoreType.DMA((1 + parts, 2, count, q_chunks)),
            pltpu.SemaphoreType.DMA((1 + parts, 2, count, o_chunks)),
            pltpu.SemaphoreType.DMA,
        ],
        compiler_params=pltpu.CompilerParams(
            collective_id=0, has_side_effects=True, vmem_limit_bytes=48 * 1024 * 1024
        ),
        name="project",
    )(hidden, w_own, o_own)


def mix_kernel(heads, subs, chunks, attn, w_all, gate, update, slots, total, x_sems, c_sems):
    head, sub = lax.axis_index("head"), lax.axis_index("sub")
    barrier = pltpu.get_barrier_semaphore()
    for hop in range(1, heads):
        pl.semaphore_signal(
            barrier, inc=1, device_id={"head": lax.rem(head + hop, heads)}, device_id_type=MESH
        )
    for hop in range(1, subs):
        pl.semaphore_signal(
            barrier, inc=1, device_id={"sub": lax.rem(sub + hop, subs)}, device_id_type=MESH
        )
    pl.semaphore_wait(barrier, heads + subs - 2)
    size = attn.shape[0] // chunks

    def to_head(hop, chunk):
        rows = pl.ds(chunk * size, size)
        return pltpu.make_async_remote_copy(
            src_ref=attn.at[rows],
            dst_ref=slots.at[hop, 0, rows],
            send_sem=x_sems.at[hop, 0, chunk],
            recv_sem=x_sems.at[hop, 1, chunk],
            device_id={"head": lax.rem(head + hop, heads)},
            device_id_type=MESH,
        )

    def to_sub(hop, turn, chunk):
        rows = pl.ds(chunk * size, size)
        return pltpu.make_async_remote_copy(
            src_ref=attn.at[rows] if hop == 0 else slots.at[hop, 0, rows],
            dst_ref=slots.at[hop, turn, rows],
            send_sem=c_sems.at[hop, turn, 0, chunk],
            recv_sem=c_sems.at[hop, turn, 1, chunk],
            device_id={"sub": lax.rem(sub + turn, subs)},
            device_id_type=MESH,
        )

    for chunk in range(chunks):
        for hop in range(1, heads):
            to_head(hop, chunk).start()
        for turn in range(1, subs):
            to_sub(0, turn, chunk).start()

    def add(chunk, hop, turn, first):
        rows = slice(chunk * size, (chunk + 1) * size)
        owner = lax.rem(head + heads - hop, heads) * subs + lax.rem(sub + subs - turn, subs)
        block = attn[rows, :] if hop == 0 and turn == 0 else slots[hop, turn, rows, :]
        product = jnp.dot(block, w_all[owner], preferred_element_type=jnp.float32)
        total[rows, :] = product if first else total[rows, :] + product

    for chunk in range(chunks):
        add(chunk, 0, 0, True)
    for chunk in range(chunks):
        for turn in range(1, subs):
            to_sub(0, turn, chunk).wait_recv()
            add(chunk, 0, turn, False)
    for chunk in range(chunks):
        for hop in range(1, heads):
            to_head(hop, chunk).wait_recv()
            for turn in range(1, subs):
                to_sub(hop, turn, chunk).start()
            add(chunk, hop, 0, False)
    for chunk in range(chunks):
        for hop in range(1, heads):
            for turn in range(1, subs):
                to_sub(hop, turn, chunk).wait_recv()
                add(chunk, hop, turn, False)
        rows = slice(chunk * size, (chunk + 1) * size)
        update[rows, :] = (gate[...] * total[rows, :]).astype(update.dtype)
    for chunk in range(chunks):
        for hop in range(1, heads):
            to_head(hop, chunk).wait_send()
        for hop in range(heads):
            for turn in range(1, subs):
                to_sub(hop, turn, chunk).wait_send()


def mix(attention, w_all, gate):
    heads, subs = lax.axis_size("head"), lax.axis_size("sub")
    rows, width = attention.shape
    chunks = pieces_of(rows, 2)
    vmem = pl.BlockSpec(memory_space=pltpu.VMEM)
    return pl.pallas_call(
        functools.partial(mix_kernel, heads, subs, chunks),
        out_shape=jax.ShapeDtypeStruct((rows, w_all.shape[-1]), jnp.bfloat16),
        in_specs=[vmem] * 3,
        out_specs=vmem,
        scratch_shapes=[
            pltpu.VMEM((heads, subs, rows, width), jnp.bfloat16),
            pltpu.VMEM((rows, w_all.shape[-1]), jnp.float32),
            pltpu.SemaphoreType.DMA((heads, 2, chunks)),
            pltpu.SemaphoreType.DMA((heads, subs, 2, chunks)),
        ],
        compiler_params=pltpu.CompilerParams(
            collective_id=1, has_side_effects=True, vmem_limit_bytes=40 * 1024 * 1024
        ),
        name="mix",
    )(attention, w_all, gate)


def modulate(tokens, modulation):
    values = tokens.astype(jnp.float32)
    center = jnp.mean(values, axis=-1, keepdims=True)
    spread = jnp.mean(jnp.square(values - center), axis=-1, keepdims=True)
    normed = (values - center) * lax.rsqrt(spread + EPSILON)
    return (normed * (1.0 + modulation[1]) + modulation[0]).astype(jnp.bfloat16)


def shards(tokens, modulation, w_qkv, w_out, pattern, counts, spatial_mask):
    row_count, feature_width = tokens.shape
    pairs_local = w_qkv.shape[1]
    head_size = w_qkv.shape[2] // 6
    frames_local = spatial_mask.shape[0]
    positions = row_count // frames_local
    slot_total = pattern.shape[1]
    scale_factor = 1.0 / math.sqrt(head_size)
    hidden = modulate(tokens, modulation)
    projected, whole_out = project(hidden, w_qkv.reshape(w_qkv.shape[0], -1), w_out)
    packed = projected.reshape(
        frames_local, positions, pairs_local, 6 * head_size
    )
    temporal_in = packed[..., : 3 * head_size].transpose(1, 0, 2, 3)
    received = lax.all_to_all(temporal_in, "seq", split_axis=0, concat_axis=1, tiled=True)
    position_span, frame_total, items, _ = received.shape
    relaid = received.reshape(position_span * frame_total, items, 3 * head_size)
    extended = with_halo(relaid[:, :, head_size:], (("seq", 0),), WIN * BLOCK)
    block_count = position_span * frame_total // BLOCK
    key_table = extended.reshape(block_count + 2 * WIN, BLOCK, items, 2 * head_size)
    queries = relaid[:, :, :head_size].reshape(block_count, BLOCK, items, head_size)
    offsets = pattern - (lax.axis_index("seq") * block_count - WIN)

    def slot_step(slot_index, state_pair):
        numerator, denominator = state_pair
        chosen = lax.dynamic_index_in_dim(offsets, slot_index, 1, keepdims=False)
        picked = jnp.take(key_table, chosen, axis=0)
        scores = (
            jnp.einsum(
                "bqnc,bknc->bnqk",
                queries,
                picked[..., :head_size],
                preferred_element_type=jnp.float32,
            )
            * scale_factor
        )
        alive = (slot_index < counts).astype(jnp.float32)
        weights = jnp.exp(scores) * alive[:, None, None, None]
        numerator = numerator + jnp.einsum(
            "bnqk,bknc->bnqc",
            weights.astype(jnp.bfloat16),
            picked[..., head_size:],
            preferred_element_type=jnp.float32,
        )
        return (numerator, denominator + jnp.sum(weights, axis=-1))

    start_state = (
        jnp.zeros((block_count, items, BLOCK, head_size), jnp.float32),
        jnp.zeros((block_count, items, BLOCK), jnp.float32),
    )
    numerator, denominator = lax.fori_loop(0, slot_total, slot_step, start_state)
    outcome = (numerator / denominator[..., None]).astype(jnp.bfloat16)
    outcome = outcome.transpose(0, 2, 1, 3).reshape(position_span, frame_total, items, head_size)
    temporal_out = lax.all_to_all(outcome, "seq", split_axis=1, concat_axis=0, tiled=True)
    spatial = packed[..., 3 * head_size :]
    blocks_frame = positions // BLOCK
    scores = (
        jnp.einsum(
            "fpnc,fqnc->fnpq",
            spatial[..., :head_size],
            spatial[..., head_size : 2 * head_size],
            preferred_element_type=jnp.float32,
        )
        * scale_factor
    )
    keep = spatial_mask.astype(jnp.float32)[:, None, :, None, :, None]
    weights = (
        jnp.exp(scores).reshape(frames_local, pairs_local, blocks_frame, BLOCK, blocks_frame, BLOCK)
        * keep
    )
    weights = weights.reshape(frames_local, pairs_local, positions, positions)
    denominator = jnp.sum(weights, axis=-1)
    numerator = jnp.einsum(
        "fnpq,fqnc->fpnc",
        weights.astype(jnp.bfloat16),
        spatial[..., 2 * head_size :],
        preferred_element_type=jnp.float32,
    )
    spatial_out = (numerator / denominator.transpose(0, 2, 1)[..., None]).astype(jnp.bfloat16)
    attention = jnp.concatenate([temporal_out.transpose(1, 0, 2, 3), spatial_out], axis=-1)
    attention = attention.reshape(row_count, pairs_local * 2 * head_size)
    out_width = w_out.shape[1]
    blocks = lax.axis_size("head") * lax.axis_size("sub")
    gate_slice = lax.dynamic_slice_in_dim(
        modulation[2], lax.axis_index(("head", "sub")) * out_width, out_width, 0
    )
    return mix(attention, whole_out.reshape(blocks, -1, out_width), gate_slice[None, :])

def push(source, target, send_sem, recv_sem, axis, place):
    return pltpu.make_async_remote_copy(
        src_ref=source,
        dst_ref=target,
        send_sem=send_sem,
        recv_sem=recv_sem,
        device_id={axis: place},
        device_id_type=MESH,
    )


def seats(count):
    return (count // 2 - 1, count // 2)


def by_pair_kernel(
    sizes, chunks, pieces, o_chunks,
    tokens, modulation, w_own, o_own, pattern, counts, mask, update,
    held, raw, stage, passing, partial, hfull, wfull, tq, sq, o_all, lists, lists_all, table, own, slots, result,
    tok_sems, l_sems, w_sems, wa_sems, p_sems, z_sems, x_sems, c_sems, o_sems, oa_sems,
    sz_sems, sx_sems, sc_sems, own_sems, sent,
):
    count, parts, heads, subs = sizes
    low, high = seats(count)
    me, group = lax.axis_index("seq"), lax.axis_index("groups")
    head, sub = lax.axis_index("head"), lax.axis_index("sub")
    other = low + high - me
    near = jnp.where(me == low, low - 1, high + 1)
    far = jnp.where(me == low, high + 1, low - 1)
    seated = jnp.logical_or(me == low, me == high)
    ended = jnp.logical_not(seated)
    outward = jnp.where(me == low, 1, 0)
    blocks = heads * subs
    quarter = held.shape[1]
    unit = quarter // chunks
    width = wfull.shape[2]
    half = w_own.shape[0] // parts
    piece = half // pieces
    block = unit * blocks

    barrier = pltpu.get_barrier_semaphore()
    others = 0
    for axis in ("seq", "groups", "head", "sub"):
        size = lax.axis_size(axis)
        for hop in range(1, size):
            partner = lax.rem(lax.axis_index(axis) + hop, size)
            pl.semaphore_signal(barrier, inc=1, device_id={axis: partner}, device_id_type=MESH)
            others += 1

    def rows_of(head_hop, sub_hop, chunk):
        owner = lax.rem(head + heads - head_hop, heads) * subs + lax.rem(sub + subs - sub_hop, subs)
        return pl.ds(pl.multiple_of((chunk * blocks + owner) * unit, unit), unit)

    def fetch(hop, chunk):
        return pltpu.make_async_copy(
            tokens.at[rows_of(hop, 0, chunk)], held.at[hop, pl.ds(chunk * unit, unit)],
            tok_sems.at[hop, min(chunk, 1) if hop == 0 else 0],
        )

    def fetched(hop, first, last):
        pltpu.make_async_copy(
            tokens.at[pl.ds(first * unit, (last - first) * unit)],
            held.at[hop, pl.ds(first * unit, (last - first) * unit)],
            tok_sems.at[hop, min(first, 1) if hop == 0 else 0],
        ).wait()

    def taken(region, sem):
        push(region, region, sem, sem, "seq", me).wait_recv()

    for chunk in range(chunks):
        fetch(0, chunk).start()
    raw_copy = pltpu.make_async_copy(w_own, raw, own_sems.at[0])
    raw_copy.start()
    o_copy = pltpu.make_async_copy(o_own, o_all.at[me], own_sems.at[1])
    o_copy.start()

    @pl.when(seated)
    def _():
        for hop in range(1, heads):
            for chunk in range(chunks):
                fetch(hop, chunk).start()

    lists[...] = jnp.zeros_like(lists)
    slots_of = pattern.shape[1]
    lists[0 : pattern.shape[0], 0:slots_of] = pattern[...]
    lists[8 : 8 + mask.shape[0], 0 : mask.shape[1]] = mask[...]
    lists[16:17, 0 : counts.shape[1]] = counts[...]
    gain = 1.0 + modulation[1:2, :]
    shift = modulation[0:1, :]

    def modulate_rows(hop, first, last):
        def some(i, carry):
            at = pl.ds(pl.multiple_of(i * 16, 16), 16)
            chunk = i // (unit // 16)
            owner = lax.rem(head + heads - hop, heads) * subs + sub
            start = (chunk * blocks + owner) * unit + lax.rem(i, unit // 16) * 16
            values = held[hop, at, :].astype(jnp.float32)
            centered = values - jnp.mean(values, axis=-1, keepdims=True)
            spread_of = jnp.mean(jnp.square(centered), axis=-1, keepdims=True)
            normed = centered * lax.rsqrt(spread_of + EPSILON)
            hfull[me, pl.ds(pl.multiple_of(start, 16), 16), :] = (normed * gain + shift).astype(hfull.dtype)
            return carry

        fetched(hop, first, last)
        lax.fori_loop(first * unit // 16, last * unit // 16, some, 0, unroll=2)

    modulate_rows(0, 0, 1)
    pl.semaphore_wait(barrier, others)

    def spot(frame, head_hop, sub_hop, chunk):
        return hfull.at[frame, rows_of(head_hop, sub_hop, chunk)]

    def z_push(frame, chunk, place):
        target = spot(frame, 0, 0, chunk)
        return push(target, target, sent.at[1], z_sems.at[frame, chunk], "seq", place)

    def x_push(frame, chunk, hop):
        target = spot(frame, 0, 0, chunk)
        return push(
            target, target, sent.at[2], x_sems.at[frame, chunk],
            "head", lax.rem(head + hop, heads),
        )

    def c_push(frame, chunk, hop, turn):
        target = spot(frame, hop, 0, chunk)
        return push(
            target, target, sent.at[3], c_sems.at[frame, chunk],
            "sub", lax.rem(sub + turn, subs),
        )

    def z_half(frame, part, place):
        start = ((chunks - 1) * blocks + head * subs + sub) * unit + part * (unit // 2)
        target = hfull.at[frame, pl.ds(pl.multiple_of(start, unit // 2), unit // 2)]
        return push(target, target, sent.at[1], z_sems.at[frame, chunks - 1 + part], "seq", place)

    def x_half(frame, part):
        start = ((chunks - 1) * blocks + head * subs + sub) * unit + part * (unit // 2)
        target = hfull.at[frame, pl.ds(pl.multiple_of(start, unit // 2), unit // 2)]
        return push(
            target, target, sent.at[2], x_sems.at[frame, chunks - 1 + part],
            "head", lax.rem(head + 1, heads),
        )

    def l_push(seat):
        return push(lists, lists_all.at[me], sent.at[9], l_sems.at[me], "seq", seat)

    def w_rows(part, step):
        return pl.ds(pl.multiple_of(part * half + step * piece, piece), piece)

    def w_along(seat, source, step):
        return push(
            stage.at[seat - low, pl.ds(step * piece, piece)], wfull.at[source, w_rows(group, step)],
            sent.at[0], w_sems.at[source, step], "seq", seat,
        )

    def w_hand(step, place):
        return push(
            stage.at[jnp.where(me < low, high, low) - low, pl.ds(step * piece, piece)],
            passing.at[pl.ds(step * piece, piece)],
            sent.at[0], p_sems.at[step], "seq", place,
        )

    def w_pass(source, step):
        return push(
            passing.at[pl.ds(step * piece, piece)], wfull.at[source, w_rows(group, step)],
            sent.at[0], w_sems.at[source, step], "seq", other,
        )

    def w_across(source, step, turn):
        target = wfull.at[source, w_rows(group, step)]
        return push(
            target, target, sent.at[4], wa_sems.at[source],
            "groups", lax.rem(group + turn, parts),
        )

    outs = LineGather(o_all, o_sems, oa_sems, sent, o_chunks, count, parts)

    for seat in (low, high):
        @pl.when(me != seat)
        def _():
            l_push(seat).start()

    columns_of = own.shape[2]

    def item(hop, turn, seat, chunk):
        return out_spot(slots, hop, turn, seat, chunk, block, low, columns_of)

    def to_head(hop, seat, chunk, source=None):
        return push(
            item(0, 0, seat, chunk) if source is None else source, item(hop, 0, seat, chunk),
            sent.at[7], sx_sems.at[seat - low, chunk],
            "head", lax.rem(head + hop, heads),
        )

    def to_sub(hop, turn, seat, chunk, source=None):
        return push(
            item(hop, 0, seat, chunk) if source is None else source, item(hop, turn, seat, chunk),
            sent.at[8], sc_sems.at[seat - low, chunk],
            "sub", lax.rem(sub + turn, subs),
        )

    toward = jnp.where(me < low, low, high)

    def open_inward(pieces_of_it):
        for way in (0, 1):
            @pl.when(outward != way)
            def _():
                outs.open_way(way, pieces_of_it)

    def relay_out(step, pieces_of_it, outgoing):
        for way in (0, 1):
            @pl.when((outward == way) == outgoing)
            def _():
                outs.relay(step, way, pieces_of_it)

    o_first, o_last = tuple(range(o_chunks // 2)), tuple(range(o_chunks // 2, o_chunks))

    def z_out(first, last):
        @pl.when(seated)
        def _():
            for chunk in range(first, last):
                z_push(me, chunk, other).start()

        @pl.when(ended)
        def _():
            for chunk in range(first, last):
                z_push(me, chunk, toward).start()

    z_out(0, 1)
    raw_copy.wait()

    def unpack(i, carry):
        start = pl.multiple_of(i * 64, 64)
        both = raw[pl.ds(pl.multiple_of(group * half + start, 64), 64)]
        first, second = both[:, 0, :], both[:, 1, :]
        stage[0, pl.ds(start, 64), :] = first
        stage[1, pl.ds(start, 64), :] = second
        return carry

    lax.fori_loop(0, half // 64, unpack, 0)

    @pl.when(ended)
    def _():
        for step in range(pieces):
            w_hand(step, toward).start()

    @pl.when(seated)
    def _():
        for step in range(pieces):
            w_along(other, me, step).start()

    modulate_rows(0, 1, chunks)
    o_copy.wait()

    @pl.when(ended)
    def _():
        z_out(1, chunks)
        for step in range(pieces):
            w_along(toward, me, step).start()
        for way in (0, 1):
            outs.open_way(way)
        for way in (0, 1):
            outs.relay(1, way)

    @pl.when(seated)
    def _():
        for way in (0, 1):
            @pl.when(outward == way)
            def _():
                outs.open_way(way)

        keep = pltpu.make_async_copy(lists, lists_all.at[me], own_sems.at[2])
        keep.start()
        for chunk in range(chunks):
            for turn in range(1, subs):
                c_push(me, chunk, 0, turn).start()
        for hop in range(1, heads):
            modulate_rows(hop, 0, chunks)
            for chunk in range(chunks):
                for turn in range(1, subs):
                    c_push(me, chunk, hop, turn).start()

        def land(frame, chunk):
            z_push(frame, chunk, other).wait_recv()
            for hop in range(1, heads):
                x_push(frame, chunk, hop).start()
            for turn in range(1, subs):
                c_push(frame, chunk, 0, turn).start()

        def crossed(frame, chunk):
            for hop in range(1, heads):
                x_push(frame, chunk, hop).wait_recv()
                for turn in range(1, subs):
                    c_push(frame, chunk, hop, turn).start()

        def gathered(frame, chunk):
            taken(hfull.at[frame, pl.ds(0, heads * (subs - 1) * unit)], c_sems.at[frame, chunk])

        def keep_pair(i, carry):
            at = pl.ds(pl.multiple_of(i * 64, 64), 64)
            both = raw[at]
            wfull[me, at, :] = jnp.where(me == low, both[:, 0, :], both[:, 1, :])
            return carry

        def w_land(source, step):
            w_along(me, source, step).wait_recv()
            for turn in range(1, parts):
                w_across(source, step, turn).start()

        span = unit
        scale = math.log2(math.e) / math.sqrt(own.shape[2] // 2)
        size = own.shape[2] // 2
        total_blocks = tq.shape[0]
        each = total_blocks // count
        window = 2 * WIN + 1

        depth = wfull.shape[1]

        def first_part(frame, slot):
            def some_rows(chunk, carry):
                rows = pl.ds(pl.multiple_of(chunk * block, block), block)
                partial[slot, rows, :] = jnp.dot(
                    hfull[frame, rows, low * depth : (high + 1) * depth],
                    wfull[low : high + 1].reshape(-1, width), preferred_element_type=jnp.float32,
                )
                return carry

            lax.fori_loop(0, chunks, some_rows, 0, unroll=2)

        def keep_qkv(frame, chunk, total):
            at = pl.ds(pl.multiple_of(frame * span, span), span)
            for i in range(blocks):
                tq[chunk * blocks + i, at, :] = total[i * span : (i + 1) * span, : 3 * size]
            sq[frame, pl.ds(pl.multiple_of(chunk * block, block), block), :] = total[:, 3 * size :]

        land(near, 0)
        land(other, 0)
        for step in range(pieces):
            w_hand(step, other).wait_recv()
            w_pass(near, step).start()
            w_land(other, step)
        for chunk in range(1, chunks):
            z_push(me, chunk, other).start()
        z_push(near, 0, other).start()
        crossed(near, 0)
        crossed(other, 0)
        lax.fori_loop(0, w_own.shape[0] // 64, keep_pair, 0)
        rest = max(pieces, chunks - 1)
        for i in range(rest):
            if i + 1 < chunks:
                land(near, i + 1)
                if i == 1:
                    open_inward(o_first)
                if i + 2 < chunks:
                    z_push(near, i + 1, other).start()
                else:
                    for part in (0, 1):
                        z_half(near, part, other).start()
            if i < pieces:
                w_land(far, i)
        open_inward(o_last)

        def crossed_w(source):
            taken(wfull.at[source, pl.ds(0, (parts - 1) * half)], wa_sems.at[source])

        def all_in(frame):
            for chunk in range(chunks):
                gathered(frame, chunk)

        crossed_w(other)
        all_in(me)
        first_part(me, 0)
        for source in (near, other, far):
            taken(lists, l_sems.at[source])
        keep.wait()
        to_table = pltpu.make_async_copy(lists_all, table, own_sems.at[3])
        to_table.start()
        for i in range(rest):
            if i + 1 < chunks:
                land(other, i + 1)
            if i < pieces:
                w_land(near, i)
            if i + 1 < chunks:
                crossed(near, i + 1)
            if i == rest - 1:
                all_in(near)
                first_part(near, 1)
        def project(frame, chunk):
            rows = pl.ds(pl.multiple_of(chunk * block, block), block)
            total = jnp.dot(
                hfull[frame, rows, :], wfull[...].reshape(-1, width), preferred_element_type=jnp.float32
            ).astype(tq.dtype)
            keep_qkv(frame, chunk, total)

        def add_part(frame, slot, source):
            at = pl.ds(pl.multiple_of(source * depth, depth), depth)

            def some_rows(chunk, carry):
                rows = pl.ds(pl.multiple_of(chunk * block, block), block)
                partial[slot, rows, :] += jnp.dot(
                    hfull[frame, rows, at], wfull[source], preferred_element_type=jnp.float32
                )
                return carry

            lax.fori_loop(0, chunks, some_rows, 0, unroll=2)

        def project_frame(frame, slot):
            at = pl.ds(pl.multiple_of(near * depth, depth), depth)

            def last_part(chunk, carry):
                rows = pl.ds(pl.multiple_of(chunk * block, block), block)
                total = partial[slot, rows, :] + jnp.dot(
                    hfull[frame, rows, at], wfull[near], preferred_element_type=jnp.float32
                )
                keep_qkv(frame, chunk, total.astype(tq.dtype))
                return carry

            lax.fori_loop(0, chunks, last_part, 0, unroll=2)

        def soft(q, keys, values, biases):
            scores = lax.dot_general(
                q, keys, (((1,), (1,)), ((), ())), preferred_element_type=jnp.float32
            )
            parts_of = []
            sums = None
            for i, bias in enumerate(biases):
                weight = jnp.exp2(scores[:, i * BLOCK : (i + 1) * BLOCK] * scale + bias)
                sums = weight if sums is None else sums + weight
                parts_of.append(weight.astype(jnp.bfloat16))
            numerator = jnp.dot(
                jnp.concatenate(parts_of, axis=1), values, preferred_element_type=jnp.float32
            )
            return (numerator / jnp.sum(sums, axis=-1, keepdims=True)).astype(own.dtype)

        def temporal(chunk):
            def query(i, carry):
                b = chunk * blocks + i
                device, row = b // each, lax.rem(b, each)
                start = jnp.clip(b - WIN, 0, total_blocks - window)
                used = table[device, 16, row]
                biases = []
                for w in range(window):
                    times = 0
                    for j in range(slots_of):
                        hit = jnp.logical_and(j < used, table[device, row, j] == start + w)
                        times = times + jnp.where(hit, 1, 0)
                    bias = jnp.float32(-jnp.inf)
                    for m in range(1, slots_of + 1):
                        bias = jnp.where(times == m, jnp.float32(math.log2(m)), bias)
                    biases.append(bias)
                near_by = pl.ds(start, window)
                result = soft(
                    tq[b, :, :size],
                    tq[near_by, :, size : 2 * size].reshape(-1, size),
                    tq[near_by, :, 2 * size :].reshape(-1, size),
                    biases,
                )
                at = pl.ds(pl.multiple_of(b * span, span), span)
                for f in range(count):
                    own[f, at, :size] = result[f * span : (f + 1) * span]
                return carry

            lax.fori_loop(0, blocks, query, 0, unroll=True)

        def spatial(frame):
            per = sq.shape[1] // BLOCK

            def query(i, carry):
                at = pl.ds(pl.multiple_of(i * BLOCK, BLOCK), BLOCK)
                biases = [
                    jnp.where(table[frame, 8 + i, j] > 0, jnp.float32(0), jnp.float32(-jnp.inf))
                    for j in range(per)
                ]
                own[frame, at, size:] = soft(
                    sq[frame, at, :size], sq[frame, :, size : 2 * size], sq[frame, :, 2 * size :], biases
                )
                return carry

            lax.fori_loop(0, per, query, 0, unroll=True)

        def send(frame, chunk):
            out_push(own, slots, sz_sems, sent, me, frame, chunk, block, low).start()

        def settle(chunk):
            send(near, chunk)
            send(other, chunk)
            keep_out(own, slots, own_sems.at[4], me, chunk, block, low).start()
            mine = own.at[me, pl.ds(chunk * block, block)]
            for hop in range(1, heads):
                to_head(hop, me, chunk, mine).start()
            for turn in range(1, subs):
                to_sub(0, turn, me, chunk, mine).start()

        def far_project(chunk):
            gathered(far, chunk)
            project(far, chunk)

        crossed(other, 1)
        land(far, 0)
        crossed_w(far)
        add_part(me, 0, far)
        crossed(other, 2)
        add_part(near, 1, far)
        crossed(other, 3)
        land(far, 1)
        all_in(other)
        first_part(other, 2)
        add_part(other, 2, far)
        crossed_w(near)
        to_table.wait()
        relay_out(1, (0,), True)
        project_frame(me, 0)
        crossed(far, 0)
        project_frame(near, 1)
        relay_out(1, (1,), True)
        project_frame(other, 2)
        crossed(far, 1)
        spatial(me)
        land(far, 2)
        spatial(near)
        relay_out(1, None, False)
        far_project(0)
        far_project(1)
        spatial(other)
        for part in (0, 1):
            z_half(far, part, other).wait_recv()
            x_half(far, part).start()
        for turn in range(1, subs):
            c_push(far, 3, 0, turn).start()
        temporal(0)
        settle(0)
        relay_out(1, (2,), True)
        crossed(far, 2)
        far_project(2)
        temporal(1)
        settle(1)
        relay_out(1, (3,), True)
        for part in (0, 1):
            x_half(far, part).wait_recv()
        for turn in range(1, subs):
            c_push(far, 3, 1, turn).start()
        far_project(3)
        spatial(far)
        send(far, 0)
        send(far, 1)
        relay_out(2, (0,), True)
        temporal(2)
        settle(2)
        send(far, 2)
        relay_out(2, (1,), True)
        temporal(3)
        settle(3)
        send(far, 3)
        relay_out(2, (2, 3), True)

    def arrive(chunk, seat):
        out_push(own, slots, sz_sems, sent, seat, me, chunk, block, low).wait_recv()
        for hop in range(1, heads):
            to_head(hop, seat, chunk).start()
        for turn in range(1, subs):
            to_sub(0, turn, seat, chunk).start()

    def pass_on(chunk, seat):
        for hop in range(1, heads):
            to_head(hop, seat, chunk).wait_recv()
            for turn in range(1, subs):
                to_sub(hop, turn, seat, chunk).start()

    o_half = o_all.shape[1] // parts
    columns = pl.ds(pl.multiple_of((head * subs + sub) * update.shape[1], 128), update.shape[1])
    gate = modulation[2:3, columns]

    def product(shard, chunk, seat):
        hop = lax.rem(head + heads - shard // subs, heads)
        turn = lax.rem(sub + subs - lax.rem(shard, subs), subs)
        start = pl.multiple_of((seat - low) * columns_of, columns_of)
        at = pl.ds(start, columns_of)
        return jnp.dot(
            slots[hop, turn, pl.ds(chunk * block, block), at], o_all[shard, at, :],
            preferred_element_type=jnp.float32,
        )

    def add_up(chunk, seat, shards, total=None):
        for shard in shards:
            term = product(shard, chunk, seat)
            total = term if total is None else total + term
        return total

    def passed(chunk, seat):
        taken(slots.at[0, 0, pl.ds(chunk * block, block)], sc_sems.at[seat - low, chunk])

    def put(chunk):
        rows = pl.ds(chunk * block, block)
        return pltpu.make_async_copy(result.at[rows], update.at[rows], own_sems.at[5])

    nearer = jnp.where(seated, me, toward)
    farther = low + high - nearer
    last = jnp.where(ended, count - 1 - me, far)
    middle = (jnp.where(ended, toward, near), jnp.where(ended, low + high - toward, other))

    def relay_end(step, pieces_of_it):
        for way in (0, 1):
            outs.relay(step, way, pieces_of_it)

    def first_half(chunk):
        passed(chunk, nearer)
        rows = pl.ds(chunk * block, block)
        partial[0, rows, :] = add_up(chunk, nearer, (me,) + middle)

    def second_half(chunk):
        passed(chunk, farther)
        rows = pl.ds(chunk * block, block)
        partial[0, rows, :] = add_up(chunk, farther, (me,) + middle, partial[0, rows, :])

    def finish(chunk):
        rows = pl.ds(chunk * block, block)
        total = add_up(chunk, nearer, (last,), partial[0, rows, :])
        total = add_up(chunk, farther, (last,), total)
        result[rows, :] = (gate * total).astype(result.dtype)
        put(chunk).start()

    @pl.when(ended)
    def _():
        relay_end(2, o_first)
        arrive(0, nearer)
        arrive(1, nearer)
        relay_end(2, o_last)
        pass_on(0, nearer)
        pass_on(1, nearer)
        for shard in middle:
            outs.complete(shard)
        first_half(0)
        first_half(1)
        relay_end(3, o_first)
        arrive(2, nearer)
        arrive(3, nearer)

    arrive(0, farther)
    arrive(1, farther)

    @pl.when(ended)
    def _():
        relay_end(3, o_last[:1])

    @pl.when(seated)
    def _():
        for chunk in range(chunks):
            pass_on(chunk, nearer)
        pltpu.make_async_copy(own.at[0], own.at[0], own_sems.at[4]).wait()
        for shard in middle:
            outs.complete(shard)
        first_half(0)
        first_half(1)

    arrive(2, farther)
    arrive(3, farther)

    @pl.when(ended)
    def _():
        relay_end(3, o_last[1:])
        pass_on(2, nearer)
        pass_on(3, nearer)

    first_half(2)
    first_half(3)
    for chunk in range(chunks):
        pass_on(chunk, farther)
        if chunk:
            second_half(chunk - 1)
    second_half(chunks - 1)
    outs.complete(last)
    for chunk in range(chunks):
        finish(chunk)

    taken(stage, sent.at[0])
    taken(slots.at[0, 0], sent.at[7])
    taken(slots.at[0], sent.at[8])
    taken(o_all.at[pl.ds(0, count - 1), pl.ds(0, (parts - 1) * o_half)], sent.at[10])

    @pl.when(ended)
    def _():
        taken(hfull.at[0, pl.ds(0, quarter)], sent.at[1])
        taken(lists_all.at[pl.ds(0, 2)], sent.at[9])
        taken(o_all.at[0, pl.ds(0, o_half)], sent.at[5])

    @pl.when(seated)
    def _():
        taken(hfull.at[0, pl.ds(0, 2 * quarter)], sent.at[1])
        taken(lists, sent.at[9])
        taken(hfull.at[0, pl.ds(0, (count - 1) * quarter)], sent.at[2])
        taken(hfull.at[pl.ds(0, 2)], sent.at[3])
        taken(wfull.at[pl.ds(0, count - 1), pl.ds(0, half)], sent.at[4])
        taken(o_all.at[pl.ds(0, count), pl.ds(0, 5 * o_half // count)], sent.at[5])
        taken(own.at[pl.ds(0, count - 1)], sent.at[6])

    pltpu.make_async_copy(result, update, own_sems.at[5]).wait()


def out_spot(slots, hop, turn, seat, chunk, block, low, columns):
    at = (seat - low) * columns
    at = pl.ds(pl.multiple_of(at, columns), columns)
    return slots.at[hop, turn, pl.ds(chunk * block, block), at]


def out_push(own, slots, sems, sent, seat, frame, chunk, block, low):
    return push(
        own.at[frame, pl.ds(chunk * block, block)],
        out_spot(slots, 0, 0, seat, chunk, block, low, own.shape[2]),
        sent.at[6], sems.at[seat - low, chunk], "seq", frame,
    )


def keep_out(own, slots, sem, seat, chunk, block, low):
    return pltpu.make_async_copy(
        own.at[seat, pl.ds(chunk * block, block)],
        out_spot(slots, 0, 0, seat, chunk, block, low, own.shape[2]),
        sem,
    )


class LineGather:
    def __init__(self, slots, sems, across_sems, sent, chunks, count, parts):
        self.slots, self.chunks = slots, chunks
        self.sems, self.across_sems, self.sent = sems, across_sems, sent
        self.count, self.parts = count, parts
        self.me = lax.axis_index("seq")
        self.group = lax.axis_index("groups")
        self.size = slots.shape[1] // (parts * chunks)

    def rows(self, group, chunk):
        start = (group * self.chunks + chunk) * self.size
        return pl.ds(pl.multiple_of(start, self.size), self.size)

    def along(self, shard, chunk, way):
        rows = self.rows(self.group, chunk)
        return push(
            self.slots.at[shard, rows], self.slots.at[shard, rows],
            self.sent.at[5], self.sems.at[shard, chunk],
            "seq", self.me + (1 if way == 0 else -1),
        )

    def across(self, shard, chunk, hop):
        rows = self.rows(self.group, chunk)
        return push(
            self.slots.at[shard, rows], self.slots.at[shard, rows],
            self.sent.at[10], self.across_sems.at[shard],
            "groups", lax.rem(self.group + hop, self.parts),
        )

    def onward(self, way):
        return self.me < self.count - 1 if way == 0 else self.me > 0

    def shard_of(self, step, way):
        return self.me - step if way == 0 else self.me + step

    def present(self, step, way):
        return self.me >= step if way == 0 else self.me + step < self.count

    def open_way(self, way, chunks=None):
        @pl.when(self.onward(way))
        def _():
            for chunk in range(self.chunks) if chunks is None else chunks:
                self.along(self.me, chunk, way).start()

    def relay(self, step, way, chunks=None):
        shard = self.shard_of(step, way)

        @pl.when(self.present(step, way))
        def _():
            for chunk in range(self.chunks) if chunks is None else chunks:
                self.along(shard, chunk, way).wait_recv()

                @pl.when(self.onward(way))
                def _():
                    self.along(shard, chunk, way).start()

                for hop in range(1, self.parts):
                    self.across(shard, chunk, hop).start()

    def complete(self, shard):
        region = self.slots.at[shard, pl.ds(0, (self.parts - 1) * self.chunks * self.size)]
        sem = self.across_sems.at[shard]
        push(region, region, sem, sem, "seq", self.me).wait_recv()


def by_pair(tokens, modulation, w_own, o_own, pattern, counts, mask):
    sizes = tuple(lax.axis_size(axis) for axis in ("seq", "groups", "head", "sub"))
    count, parts, heads, subs = sizes
    rows, depth = tokens.shape
    width = w_own.shape[2]
    blocks = heads * subs
    quarter = rows // blocks
    chunks = rows // BLOCK
    pieces = 3
    o_chunks = 4
    columns = width // 3
    seated = len(seats(count))
    vmem = pl.BlockSpec(memory_space=pltpu.VMEM)
    whole = pl.BlockSpec(memory_space=pl.ANY)
    dma = pltpu.SemaphoreType.DMA
    kept = jnp.bfloat16
    return pl.pallas_call(
        functools.partial(by_pair_kernel, sizes, chunks, pieces, o_chunks),
        out_shape=jax.ShapeDtypeStruct((rows, o_own.shape[1]), kept),
        in_specs=[whole, vmem, whole, whole, vmem, vmem, vmem],
        out_specs=whole,
        scratch_shapes=[
            pltpu.VMEM((heads, quarter, depth), kept),
            pltpu.VMEM(w_own.shape, kept),
            pltpu.VMEM((seated, w_own.shape[0] // parts, width), kept),
            pltpu.VMEM((w_own.shape[0] // parts, width), kept),
            pltpu.VMEM((count - 1, rows, width), jnp.float32),
            pltpu.VMEM((count, rows, depth), kept),
            pltpu.VMEM((count, w_own.shape[0], width), kept),
            pltpu.VMEM((count * rows // BLOCK, BLOCK, width // 2), kept),
            pltpu.VMEM((count, rows, width // 2), kept),
            pltpu.VMEM((count,) + o_own.shape, kept),
            pltpu.VMEM((24, 128), jnp.int32),
            pltpu.VMEM((count, 24, 128), jnp.int32),
            pltpu.SMEM((count, 24, 128), jnp.int32),
            pltpu.VMEM((count, rows, columns), kept),
            pltpu.VMEM((heads, subs, rows, seated * columns), kept),
            pltpu.VMEM((rows, o_own.shape[1]), kept),
            dma((heads, 2)),
            dma((count,)),
            dma((count, pieces)),
            dma((count,)),
            dma((pieces,)),
            dma((count, chunks + 1)),
            dma((count, chunks + 1)),
            dma((count, chunks)),
            dma((count, o_chunks)),
            dma((count,)),
            dma((seated, chunks)),
            dma((seated, chunks)),
            dma((seated, chunks)),
            dma((6,)),
            dma((11,)),
        ],
        compiler_params=pltpu.CompilerParams(
            collective_id=2, has_side_effects=True, vmem_limit_bytes=60 * 1024 * 1024
        ),
        name="by_pair",
    )(tokens, modulation, w_own, o_own, pattern, counts, mask)


def shards_by_pair(tokens, modulation, w_qkv, w_out, pattern, counts, spatial_mask):
    return by_pair(tokens, modulation, w_qkv, w_out, pattern, counts[None, :], spatial_mask[0])


def one_pair_each(count, heads, subs, parts, tokens, w_qkv, w_out, pattern, spatial_mask):
    rows, frames = tokens.shape[0], spatial_mask.shape[0]
    return (
        count == 4
        and heads == subs == parts == 2
        and w_qkv.shape[1] == len(seats(count))
        and frames == 1
        and rows == BLOCK * pattern.shape[0] == BLOCK * spatial_mask.shape[1]
        and pattern.shape[0] == count
        and BLOCK % (16 * count) == 0
        and w_qkv.shape[0] % (192 * parts) == 0
        and w_out.shape[0] % (64 * parts) == 0
    )


def shards_any(*args):
    tokens, _, w_qkv, w_out, pattern, _, spatial_mask = args
    sizes = tuple(lax.axis_size(axis) for axis in ("seq", "head", "sub", "groups"))
    if one_pair_each(*sizes, tokens, w_qkv, w_out, pattern, spatial_mask):
        return shards_by_pair(*args)
    return shards(*args)


def solution(mesh):
    return jax.shard_map(
        shards_any,
        mesh=mesh,
        in_specs=(
            P(("groups", "seq"), None),
            P(),
            P("seq", ("head", "sub"), None),
            P("seq", ("head", "sub")),
            P(("groups", "seq"), None),
            P(("groups", "seq")),
            P(("groups", "seq"), None, None),
        ),
        out_specs=P(("groups", "seq"), ("head", "sub")),
        check_vma=False,
    )
```

```python
import functools
import math

import jax
import jax.numpy as jnp
from jax import lax
from jax.experimental import pallas as pl
from jax.experimental.pallas import tpu as pltpu
from jax.sharding import PartitionSpec as P

BLOCK = 128
WIN = 2


EPSILON = 1e-06


def with_halo(cells, sides, width):
    for axis, dim in sides:
        count = lax.axis_size(axis)
        ends = count - 1
        head = lax.slice_in_dim(cells, 0, width, axis=dim)
        tail = lax.slice_in_dim(cells, cells.shape[dim] - width, cells.shape[dim], axis=dim)
        cells = jnp.concatenate(
            [
                lax.ppermute(tail, axis, [(i, (i + 1) % count) for i in range(ends)]),
                cells,
                lax.ppermute(head, axis, [((i + 1) % count, i) for i in range(ends)]),
            ],
            axis=dim,
        )
    return cells


MESH = pl.DeviceIdType.MESH


def pieces_of(rows, most=4):
    for count in range(most, 0, -1):
        if rows % (16 * count) == 0:
            return count
    return 1


class ShardLine:
    def __init__(self, own, slots, sems, chunks, count, parts):
        self.own, self.slots, self.chunks = own, slots, chunks
        self.sems, self.count, self.parts = sems, count, parts
        self.me = lax.axis_index("seq")
        self.group = lax.axis_index("groups")
        self.size = own.shape[0] // (parts * chunks)

    def rows(self, group, chunk):
        start = (group * self.chunks + chunk) * self.size
        return pl.ds(pl.multiple_of(start, self.size), self.size)

    def along(self, shard, chunk, way, own):
        rows = self.rows(self.group, chunk)
        source = self.own.at[rows] if own else self.slots.at[shard, rows]
        return pltpu.make_async_remote_copy(
            src_ref=source,
            dst_ref=self.slots.at[shard, rows],
            send_sem=self.sems.at[way, 0, shard, chunk],
            recv_sem=self.sems.at[way, 1, shard, chunk],
            device_id={"seq": self.me + (1 if way == 0 else -1)},
            device_id_type=MESH,
        )

    def across(self, shard, chunk, hop):
        rows = self.rows(self.group, chunk)
        return pltpu.make_async_remote_copy(
            src_ref=self.slots.at[shard, rows],
            dst_ref=self.slots.at[shard, rows],
            send_sem=self.sems.at[1 + hop, 0, shard, chunk],
            recv_sem=self.sems.at[1 + hop, 1, shard, chunk],
            device_id={"groups": lax.rem(self.group + hop, self.parts)},
            device_id_type=MESH,
        )

    def open_line(self):
        for chunk in range(self.chunks):
            for way in (0, 1):
                @pl.when(self.onward(way))
                def _():
                    self.along(self.me, chunk, way, True).start()

    def onward(self, way):
        return self.me < self.count - 1 if way == 0 else self.me > 0

    def shard_of(self, step, way):
        return self.me - step if way == 0 else self.me + step

    def present(self, step, way):
        return self.me >= step if way == 0 else self.me + step < self.count

    def relay(self, step):
        for chunk in range(self.chunks):
            for way in (0, 1):
                shard = self.shard_of(step, way)

                @pl.when(self.present(step, way))
                def _():
                    self.along(shard, chunk, way, False).wait_recv()

                    @pl.when(self.onward(way))
                    def _():
                        self.along(shard, chunk, way, False).start()

                    for hop in range(1, self.parts):
                        self.across(shard, chunk, hop).start()

    def complete(self, shard):
        for chunk in range(self.chunks):
            for hop in range(1, self.parts):
                self.across(shard, chunk, hop).wait_recv()

    def close_sends(self, step):
        for chunk in range(self.chunks):
            for way in (0, 1):
                shard = self.shard_of(step, way)

                @pl.when(self.present(step, way))
                def _():
                    @pl.when(self.onward(way))
                    def _():
                        self.along(shard, chunk, way, False).wait_send()

                    for hop in range(1, self.parts):
                        self.across(shard, chunk, hop).wait_send()

    def close_own(self):
        for chunk in range(self.chunks):
            for way in (0, 1):
                @pl.when(self.onward(way))
                def _():
                    self.along(self.me, chunk, way, True).wait_send()


def project_kernel(count, parts, q_chunks, o_chunks, hidden, w_own, o_own, qkv, o_all, slots, total, q_sems, o_sems, own_sem):
    me = lax.axis_index("seq")
    group = lax.axis_index("groups")
    barrier = pltpu.get_barrier_semaphore()

    @pl.when(me > 0)
    def _():
        pl.semaphore_signal(barrier, inc=1, device_id={"seq": me - 1}, device_id_type=MESH)

    @pl.when(me < count - 1)
    def _():
        pl.semaphore_signal(barrier, inc=1, device_id={"seq": me + 1}, device_id_type=MESH)

    for hop in range(1, parts):
        pl.semaphore_signal(
            barrier, inc=1, device_id={"groups": lax.rem(group + hop, parts)}, device_id_type=MESH
        )
    neighbours = jnp.where(me > 0, 1, 0) + jnp.where(me < count - 1, 1, 0) + (parts - 1)
    pl.semaphore_wait(barrier, neighbours)

    line = ShardLine(w_own, slots, q_sems, q_chunks, count, parts)
    outs = ShardLine(o_own, o_all, o_sems, o_chunks, count, parts)
    line.open_line()
    keep = pltpu.make_async_copy(o_own, o_all.at[me], own_sem)
    keep.start()
    tile = 256

    def add(shard, block, first):
        def column(j, carry):
            at = pl.ds(pl.multiple_of(j * tile, tile), tile)
            product = jnp.dot(hidden[shard], block[:, at], preferred_element_type=jnp.float32)
            total[:, at] = product if first else total[:, at] + product
            return carry

        lax.fori_loop(0, total.shape[1] // tile, column, 0)

    def finish(step):
        for way in (0, 1):
            shard = line.shard_of(step, way)

            @pl.when(line.present(step, way))
            def _():
                line.complete(shard)
                add(shard, slots.at[shard], False)

    add(me, w_own, True)

    def q_step(step, carry):
        line.relay(step)

        @pl.when(step > 1)
        def _():
            finish(step - 1)

        return carry

    lax.fori_loop(1, count, q_step, 0)
    outs.open_line()
    finish(count - 1)
    qkv[...] = total[...].astype(qkv.dtype)

    def o_step(step, carry):
        outs.relay(step)
        return carry

    lax.fori_loop(1, count, o_step, 0)

    def last(step, carry):
        line.close_sends(step)
        outs.close_sends(step)
        for way in (0, 1):
            shard = outs.shard_of(step, way)

            @pl.when(outs.present(step, way))
            def _():
                outs.complete(shard)

        return carry

    lax.fori_loop(1, count, last, 0)
    line.close_own()
    outs.close_own()
    keep.wait()


def project(hidden, w_own, o_own):
    count, parts = lax.axis_size("seq"), lax.axis_size("groups")
    rows, depth = hidden.shape
    hidden = hidden.reshape(rows, count, depth // count).transpose(1, 0, 2)
    width = w_own.shape[1]
    most = 4 if count <= 8 else 1
    q_chunks = pieces_of(w_own.shape[0] // parts, most)
    o_chunks = pieces_of(o_own.shape[0] // parts, most)
    vmem = pl.BlockSpec(memory_space=pltpu.VMEM)
    return pl.pallas_call(
        functools.partial(project_kernel, count, parts, q_chunks, o_chunks),
        out_shape=[
            jax.ShapeDtypeStruct((rows, width), jnp.bfloat16),
            jax.ShapeDtypeStruct((count,) + o_own.shape, jnp.bfloat16),
        ],
        in_specs=[vmem] * 3,
        out_specs=[vmem, pl.BlockSpec(memory_space=pl.ANY)],
        scratch_shapes=[
            pltpu.VMEM((count,) + w_own.shape, jnp.bfloat16),
            pltpu.VMEM((rows, width), jnp.float32),
            pltpu.SemaphoreType.DMA((1 + parts, 2, count, q_chunks)),
            pltpu.SemaphoreType.DMA((1 + parts, 2, count, o_chunks)),
            pltpu.SemaphoreType.DMA,
        ],
        compiler_params=pltpu.CompilerParams(
            collective_id=0, has_side_effects=True, vmem_limit_bytes=48 * 1024 * 1024
        ),
        name="project",
    )(hidden, w_own, o_own)


def mix_kernel(heads, subs, chunks, attn, w_all, gate, update, slots, total, x_sems, c_sems):
    head, sub = lax.axis_index("head"), lax.axis_index("sub")
    barrier = pltpu.get_barrier_semaphore()
    for hop in range(1, heads):
        pl.semaphore_signal(
            barrier, inc=1, device_id={"head": lax.rem(head + hop, heads)}, device_id_type=MESH
        )
    for hop in range(1, subs):
        pl.semaphore_signal(
            barrier, inc=1, device_id={"sub": lax.rem(sub + hop, subs)}, device_id_type=MESH
        )
    pl.semaphore_wait(barrier, heads + subs - 2)
    size = attn.shape[0] // chunks

    def to_head(hop, chunk):
        rows = pl.ds(chunk * size, size)
        return pltpu.make_async_remote_copy(
            src_ref=attn.at[rows],
            dst_ref=slots.at[hop, 0, rows],
            send_sem=x_sems.at[hop, 0, chunk],
            recv_sem=x_sems.at[hop, 1, chunk],
            device_id={"head": lax.rem(head + hop, heads)},
            device_id_type=MESH,
        )

    def to_sub(hop, turn, chunk):
        rows = pl.ds(chunk * size, size)
        return pltpu.make_async_remote_copy(
            src_ref=attn.at[rows] if hop == 0 else slots.at[hop, 0, rows],
            dst_ref=slots.at[hop, turn, rows],
            send_sem=c_sems.at[hop, turn, 0, chunk],
            recv_sem=c_sems.at[hop, turn, 1, chunk],
            device_id={"sub": lax.rem(sub + turn, subs)},
            device_id_type=MESH,
        )

    for chunk in range(chunks):
        for hop in range(1, heads):
            to_head(hop, chunk).start()
        for turn in range(1, subs):
            to_sub(0, turn, chunk).start()

    def add(chunk, hop, turn, first):
        rows = slice(chunk * size, (chunk + 1) * size)
        owner = lax.rem(head + heads - hop, heads) * subs + lax.rem(sub + subs - turn, subs)
        block = attn[rows, :] if hop == 0 and turn == 0 else slots[hop, turn, rows, :]
        product = jnp.dot(block, w_all[owner], preferred_element_type=jnp.float32)
        total[rows, :] = product if first else total[rows, :] + product

    for chunk in range(chunks):
        add(chunk, 0, 0, True)
    for chunk in range(chunks):
        for turn in range(1, subs):
            to_sub(0, turn, chunk).wait_recv()
            add(chunk, 0, turn, False)
    for chunk in range(chunks):
        for hop in range(1, heads):
            to_head(hop, chunk).wait_recv()
            for turn in range(1, subs):
                to_sub(hop, turn, chunk).start()
            add(chunk, hop, 0, False)
    for chunk in range(chunks):
        for hop in range(1, heads):
            for turn in range(1, subs):
                to_sub(hop, turn, chunk).wait_recv()
                add(chunk, hop, turn, False)
        rows = slice(chunk * size, (chunk + 1) * size)
        update[rows, :] = (gate[...] * total[rows, :]).astype(update.dtype)
    for chunk in range(chunks):
        for hop in range(1, heads):
            to_head(hop, chunk).wait_send()
        for hop in range(heads):
            for turn in range(1, subs):
                to_sub(hop, turn, chunk).wait_send()


def mix(attention, w_all, gate):
    heads, subs = lax.axis_size("head"), lax.axis_size("sub")
    rows, width = attention.shape
    chunks = pieces_of(rows, 2)
    vmem = pl.BlockSpec(memory_space=pltpu.VMEM)
    return pl.pallas_call(
        functools.partial(mix_kernel, heads, subs, chunks),
        out_shape=jax.ShapeDtypeStruct((rows, w_all.shape[-1]), jnp.bfloat16),
        in_specs=[vmem] * 3,
        out_specs=vmem,
        scratch_shapes=[
            pltpu.VMEM((heads, subs, rows, width), jnp.bfloat16),
            pltpu.VMEM((rows, w_all.shape[-1]), jnp.float32),
            pltpu.SemaphoreType.DMA((heads, 2, chunks)),
            pltpu.SemaphoreType.DMA((heads, subs, 2, chunks)),
        ],
        compiler_params=pltpu.CompilerParams(
            collective_id=1, has_side_effects=True, vmem_limit_bytes=40 * 1024 * 1024
        ),
        name="mix",
    )(attention, w_all, gate)


def modulate(tokens, modulation):
    values = tokens.astype(jnp.float32)
    center = jnp.mean(values, axis=-1, keepdims=True)
    spread = jnp.mean(jnp.square(values - center), axis=-1, keepdims=True)
    normed = (values - center) * lax.rsqrt(spread + EPSILON)
    return (normed * (1.0 + modulation[1]) + modulation[0]).astype(jnp.bfloat16)


def shards(tokens, modulation, w_qkv, w_out, pattern, counts, spatial_mask):
    row_count, feature_width = tokens.shape
    pairs_local = w_qkv.shape[1]
    head_size = w_qkv.shape[2] // 6
    frames_local = spatial_mask.shape[0]
    positions = row_count // frames_local
    slot_total = pattern.shape[1]
    scale_factor = 1.0 / math.sqrt(head_size)
    hidden = modulate(tokens, modulation)
    projected, whole_out = project(hidden, w_qkv.reshape(w_qkv.shape[0], -1), w_out)
    packed = projected.reshape(
        frames_local, positions, pairs_local, 6 * head_size
    )
    temporal_in = packed[..., : 3 * head_size].transpose(1, 0, 2, 3)
    received = lax.all_to_all(temporal_in, "seq", split_axis=0, concat_axis=1, tiled=True)
    position_span, frame_total, items, _ = received.shape
    relaid = received.reshape(position_span * frame_total, items, 3 * head_size)
    extended = with_halo(relaid[:, :, head_size:], (("seq", 0),), WIN * BLOCK)
    block_count = position_span * frame_total // BLOCK
    key_table = extended.reshape(block_count + 2 * WIN, BLOCK, items, 2 * head_size)
    queries = relaid[:, :, :head_size].reshape(block_count, BLOCK, items, head_size)
    offsets = pattern - (lax.axis_index("seq") * block_count - WIN)

    def slot_step(slot_index, state_pair):
        numerator, denominator = state_pair
        chosen = lax.dynamic_index_in_dim(offsets, slot_index, 1, keepdims=False)
        picked = jnp.take(key_table, chosen, axis=0)
        scores = (
            jnp.einsum(
                "bqnc,bknc->bnqk",
                queries,
                picked[..., :head_size],
                preferred_element_type=jnp.float32,
            )
            * scale_factor
        )
        alive = (slot_index < counts).astype(jnp.float32)
        weights = jnp.exp(scores) * alive[:, None, None, None]
        numerator = numerator + jnp.einsum(
            "bnqk,bknc->bnqc",
            weights.astype(jnp.bfloat16),
            picked[..., head_size:],
            preferred_element_type=jnp.float32,
        )
        return (numerator, denominator + jnp.sum(weights, axis=-1))

    start_state = (
        jnp.zeros((block_count, items, BLOCK, head_size), jnp.float32),
        jnp.zeros((block_count, items, BLOCK), jnp.float32),
    )
    numerator, denominator = lax.fori_loop(0, slot_total, slot_step, start_state)
    outcome = (numerator / denominator[..., None]).astype(jnp.bfloat16)
    outcome = outcome.transpose(0, 2, 1, 3).reshape(position_span, frame_total, items, head_size)
    temporal_out = lax.all_to_all(outcome, "seq", split_axis=1, concat_axis=0, tiled=True)
    spatial = packed[..., 3 * head_size :]
    blocks_frame = positions // BLOCK
    scores = (
        jnp.einsum(
            "fpnc,fqnc->fnpq",
            spatial[..., :head_size],
            spatial[..., head_size : 2 * head_size],
            preferred_element_type=jnp.float32,
        )
        * scale_factor
    )
    keep = spatial_mask.astype(jnp.float32)[:, None, :, None, :, None]
    weights = (
        jnp.exp(scores).reshape(frames_local, pairs_local, blocks_frame, BLOCK, blocks_frame, BLOCK)
        * keep
    )
    weights = weights.reshape(frames_local, pairs_local, positions, positions)
    denominator = jnp.sum(weights, axis=-1)
    numerator = jnp.einsum(
        "fnpq,fqnc->fpnc",
        weights.astype(jnp.bfloat16),
        spatial[..., 2 * head_size :],
        preferred_element_type=jnp.float32,
    )
    spatial_out = (numerator / denominator.transpose(0, 2, 1)[..., None]).astype(jnp.bfloat16)
    attention = jnp.concatenate([temporal_out.transpose(1, 0, 2, 3), spatial_out], axis=-1)
    attention = attention.reshape(row_count, pairs_local * 2 * head_size)
    out_width = w_out.shape[1]
    blocks = lax.axis_size("head") * lax.axis_size("sub")
    gate_slice = lax.dynamic_slice_in_dim(
        modulation[2], lax.axis_index(("head", "sub")) * out_width, out_width, 0
    )
    return mix(attention, whole_out.reshape(blocks, -1, out_width), gate_slice[None, :])

def push(source, target, send_sem, recv_sem, axis, place):
    return pltpu.make_async_remote_copy(
        src_ref=source,
        dst_ref=target,
        send_sem=send_sem,
        recv_sem=recv_sem,
        device_id={axis: place},
        device_id_type=MESH,
    )


def seats(count):
    return (count // 2 - 1, count // 2)


def by_pair_kernel(
    sizes, chunks, pieces, o_chunks,
    tokens, modulation, w_own, o_own, pattern, counts, mask, update,
    held, raw, stage, passing, partial, hfull, wfull, tq, sq, o_all, lists, lists_all, table, own, slots, result,
    tok_sems, l_sems, w_sems, wa_sems, p_sems, z_sems, x_sems, c_sems, o_sems, oa_sems,
    sz_sems, sx_sems, sc_sems, own_sems, sent,
):
    count, parts, heads, subs = sizes
    low, high = seats(count)
    me, group = lax.axis_index("seq"), lax.axis_index("groups")
    head, sub = lax.axis_index("head"), lax.axis_index("sub")
    other = low + high - me
    near = jnp.where(me == low, low - 1, high + 1)
    far = jnp.where(me == low, high + 1, low - 1)
    seated = jnp.logical_or(me == low, me == high)
    ended = jnp.logical_not(seated)
    outward = jnp.where(me == low, 1, 0)
    blocks = heads * subs
    quarter = held.shape[1]
    unit = quarter // chunks
    width = wfull.shape[2]
    half = w_own.shape[0] // parts
    piece = half // pieces
    block = unit * blocks

    barrier = pltpu.get_barrier_semaphore()
    others = 0
    for axis in ("seq", "groups", "head", "sub"):
        size = lax.axis_size(axis)
        for hop in range(1, size):
            partner = lax.rem(lax.axis_index(axis) + hop, size)
            pl.semaphore_signal(barrier, inc=1, device_id={axis: partner}, device_id_type=MESH)
            others += 1

    def rows_of(head_hop, sub_hop, chunk):
        owner = lax.rem(head + heads - head_hop, heads) * subs + lax.rem(sub + subs - sub_hop, subs)
        return pl.ds(pl.multiple_of((chunk * blocks + owner) * unit, unit), unit)

    def fetch(hop, chunk):
        return pltpu.make_async_copy(
            tokens.at[rows_of(hop, 0, chunk)], held.at[hop, pl.ds(chunk * unit, unit)],
            tok_sems.at[hop, min(chunk, 1) if hop == 0 else 0],
        )

    def fetched(hop, first, last):
        pltpu.make_async_copy(
            tokens.at[pl.ds(first * unit, (last - first) * unit)],
            held.at[hop, pl.ds(first * unit, (last - first) * unit)],
            tok_sems.at[hop, min(first, 1) if hop == 0 else 0],
        ).wait()

    def taken(region, sem):
        push(region, region, sem, sem, "seq", me).wait_recv()

    for chunk in range(chunks):
        fetch(0, chunk).start()
    raw_copy = pltpu.make_async_copy(w_own, raw, own_sems.at[0])
    raw_copy.start()
    o_copy = pltpu.make_async_copy(o_own, o_all.at[me], own_sems.at[1])
    o_copy.start()

    @pl.when(seated)
    def _():
        for hop in range(1, heads):
            for chunk in range(chunks):
                fetch(hop, chunk).start()

    lists[...] = jnp.zeros_like(lists)
    slots_of = pattern.shape[1]
    lists[0 : pattern.shape[0], 0:slots_of] = pattern[...]
    lists[8 : 8 + mask.shape[0], 0 : mask.shape[1]] = mask[...]
    lists[16:17, 0 : counts.shape[1]] = counts[...]
    gain = 1.0 + modulation[1:2, :]
    shift = modulation[0:1, :]

    def modulate_rows(hop, first, last):
        def some(i, carry):
            at = pl.ds(pl.multiple_of(i * 16, 16), 16)
            chunk = i // (unit // 16)
            owner = lax.rem(head + heads - hop, heads) * subs + sub
            start = (chunk * blocks + owner) * unit + lax.rem(i, unit // 16) * 16
            values = held[hop, at, :].astype(jnp.float32)
            centered = values - jnp.mean(values, axis=-1, keepdims=True)
            spread_of = jnp.mean(jnp.square(centered), axis=-1, keepdims=True)
            normed = centered * lax.rsqrt(spread_of + EPSILON)
            hfull[me, pl.ds(pl.multiple_of(start, 16), 16), :] = (normed * gain + shift).astype(hfull.dtype)
            return carry

        fetched(hop, first, last)
        lax.fori_loop(first * unit // 16, last * unit // 16, some, 0, unroll=2)

    modulate_rows(0, 0, 1)
    pl.semaphore_wait(barrier, others)

    def spot(frame, head_hop, sub_hop, chunk):
        return hfull.at[frame, rows_of(head_hop, sub_hop, chunk)]

    def z_push(frame, chunk, place):
        target = spot(frame, 0, 0, chunk)
        return push(target, target, sent.at[1], z_sems.at[frame, chunk], "seq", place)

    def x_push(frame, chunk, hop):
        target = spot(frame, 0, 0, chunk)
        return push(
            target, target, sent.at[2], x_sems.at[frame, chunk],
            "head", lax.rem(head + hop, heads),
        )

    def c_push(frame, chunk, hop, turn):
        target = spot(frame, hop, 0, chunk)
        return push(
            target, target, sent.at[3], c_sems.at[frame, chunk],
            "sub", lax.rem(sub + turn, subs),
        )

    def z_half(frame, part, place):
        start = ((chunks - 1) * blocks + head * subs + sub) * unit + part * (unit // 2)
        target = hfull.at[frame, pl.ds(pl.multiple_of(start, unit // 2), unit // 2)]
        return push(target, target, sent.at[1], z_sems.at[frame, chunks - 1 + part], "seq", place)

    def x_half(frame, part):
        start = ((chunks - 1) * blocks + head * subs + sub) * unit + part * (unit // 2)
        target = hfull.at[frame, pl.ds(pl.multiple_of(start, unit // 2), unit // 2)]
        return push(
            target, target, sent.at[2], x_sems.at[frame, chunks - 1 + part],
            "head", lax.rem(head + 1, heads),
        )

    def l_push(seat):
        return push(lists, lists_all.at[me], sent.at[9], l_sems.at[me], "seq", seat)

    def w_rows(part, step):
        return pl.ds(pl.multiple_of(part * half + step * piece, piece), piece)

    def w_along(seat, source, step):
        return push(
            stage.at[seat - low, pl.ds(step * piece, piece)], wfull.at[source, w_rows(group, step)],
            sent.at[0], w_sems.at[source, step], "seq", seat,
        )

    def w_hand(step, place):
        return push(
            stage.at[jnp.where(me < low, high, low) - low, pl.ds(step * piece, piece)],
            passing.at[pl.ds(step * piece, piece)],
            sent.at[0], p_sems.at[step], "seq", place,
        )

    def w_pass(source, step):
        return push(
            passing.at[pl.ds(step * piece, piece)], wfull.at[source, w_rows(group, step)],
            sent.at[0], w_sems.at[source, step], "seq", other,
        )

    def w_across(source, step, turn):
        target = wfull.at[source, w_rows(group, step)]
        return push(
            target, target, sent.at[4], wa_sems.at[source],
            "groups", lax.rem(group + turn, parts),
        )

    outs = LineGather(o_all, o_sems, oa_sems, sent, o_chunks, count, parts)

    for seat in (low, high):
        @pl.when(me != seat)
        def _():
            l_push(seat).start()

    columns_of = own.shape[2]

    def item(hop, turn, seat, chunk):
        return out_spot(slots, hop, turn, seat, chunk, block, low, columns_of)

    def to_head(hop, seat, chunk, source=None):
        return push(
            item(0, 0, seat, chunk) if source is None else source, item(hop, 0, seat, chunk),
            sent.at[7], sx_sems.at[seat - low, chunk],
            "head", lax.rem(head + hop, heads),
        )

    def to_sub(hop, turn, seat, chunk, source=None):
        return push(
            item(hop, 0, seat, chunk) if source is None else source, item(hop, turn, seat, chunk),
            sent.at[8], sc_sems.at[seat - low, chunk],
            "sub", lax.rem(sub + turn, subs),
        )

    toward = jnp.where(me < low, low, high)

    def open_inward(pieces_of_it):
        for way in (0, 1):
            @pl.when(outward != way)
            def _():
                outs.open_way(way, pieces_of_it)

    def relay_out(step, pieces_of_it, outgoing):
        for way in (0, 1):
            @pl.when((outward == way) == outgoing)
            def _():
                outs.relay(step, way, pieces_of_it)

    o_first, o_last = tuple(range(o_chunks // 2)), tuple(range(o_chunks // 2, o_chunks))

    def z_out(first, last):
        @pl.when(seated)
        def _():
            for chunk in range(first, last):
                z_push(me, chunk, other).start()

        @pl.when(ended)
        def _():
            for chunk in range(first, last):
                z_push(me, chunk, toward).start()

    z_out(0, 1)
    raw_copy.wait()

    def unpack(i, carry):
        start = pl.multiple_of(i * 64, 64)
        both = raw[pl.ds(pl.multiple_of(group * half + start, 64), 64)]
        first, second = both[:, 0, :], both[:, 1, :]
        stage[0, pl.ds(start, 64), :] = first
        stage[1, pl.ds(start, 64), :] = second
        return carry

    lax.fori_loop(0, half // 64, unpack, 0)

    @pl.when(ended)
    def _():
        for step in range(pieces):
            w_hand(step, toward).start()

    @pl.when(seated)
    def _():
        for step in range(pieces):
            w_along(other, me, step).start()

    modulate_rows(0, 1, chunks)
    o_copy.wait()

    @pl.when(ended)
    def _():
        z_out(1, chunks)
        for step in range(pieces):
            w_along(toward, me, step).start()
        for way in (0, 1):
            outs.open_way(way)
        for way in (0, 1):
            outs.relay(1, way)

    @pl.when(seated)
    def _():
        for way in (0, 1):
            @pl.when(outward == way)
            def _():
                outs.open_way(way)

        keep = pltpu.make_async_copy(lists, lists_all.at[me], own_sems.at[2])
        keep.start()
        for chunk in range(chunks):
            for turn in range(1, subs):
                c_push(me, chunk, 0, turn).start()
        for hop in range(1, heads):
            modulate_rows(hop, 0, chunks)
            for chunk in range(chunks):
                for turn in range(1, subs):
                    c_push(me, chunk, hop, turn).start()

        def land(frame, chunk):
            z_push(frame, chunk, other).wait_recv()
            for hop in range(1, heads):
                x_push(frame, chunk, hop).start()
            for turn in range(1, subs):
                c_push(frame, chunk, 0, turn).start()

        def crossed(frame, chunk):
            for hop in range(1, heads):
                x_push(frame, chunk, hop).wait_recv()
                for turn in range(1, subs):
                    c_push(frame, chunk, hop, turn).start()

        def gathered(frame, chunk):
            taken(hfull.at[frame, pl.ds(0, heads * (subs - 1) * unit)], c_sems.at[frame, chunk])

        def keep_pair(i, carry):
            at = pl.ds(pl.multiple_of(i * 64, 64), 64)
            both = raw[at]
            wfull[me, at, :] = jnp.where(me == low, both[:, 0, :], both[:, 1, :])
            return carry

        def w_land(source, step):
            w_along(me, source, step).wait_recv()
            for turn in range(1, parts):
                w_across(source, step, turn).start()

        span = unit
        scale = math.log2(math.e) / math.sqrt(own.shape[2] // 2)
        size = own.shape[2] // 2
        total_blocks = tq.shape[0]
        each = total_blocks // count
        window = 2 * WIN + 1

        depth = wfull.shape[1]

        def first_part(frame, slot):
            def some_rows(chunk, carry):
                rows = pl.ds(pl.multiple_of(chunk * block, block), block)
                partial[slot, rows, :] = jnp.dot(
                    hfull[frame, rows, low * depth : (high + 1) * depth],
                    wfull[low : high + 1].reshape(-1, width), preferred_element_type=jnp.float32,
                )
                return carry

            lax.fori_loop(0, chunks, some_rows, 0, unroll=2)

        def keep_qkv(frame, chunk, total):
            at = pl.ds(pl.multiple_of(frame * span, span), span)
            for i in range(blocks):
                tq[chunk * blocks + i, at, :] = total[i * span : (i + 1) * span, : 3 * size]
            sq[frame, pl.ds(pl.multiple_of(chunk * block, block), block), :] = total[:, 3 * size :]

        land(near, 0)
        land(other, 0)
        for step in range(pieces):
            w_hand(step, other).wait_recv()
            w_pass(near, step).start()
            w_land(other, step)
        for chunk in range(1, chunks):
            z_push(me, chunk, other).start()
        z_push(near, 0, other).start()
        crossed(near, 0)
        crossed(other, 0)
        lax.fori_loop(0, w_own.shape[0] // 64, keep_pair, 0)
        rest = max(pieces, chunks - 1)
        for i in range(rest):
            if i + 1 < chunks:
                land(near, i + 1)
                if i == 1:
                    open_inward(o_first)
                if i + 2 < chunks:
                    z_push(near, i + 1, other).start()
                else:
                    for part in (0, 1):
                        z_half(near, part, other).start()
            if i < pieces:
                w_land(far, i)
        open_inward(o_last)

        def crossed_w(source):
            taken(wfull.at[source, pl.ds(0, (parts - 1) * half)], wa_sems.at[source])

        def all_in(frame):
            for chunk in range(chunks):
                gathered(frame, chunk)

        crossed_w(other)
        all_in(me)
        first_part(me, 0)
        for source in (near, other, far):
            taken(lists, l_sems.at[source])
        keep.wait()
        to_table = pltpu.make_async_copy(lists_all, table, own_sems.at[3])
        to_table.start()
        for i in range(rest):
            if i + 1 < chunks:
                land(other, i + 1)
            if i < pieces:
                w_land(near, i)
            if i + 1 < chunks:
                crossed(near, i + 1)
            if i == rest - 1:
                all_in(near)
                first_part(near, 1)
        def project(frame, chunk):
            rows = pl.ds(pl.multiple_of(chunk * block, block), block)
            total = jnp.dot(
                hfull[frame, rows, :], wfull[...].reshape(-1, width), preferred_element_type=jnp.float32
            ).astype(tq.dtype)
            keep_qkv(frame, chunk, total)

        def add_part(frame, slot, source):
            at = pl.ds(pl.multiple_of(source * depth, depth), depth)

            def some_rows(chunk, carry):
                rows = pl.ds(pl.multiple_of(chunk * block, block), block)
                partial[slot, rows, :] += jnp.dot(
                    hfull[frame, rows, at], wfull[source], preferred_element_type=jnp.float32
                )
                return carry

            lax.fori_loop(0, chunks, some_rows, 0, unroll=2)

        def project_frame(frame, slot):
            at = pl.ds(pl.multiple_of(near * depth, depth), depth)

            def last_part(chunk, carry):
                rows = pl.ds(pl.multiple_of(chunk * block, block), block)
                total = partial[slot, rows, :] + jnp.dot(
                    hfull[frame, rows, at], wfull[near], preferred_element_type=jnp.float32
                )
                keep_qkv(frame, chunk, total.astype(tq.dtype))
                return carry

            lax.fori_loop(0, chunks, last_part, 0, unroll=2)

        def soft(q, keys, values, biases):
            scores = lax.dot_general(
                q, keys, (((1,), (1,)), ((), ())), preferred_element_type=jnp.float32
            )
            parts_of = []
            sums = None
            for i, bias in enumerate(biases):
                weight = jnp.exp2(scores[:, i * BLOCK : (i + 1) * BLOCK] * scale + bias)
                sums = weight if sums is None else sums + weight
                parts_of.append(weight.astype(jnp.bfloat16))
            numerator = jnp.dot(
                jnp.concatenate(parts_of, axis=1), values, preferred_element_type=jnp.float32
            )
            return (numerator / jnp.sum(sums, axis=-1, keepdims=True)).astype(own.dtype)

        def temporal(chunk):
            def query(i, carry):
                b = chunk * blocks + i
                device, row = b // each, lax.rem(b, each)
                start = jnp.clip(b - WIN, 0, total_blocks - window)
                used = table[device, 16, row]
                biases = []
                for w in range(window):
                    times = 0
                    for j in range(slots_of):
                        hit = jnp.logical_and(j < used, table[device, row, j] == start + w)
                        times = times + jnp.where(hit, 1, 0)
                    bias = jnp.float32(-jnp.inf)
                    for m in range(1, slots_of + 1):
                        bias = jnp.where(times == m, jnp.float32(math.log2(m)), bias)
                    biases.append(bias)
                near_by = pl.ds(start, window)
                result = soft(
                    tq[b, :, :size],
                    tq[near_by, :, size : 2 * size].reshape(-1, size),
                    tq[near_by, :, 2 * size :].reshape(-1, size),
                    biases,
                )
                at = pl.ds(pl.multiple_of(b * span, span), span)
                for f in range(count):
                    own[f, at, :size] = result[f * span : (f + 1) * span]
                return carry

            lax.fori_loop(0, blocks, query, 0, unroll=True)

        def spatial(frame):
            per = sq.shape[1] // BLOCK

            def query(i, carry):
                at = pl.ds(pl.multiple_of(i * BLOCK, BLOCK), BLOCK)
                biases = [
                    jnp.where(table[frame, 8 + i, j] > 0, jnp.float32(0), jnp.float32(-jnp.inf))
                    for j in range(per)
                ]
                own[frame, at, size:] = soft(
                    sq[frame, at, :size], sq[frame, :, size : 2 * size], sq[frame, :, 2 * size :], biases
                )
                return carry

            lax.fori_loop(0, per, query, 0, unroll=True)

        def send(frame, chunk):
            out_push(own, slots, sz_sems, sent, me, frame, chunk, block, low).start()

        def send_part(frame, chunk, first):
            rows = pl.ds(chunk * block, block)
            start = pl.multiple_of((me - low) * columns_of + first, size)
            push(
                own.at[frame, rows, pl.ds(first, size)],
                slots.at[0, 0, rows, pl.ds(start, size)],
                sent.at[6], sz_sems.at[me - low, chunk], "seq", frame,
            ).start()

        def settle(chunk):
            send_part(near, chunk, 0)
            send(other, chunk)
            keep_out(own, slots, own_sems.at[4], me, chunk, block, low).start()
            mine = own.at[me, pl.ds(chunk * block, block)]
            for hop in range(1, heads):
                to_head(hop, me, chunk, mine).start()
            for turn in range(1, subs):
                to_sub(0, turn, me, chunk, mine).start()

        def far_project(chunk):
            gathered(far, chunk)
            project(far, chunk)

        crossed(other, 1)
        land(far, 0)
        crossed_w(far)
        add_part(me, 0, far)
        crossed(other, 2)
        add_part(near, 1, far)
        crossed(other, 3)
        land(far, 1)
        all_in(other)
        first_part(other, 2)
        add_part(other, 2, far)
        crossed_w(near)
        to_table.wait()
        relay_out(1, (0,), True)
        project_frame(me, 0)
        crossed(far, 0)
        project_frame(near, 1)
        relay_out(1, (1,), True)
        project_frame(other, 2)
        crossed(far, 1)
        spatial(me)
        land(far, 2)
        spatial(near)
        for chunk in range(chunks):
            send_part(near, chunk, size)
        relay_out(1, None, False)
        far_project(0)
        far_project(1)
        spatial(other)
        for part in (0, 1):
            z_half(far, part, other).wait_recv()
            x_half(far, part).start()
        for turn in range(1, subs):
            c_push(far, 3, 0, turn).start()
        temporal(0)
        settle(0)
        relay_out(1, (2,), True)
        crossed(far, 2)
        far_project(2)
        temporal(1)
        settle(1)
        relay_out(1, (3,), True)
        for part in (0, 1):
            x_half(far, part).wait_recv()
        for turn in range(1, subs):
            c_push(far, 3, 1, turn).start()
        far_project(3)
        spatial(far)
        send(far, 0)
        send(far, 1)
        relay_out(2, (0,), True)
        temporal(2)
        settle(2)
        send(far, 2)
        relay_out(2, (1,), True)
        temporal(3)
        settle(3)
        send(far, 3)
        relay_out(2, (2, 3), True)

    def arrive(chunk, seat):
        out_push(own, slots, sz_sems, sent, seat, me, chunk, block, low).wait_recv()
        for hop in range(1, heads):
            to_head(hop, seat, chunk).start()
        for turn in range(1, subs):
            to_sub(0, turn, seat, chunk).start()

    def pass_on(chunk, seat):
        for hop in range(1, heads):
            to_head(hop, seat, chunk).wait_recv()
            for turn in range(1, subs):
                to_sub(hop, turn, seat, chunk).start()

    o_half = o_all.shape[1] // parts
    columns = pl.ds(pl.multiple_of((head * subs + sub) * update.shape[1], 128), update.shape[1])
    gate = modulation[2:3, columns]

    def product(shard, chunk, seat):
        hop = lax.rem(head + heads - shard // subs, heads)
        turn = lax.rem(sub + subs - lax.rem(shard, subs), subs)
        start = pl.multiple_of((seat - low) * columns_of, columns_of)
        at = pl.ds(start, columns_of)
        return jnp.dot(
            slots[hop, turn, pl.ds(chunk * block, block), at], o_all[shard, at, :],
            preferred_element_type=jnp.float32,
        )

    def add_up(chunk, seat, shards, total=None):
        for shard in shards:
            term = product(shard, chunk, seat)
            total = term if total is None else total + term
        return total

    def passed(chunk, seat):
        taken(slots.at[0, 0, pl.ds(chunk * block, block)], sc_sems.at[seat - low, chunk])

    def put(chunk):
        rows = pl.ds(chunk * 2 * block, 2 * block)
        return pltpu.make_async_copy(result.at[rows], update.at[rows], own_sems.at[5])

    nearer = jnp.where(seated, me, toward)
    farther = low + high - nearer
    last = jnp.where(ended, count - 1 - me, far)
    middle = (jnp.where(ended, toward, near), jnp.where(ended, low + high - toward, other))

    def relay_end(step, pieces_of_it):
        for way in (0, 1):
            outs.relay(step, way, pieces_of_it)

    def first_half(chunk):
        passed(chunk, nearer)
        rows = pl.ds(chunk * block, block)
        partial[0, rows, :] = add_up(chunk, nearer, (me,) + middle)

    def second_half(chunk):
        passed(chunk, farther)
        rows = pl.ds(chunk * block, block)
        partial[0, rows, :] = add_up(chunk, farther, (me,) + middle, partial[0, rows, :])

    def finish(part):
        hop = lax.rem(head + heads - last // subs, heads)
        turn = lax.rem(sub + subs - lax.rem(last, subs), subs)
        rows = pl.ds(part * 2 * block, 2 * block)
        total = partial[0, rows, :] + jnp.dot(
            slots[hop, turn, rows, :], o_all[last], preferred_element_type=jnp.float32
        )
        result[rows, :] = (gate * total).astype(result.dtype)
        put(part).start()

    @pl.when(ended)
    def _():
        relay_end(2, o_first)
        arrive(0, nearer)
        arrive(1, nearer)
        relay_end(2, o_last)
        pass_on(0, nearer)
        pass_on(1, nearer)
        for shard in middle:
            outs.complete(shard)
        first_half(0)
        first_half(1)
        relay_end(3, o_first)
        arrive(2, nearer)
        arrive(3, nearer)

    arrive(0, farther)
    arrive(1, farther)

    @pl.when(ended)
    def _():
        relay_end(3, o_last[:1])

    @pl.when(seated)
    def _():
        for chunk in range(chunks):
            pass_on(chunk, nearer)
        pltpu.make_async_copy(own.at[0], own.at[0], own_sems.at[4]).wait()
        for shard in middle:
            outs.complete(shard)
        first_half(0)
        first_half(1)

    arrive(2, farther)
    arrive(3, farther)

    @pl.when(ended)
    def _():
        relay_end(3, o_last[1:])
        pass_on(2, nearer)
        pass_on(3, nearer)

    first_half(2)
    first_half(3)
    for chunk in range(chunks):
        pass_on(chunk, farther)
        if chunk:
            second_half(chunk - 1)
    second_half(chunks - 1)
    outs.complete(last)
    for part in range(chunks // 2):
        finish(part)

    taken(stage, sent.at[0])
    taken(slots.at[0, 0], sent.at[7])
    taken(slots.at[0], sent.at[8])
    taken(o_all.at[pl.ds(0, count - 1), pl.ds(0, (parts - 1) * o_half)], sent.at[10])

    @pl.when(ended)
    def _():
        taken(hfull.at[0, pl.ds(0, quarter)], sent.at[1])
        taken(lists_all.at[pl.ds(0, 2)], sent.at[9])
        taken(o_all.at[0, pl.ds(0, o_half)], sent.at[5])

    @pl.when(seated)
    def _():
        taken(hfull.at[0, pl.ds(0, 2 * quarter)], sent.at[1])
        taken(lists, sent.at[9])
        taken(hfull.at[0, pl.ds(0, (count - 1) * quarter)], sent.at[2])
        taken(hfull.at[pl.ds(0, 2)], sent.at[3])
        taken(wfull.at[pl.ds(0, count - 1), pl.ds(0, half)], sent.at[4])
        taken(o_all.at[pl.ds(0, count), pl.ds(0, 5 * o_half // count)], sent.at[5])
        taken(own.at[pl.ds(0, count - 1)], sent.at[6])

    pltpu.make_async_copy(result, update, own_sems.at[5]).wait()


def out_spot(slots, hop, turn, seat, chunk, block, low, columns):
    at = (seat - low) * columns
    at = pl.ds(pl.multiple_of(at, columns), columns)
    return slots.at[hop, turn, pl.ds(chunk * block, block), at]


def out_push(own, slots, sems, sent, seat, frame, chunk, block, low):
    return push(
        own.at[frame, pl.ds(chunk * block, block)],
        out_spot(slots, 0, 0, seat, chunk, block, low, own.shape[2]),
        sent.at[6], sems.at[seat - low, chunk], "seq", frame,
    )


def keep_out(own, slots, sem, seat, chunk, block, low):
    return pltpu.make_async_copy(
        own.at[seat, pl.ds(chunk * block, block)],
        out_spot(slots, 0, 0, seat, chunk, block, low, own.shape[2]),
        sem,
    )


class LineGather:
    def __init__(self, slots, sems, across_sems, sent, chunks, count, parts):
        self.slots, self.chunks = slots, chunks
        self.sems, self.across_sems, self.sent = sems, across_sems, sent
        self.count, self.parts = count, parts
        self.me = lax.axis_index("seq")
        self.group = lax.axis_index("groups")
        self.size = slots.shape[1] // (parts * chunks)

    def rows(self, group, chunk):
        start = (group * self.chunks + chunk) * self.size
        return pl.ds(pl.multiple_of(start, self.size), self.size)

    def along(self, shard, chunk, way):
        rows = self.rows(self.group, chunk)
        return push(
            self.slots.at[shard, rows], self.slots.at[shard, rows],
            self.sent.at[5], self.sems.at[shard, chunk],
            "seq", self.me + (1 if way == 0 else -1),
        )

    def across(self, shard, chunk, hop):
        rows = self.rows(self.group, chunk)
        return push(
            self.slots.at[shard, rows], self.slots.at[shard, rows],
            self.sent.at[10], self.across_sems.at[shard],
            "groups", lax.rem(self.group + hop, self.parts),
        )

    def onward(self, way):
        return self.me < self.count - 1 if way == 0 else self.me > 0

    def shard_of(self, step, way):
        return self.me - step if way == 0 else self.me + step

    def present(self, step, way):
        return self.me >= step if way == 0 else self.me + step < self.count

    def open_way(self, way, chunks=None):
        @pl.when(self.onward(way))
        def _():
            for chunk in range(self.chunks) if chunks is None else chunks:
                self.along(self.me, chunk, way).start()

    def relay(self, step, way, chunks=None):
        shard = self.shard_of(step, way)

        @pl.when(self.present(step, way))
        def _():
            for chunk in range(self.chunks) if chunks is None else chunks:
                self.along(shard, chunk, way).wait_recv()

                @pl.when(self.onward(way))
                def _():
                    self.along(shard, chunk, way).start()

                for hop in range(1, self.parts):
                    self.across(shard, chunk, hop).start()

    def complete(self, shard):
        region = self.slots.at[shard, pl.ds(0, (self.parts - 1) * self.chunks * self.size)]
        sem = self.across_sems.at[shard]
        push(region, region, sem, sem, "seq", self.me).wait_recv()


def by_pair(tokens, modulation, w_own, o_own, pattern, counts, mask):
    sizes = tuple(lax.axis_size(axis) for axis in ("seq", "groups", "head", "sub"))
    count, parts, heads, subs = sizes
    rows, depth = tokens.shape
    width = w_own.shape[2]
    blocks = heads * subs
    quarter = rows // blocks
    chunks = rows // BLOCK
    pieces = 3
    o_chunks = 4
    columns = width // 3
    seated = len(seats(count))
    vmem = pl.BlockSpec(memory_space=pltpu.VMEM)
    whole = pl.BlockSpec(memory_space=pl.ANY)
    dma = pltpu.SemaphoreType.DMA
    kept = jnp.bfloat16
    return pl.pallas_call(
        functools.partial(by_pair_kernel, sizes, chunks, pieces, o_chunks),
        out_shape=jax.ShapeDtypeStruct((rows, o_own.shape[1]), kept),
        in_specs=[whole, vmem, whole, whole, vmem, vmem, vmem],
        out_specs=whole,
        scratch_shapes=[
            pltpu.VMEM((heads, quarter, depth), kept),
            pltpu.VMEM(w_own.shape, kept),
            pltpu.VMEM((seated, w_own.shape[0] // parts, width), kept),
            pltpu.VMEM((w_own.shape[0] // parts, width), kept),
            pltpu.VMEM((count - 1, rows, width), jnp.float32),
            pltpu.VMEM((count, rows, depth), kept),
            pltpu.VMEM((count, w_own.shape[0], width), kept),
            pltpu.VMEM((count * rows // BLOCK, BLOCK, width // 2), kept),
            pltpu.VMEM((count, rows, width // 2), kept),
            pltpu.VMEM((count,) + o_own.shape, kept),
            pltpu.VMEM((24, 128), jnp.int32),
            pltpu.VMEM((count, 24, 128), jnp.int32),
            pltpu.SMEM((count, 24, 128), jnp.int32),
            pltpu.VMEM((count, rows, columns), kept),
            pltpu.VMEM((heads, subs, rows, seated * columns), kept),
            pltpu.VMEM((rows, o_own.shape[1]), kept),
            dma((heads, 2)),
            dma((count,)),
            dma((count, pieces)),
            dma((count,)),
            dma((pieces,)),
            dma((count, chunks + 1)),
            dma((count, chunks + 1)),
            dma((count, chunks)),
            dma((count, o_chunks)),
            dma((count,)),
            dma((seated, chunks)),
            dma((seated, chunks)),
            dma((seated, chunks)),
            dma((6,)),
            dma((11,)),
        ],
        compiler_params=pltpu.CompilerParams(
            collective_id=2, has_side_effects=True, vmem_limit_bytes=60 * 1024 * 1024
        ),
        name="by_pair",
    )(tokens, modulation, w_own, o_own, pattern, counts, mask)


def shards_by_pair(tokens, modulation, w_qkv, w_out, pattern, counts, spatial_mask):
    return by_pair(tokens, modulation, w_qkv, w_out, pattern, counts[None, :], spatial_mask[0])


def one_pair_each(count, heads, subs, parts, tokens, w_qkv, w_out, pattern, spatial_mask):
    rows, frames = tokens.shape[0], spatial_mask.shape[0]
    return (
        count == 4
        and heads == subs == parts == 2
        and w_qkv.shape[1] == len(seats(count))
        and frames == 1
        and rows == BLOCK * pattern.shape[0] == BLOCK * spatial_mask.shape[1]
        and pattern.shape[0] == count
        and BLOCK % (16 * count) == 0
        and w_qkv.shape[0] % (192 * parts) == 0
        and w_out.shape[0] % (64 * parts) == 0
    )


def shards_any(*args):
    tokens, _, w_qkv, w_out, pattern, _, spatial_mask = args
    sizes = tuple(lax.axis_size(axis) for axis in ("seq", "head", "sub", "groups"))
    if one_pair_each(*sizes, tokens, w_qkv, w_out, pattern, spatial_mask):
        return shards_by_pair(*args)
    return shards(*args)


def solution(mesh):
    return jax.shard_map(
        shards_any,
        mesh=mesh,
        in_specs=(
            P(("groups", "seq"), None),
            P(),
            P("seq", ("head", "sub"), None),
            P("seq", ("head", "sub")),
            P(("groups", "seq"), None),
            P(("groups", "seq")),
            P(("groups", "seq"), None, None),
        ),
        out_specs=P(("groups", "seq"), ("head", "sub")),
        check_vma=False,
    )
```
